256 devices in a mesh: lat: 64 (over z, x, y_hi), lon: 4 (over y_lo, core).
Axes of the slice: x: 4, y: 4 (y_hi: 2, y_lo: 2; y = y_hi * 2 + y_lo), z: 8, core: 2. Of those that a mesh axis runs over, the one named last changes fastest.
Arguments:
- tracers: float32 [4, 8, 256, 5760], P(None, None, 'lat', 'lon'), may hold values from -6 to 6
- merid_courant: float32 [8, 256, 5760], P(None, 'lat', 'lon'), may hold values from -0.45 to 0.45
- zonal_shift: int32 [8, 256], P(None, 'lat'), may hold values from 0 to 64, as said below
- zonal_fraction: float32 [8, 256], P(None, 'lat'), may hold values from 0 to 1
- cutoff: int32 [256], replicated, may hold values from 1 to 1023
- damping: float32 [256], replicated, may hold values from 0.1 to 0.6
Outputs:
- tracer_out: float32 [4, 8, 256, 5760], P(None, None, 'lat', 'lon')
The draws below stay inside these ranges and needn't reach their ends.
Inputs may be any that keep to these rules, and one draw needn't show every extreme that they name: `zonal_shift`: in row j no displacement exceeds 1 + (64 * |2j - 255|) // 256, a limit that grows toward the poles; below it the values are random.
All inputs are finite; a program needn't handle non-finite values.
Results may differ from the reference program's by a relative error of at most 0.00005.
Values sent between devices are 32-bit elements; how exact they have to be, the bound alone decides.
A program may use at most 64 MiB of HBM per device.

```python
import jax
import jax.numpy as jnp

NLON = 5760
NTR = 4
MODES = 1024
SMAX = 64
LEV = 8
NLAT = 256


def draw_zonal_shift(key, part):
    row_index = jnp.arange(NLAT, dtype=jnp.int32)
    distance = jnp.abs(2 * row_index + 1 - NLAT)
    row_limit = 1 + SMAX * distance // NLAT
    values = jax.random.randint(key, (LEV, NLAT), 0, SMAX + 1, dtype=jnp.int32)
    values = jnp.minimum(values, row_limit[None, :])
    return values.at[0, 0].set(SMAX).astype(jnp.int32)


def draw_cutoff(key, part):
    values = jax.random.randint(key, (NLAT,), 1, MODES, dtype=jnp.int32)
    return values.at[0].set(MODES - 1).astype(jnp.int32)


def steps_of(rng, dims, pieces, low, high):
    loudness = 1.0
    for position, shards_of in pieces:
        steps = jax.random.uniform(jax.random.fold_in(jax.random.fold_in(rng, 6), position), (shards_of,), jnp.float32, low / len(pieces), high / len(pieces))
        loudness = loudness * jnp.repeat(jnp.exp(steps), dims[position] // shards_of).reshape((-1,) + (1,) * (len(dims) - 1 - position))
    return loudness


def gaussian(stream_key, extent, width, limit, pieces=(), kind=jnp.bfloat16):
    array = width * jax.random.normal(stream_key, extent, jnp.float32)
    if pieces:
        array = array * steps_of(stream_key, extent, pieces, -0.22, 0.18)
    return jnp.clip(array, -limit, limit).astype(kind)


def setup_inputs(seed: int = 0) -> dict:
    keys = jax.random.split(jax.random.key(seed), 7)
    tracers = gaussian(keys[0], (NTR, LEV, NLAT, NLON), 1.0, 6.0, ((2, 64), (3, 4)), jnp.float32)
    merid_courant = jnp.clip(jax.random.uniform(keys[1], (LEV, NLAT, NLON), jnp.float32, -0.45, 0.45) * steps_of(keys[1], (LEV, NLAT, NLON), ((1, 64), (2, 4)), -0.4, 0.0), -0.45, 0.45)
    zonal_shift = draw_zonal_shift(jax.random.fold_in(keys[6], 71), 0)
    zonal_fraction = jnp.clip(1.0 * jax.random.uniform(keys[3], (LEV, NLAT), jnp.float32) ** steps_of(keys[3], (LEV, NLAT), ((1, 64),), -0.2, 0.2), 0.0, 1.0)
    cutoff = draw_cutoff(jax.random.fold_in(keys[6], 71), 0)
    damping = jnp.clip(jax.random.uniform(keys[5], (NLAT,), jnp.float32, 0.1, 0.6), 0.1, 0.6)
    return dict(tracers=tracers, merid_courant=merid_courant, zonal_shift=zonal_shift, zonal_fraction=zonal_fraction, cutoff=cutoff, damping=damping)


def reference(tracers, merid_courant, zonal_shift, zonal_fraction, cutoff, damping):
    zeros_row = jnp.zeros_like(tracers[:, :, :1])
    below_cells = jnp.concatenate([zeros_row, tracers[:, :, :-1]], axis=2)
    face_flux = jnp.maximum(merid_courant, 0.0)[None] * below_cells + jnp.minimum(merid_courant, 0.0)[None] * tracers
    face_flux = face_flux.at[:, :, 0].set(0.0)
    north_flux = jnp.concatenate([face_flux[:, :, 1:], zeros_row], axis=2)
    advected = tracers + face_flux - north_flux
    columns = jnp.arange(NLON, dtype=jnp.int32)
    source = (columns[None, None, :] - zonal_shift[:, :, None]) % NLON
    prior = (source - 1) % NLON

    def pick_cells(index_grid):
        return jnp.take_along_axis(advected, jnp.broadcast_to(index_grid[None], advected.shape), axis=3)

    fraction_here = zonal_fraction[None, :, :, None]
    shifted = (1.0 - fraction_here) * pick_cells(source) + fraction_here * pick_cells(prior)
    spectrum = jnp.fft.rfft(shifted, axis=3)
    wavenumber = jnp.arange(NLON // 2 + 1, dtype=jnp.int32)
    kept_modes = (wavenumber[None, :] <= cutoff[:, None]).astype(shifted.dtype)
    low_part = jnp.fft.irfft(spectrum * kept_modes[None, None], n=NLON, axis=3).astype(shifted.dtype)
    damp_factor = damping[None, None, :, None]
    filtered = damp_factor * shifted + (1.0 - damp_factor) * low_part
    row_index = jnp.arange(NLAT, dtype=jnp.int32)
    in_caps = (row_index < NLAT // 4) | (row_index >= NLAT - NLAT // 4)
    return jnp.where(in_caps[None, None, :, None], filtered, shifted)
```

```python
import functools
import math

import jax
import jax.numpy as jnp
import numpy as np
from jax import lax
from jax.experimental import pallas as pl
from jax.experimental.pallas import tpu as pltpu
from jax.sharding import PartitionSpec as P

MODES = 1024
LANES = 128
PTS = 45
HALF = 23
SPAN = 23
MESH = pl.DeviceIdType.MESH


def residues():
    found = []
    for k5 in range(3):
        for k9 in range(5 if k5 == 0 else 9):
            kk = next(k for k in range(PTS) if k % 5 == k5 and k % 9 == k9)
            found.append(kk if kk <= PTS // 2 else kk - PTS)
    return found


def tables(lon_cells):
    res = np.array(residues(), np.int64)
    lane = np.arange(LANES, dtype=np.int64)
    ang = (res[:, None] * lane[None, :] % lon_cells) * (2 * math.pi / lon_cells)
    twid = np.stack([np.cos(ang), np.sin(ang)]).astype(np.float32)
    half = LANES // 2
    k2 = np.zeros(LANES, np.int64)
    valid = np.zeros(LANES, bool)
    for part in range(2):
        k2[part * half : part * half + 2 * SPAN + 1] = np.arange(-SPAN, SPAN + 1)
        valid[part * half : part * half + 2 * SPAN + 1] = True
    mode = res[:, None] + PTS * k2[None, :]
    kabs = np.abs(mode)
    keep = valid[None, :] & (kabs < MODES) & ~((res[:, None] == 0) & (mode < 0))
    kabs = np.where(keep, kabs, 1 << 20).astype(np.int32)
    scale = np.where(mode == 0, 1.0, 2.0) / lon_cells
    scale = np.where(keep, scale, 0.0).astype(np.float32)
    ang2 = (k2[None, :] * lane[:, None] % LANES) * (2 * math.pi / LANES)
    c2 = np.cos(ang2) * valid[None, :]
    s2 = np.sin(ang2) * valid[None, :]
    first = np.arange(LANES) < half
    fwd = np.concatenate(
        [np.where(first, c2, -s2), np.where(first, s2, c2)], axis=0
    )
    inv = np.concatenate(
        [np.where(first, c2, -s2), np.where(first, s2, c2)], axis=0
    ).T
    return twid, kabs, scale, fwd.astype(np.float32), inv.astype(np.float32)


def halves(table):
    high = jnp.asarray(table).astype(jnp.bfloat16)
    low = (jnp.asarray(table) - high.astype(jnp.float32)).astype(jnp.bfloat16)
    return high, low


def split_dot(value, high, low):
    vh = value.astype(jnp.bfloat16)
    vl = (value - vh.astype(jnp.float32)).astype(jnp.bfloat16)
    dot = functools.partial(jnp.dot, preferred_element_type=jnp.float32)
    return dot(vh, high) + (dot(vl, high) + dot(vh, low))


def cs(count, turn):
    return math.cos(2 * math.pi * turn / count), math.sin(2 * math.pi * turn / count)


def real5(x):
    e1, o1, e2, o2 = x[1] + x[4], x[1] - x[4], x[2] + x[3], x[2] - x[3]
    c1, s1 = cs(5, 1)
    c2, s2 = cs(5, 2)
    return (
        x[0] + (e1 + e2),
        (x[0] + (c1 * e1 + c2 * e2), -(s1 * o1 + s2 * o2)),
        (x[0] + (c2 * e1 + c1 * e2), s1 * o2 - s2 * o1),
    )


def total(terms):
    while len(terms) > 1:
        terms = [sum(terms[i : i + 2][1:], terms[i]) for i in range(0, len(terms), 2)]
    return terms[0]


def real9(x):
    e = [x[j] + x[9 - j] for j in range(1, 5)]
    o = [x[j] - x[9 - j] for j in range(1, 5)]
    out = [(total([x[0]] + e), None)]
    for k in range(1, 5):
        re = total([x[0]] + [cs(9, j * k)[0] * e[j - 1] for j in range(1, 5)])
        im = total([-cs(9, j * k)[1] * o[j - 1] for j in range(1, 5)])
        out.append((re, im))
    return out


def complex9(re, im, sign):
    er = [re[j] + re[9 - j] for j in range(1, 5)]
    ei = [im[j] + im[9 - j] for j in range(1, 5)]
    dr = [re[j] - re[9 - j] for j in range(1, 5)]
    di = [im[j] - im[9 - j] for j in range(1, 5)]
    out = [None] * 9
    out[0] = (total([re[0]] + er), total([im[0]] + ei))
    for k in range(1, 5):
        c = [cs(9, j * k)[0] for j in range(1, 5)]
        s = [sign * cs(9, j * k)[1] for j in range(1, 5)]
        pr = total([re[0]] + [c[j] * er[j] for j in range(4)])
        pi = total([im[0]] + [c[j] * ei[j] for j in range(4)])
        qr = total([s[j] * di[j] for j in range(4)])
        qi = total([s[j] * dr[j] for j in range(4)])
        out[k] = (pr - qr, pi + qi)
        out[9 - k] = (pr + qr, pi - qi)
    return out


def forward45(x):
    zero, one, two = [], [], []
    for p9 in range(9):
        a0, a1, a2 = real5([x[(9 * p5 + 5 * p9) % PTS] for p5 in range(5)])
        zero.append(a0)
        one.append(a1)
        two.append(a2)
    out = real9(zero)
    for part in (one, two):
        out += complex9([a[0] for a in part], [a[1] for a in part], -1.0)
    return out


def inverse45(v):
    zero, one, two = v[:5], v[5:14], v[14:]
    b0 = [None] * 9
    b0[0] = total([z[0] for z in zero])
    for p in range(1, 5):
        pr = total([zero[0][0]] + [cs(9, p * k)[0] * zero[k][0] for k in range(1, 5)])
        qr = total([cs(9, p * k)[1] * zero[k][1] for k in range(1, 5)])
        b0[p] = pr - qr
        b0[9 - p] = pr + qr
    b1 = complex9([a[0] for a in one], [a[1] for a in one], 1.0)
    b2 = complex9([a[0] for a in two], [a[1] for a in two], 1.0)
    c1, s1 = cs(5, 1)
    c2, s2 = cs(5, 2)
    out = [None] * PTS
    for p9 in range(9):
        (r1, i1), (r2, i2), base = b1[p9], b2[p9], b0[p9]
        ca = base + (c1 * r1 + c2 * r2)
        sa = s1 * i1 + s2 * i2
        cb = base + (c2 * r1 + c1 * r2)
        sb = s2 * i1 - s1 * i2
        vals = [base + (r1 + r2), ca - sa, cb - sb, cb + sb, ca + sa]
        for p5 in range(5):
            out[(9 * p5 + 5 * p9) % PTS] = vals[p5]
    return out


def compute_kernel(
    tr, cour, south, north_t, north_c, shift, frac, cut, damp, open_s, open_n, cap,
    twid, kabs, scale, fwd_h, fwd_l, inv_h, inv_l, out,
    line, moved, spec, wave,
):
    tracer_count = tr.shape[1]
    columns = tr.shape[-1]
    lon_count = tr.shape[0]
    shape = (8, LANES)
    sub = lax.broadcasted_iota(jnp.int32, (8, columns), 0)
    upper = sub >= 4
    lane = lax.broadcasted_iota(jnp.int32, shape, 1)
    s0 = jnp.broadcast_to(shift[...], shape)
    s1 = s0 + 1
    here = jnp.broadcast_to(frac[...], shape)
    open_s8 = jnp.broadcast_to(open_s[...], (8, columns)) > 0
    open_n8 = jnp.broadcast_to(open_n[...], (8, columns)) > 0
    fold0, fold1 = (lane - s0) & (LANES - 1), (lane - s1) & (LANES - 1)
    own0, own1 = lane >= s0, lane >= s1

    def pair(ref_rows):
        a, b = ref_rows
        return jnp.where(upper, jnp.broadcast_to(b, (8, columns)), jnp.broadcast_to(a, (8, columns)))

    def tracer(t, carry):
        for seg in range(lon_count):
            x = jnp.concatenate([tr[seg, t, 0], tr[seg, t, 1]], axis=0)
            c = jnp.concatenate([cour[seg, 0], cour[seg, 1]], axis=0)
            lo = pair((south[seg, t, 0:1], south[seg, t, 1:2]))
            hi = pair((north_t[seg, t, 0:1], north_t[seg, t, 1:2]))
            ch = pair((north_c[seg, 0:1], north_c[seg, 1:2]))
            below = jnp.where((sub & 3) == 0, lo, pltpu.roll(x, 1, 0))
            flux = jnp.maximum(c, 0.0) * below + jnp.minimum(c, 0.0) * x
            flux = jnp.where(open_s8, flux, 0.0)
            edge = jnp.maximum(ch, 0.0) * x + jnp.minimum(ch, 0.0) * hi
            top = jnp.where((sub & 3) == 3, edge, pltpu.roll(flux, 7, 0))
            top = jnp.where(open_n8, top, 0.0)
            line[:, seg * columns : (seg + 1) * columns] = x + flux - top

        def gathered(p):
            tile = line[:, p * LANES : (p + 1) * LANES]
            return (
                jnp.take_along_axis(tile, fold0, axis=1),
                jnp.take_along_axis(tile, fold1, axis=1),
            )

        previous = gathered(PTS - 1)
        x = []
        for p in range(PTS):
            now = gathered(p)
            current = jnp.where(own0, now[0], previous[0])
            earlier = jnp.where(own1, now[1], previous[1])
            value = (1.0 - here) * current + here * earlier
            moved[t, :, p * LANES : (p + 1) * LANES] = value
            x.append(value)
            previous = now
        for r, (re, im) in enumerate(forward45(x)):
            tc, ts = twid[0, r : r + 1], twid[1, r : r + 1]
            row = pl.multiple_of((t * HALF + r) * 8, 8)
            if im is None:
                spec[pl.ds(row, 8), :LANES] = re * tc
                spec[pl.ds(row, 8), LANES:] = -(re * ts)
            else:
                spec[pl.ds(row, 8), :LANES] = re * tc + im * ts
                spec[pl.ds(row, 8), LANES:] = im * tc - re * ts
        return carry

    lax.fori_loop(0, tracer_count, tracer, 0)
    wave[...] = split_dot(spec[...], fwd_h[...], fwd_l[...])
    cut8 = jnp.broadcast_to(cut[...], shape)
    for r in range(HALF):
        weight = jnp.where(kabs[r : r + 1] <= cut8, scale[r : r + 1], 0.0)
        for t in range(tracer_count):
            row = (t * HALF + r) * 8
            wave[row : row + 8, :] = wave[row : row + 8, :] * weight
    spec[...] = split_dot(wave[...], inv_h[...], inv_l[...])

    damp8 = jnp.broadcast_to(damp[...], shape)
    cap8 = jnp.broadcast_to(cap[...], shape) > 0

    def back(t, carry):
        v = []
        for r in range(HALF):
            tc, ts = twid[0, r : r + 1], twid[1, r : r + 1]
            row = pl.multiple_of((t * HALF + r) * 8, 8)
            re, im = spec[pl.ds(row, 8), :LANES], spec[pl.ds(row, 8), LANES:]
            v.append((re * tc - im * ts, re * ts + im * tc))
        for p, low in enumerate(inverse45(v)):
            cols = slice(p * LANES, (p + 1) * LANES)
            shifted = moved[t, :, cols]
            filtered = damp8 * shifted + (1.0 - damp8) * low
            line[:, cols] = jnp.where(cap8, filtered, shifted)
        for seg in range(lon_count):
            value = line[:, seg * columns : (seg + 1) * columns]
            out[seg, t, 0] = value[:4]
            out[seg, t, 1] = value[4:]
        return carry

    lax.fori_loop(0, tracer_count, back, 0)


def compute(*operands, lon_count, tracer_count, columns):
    vmem = pl.BlockSpec(memory_space=pltpu.VMEM)
    rows = tracer_count * HALF * 8
    lon_cells = columns * lon_count
    return pl.pallas_call(
        compute_kernel,
        out_shape=jax.ShapeDtypeStruct((lon_count, tracer_count, 2, 4, columns), jnp.float32),
        in_specs=[vmem] * len(operands),
        out_specs=vmem,
        scratch_shapes=[
            pltpu.VMEM((8, lon_cells), jnp.float32),
            pltpu.VMEM((tracer_count, 8, lon_cells), jnp.float32),
            pltpu.VMEM((rows, 2 * LANES), jnp.float32),
            pltpu.VMEM((rows, LANES), jnp.float32),
        ],
        compiler_params=pltpu.CompilerParams(vmem_limit_bytes=40 << 20),
    )(*operands)


def greet(devices):
    barrier = pltpu.get_barrier_semaphore()
    for device in devices:
        pl.semaphore_signal(barrier, inc=1, device_id=device, device_id_type=MESH)
    pl.semaphore_wait(barrier, len(devices))


def gather_kernel(
    lat_count, lon_count, tr, cour, tr_top, tr_low, cour_low,
    got_t, got_c, south, north_t, north_c, send, recv, local,
):
    lat = lax.axis_index("lat")
    lon = lax.axis_index("lon")
    up = lax.rem(lat + 1, lat_count)
    down = lax.rem(lat + lat_count - 1, lat_count)
    turns = [lax.rem(lon + j, lon_count) for j in range(lon_count)]
    group = [{"lat": lat, "lon": turns[j]} for j in range(1, lon_count)]
    above = [{"lat": up, "lon": d} for d in turns]
    under = [{"lat": down, "lon": d} for d in turns]
    greet(group + above + under)
    copies = []

    def push(src, dst, device):
        index = len(copies)
        copy = pltpu.make_async_remote_copy(
            src_ref=src, dst_ref=dst, send_sem=send.at[index], recv_sem=recv.at[index],
            device_id=device, device_id_type=MESH,
        )
        copy.start()
        copies.append(copy)

    for j in (2, 1, 3):
        levels = pl.ds(2 * turns[j], 2)
        push(tr.at[:, levels], got_t.at[lon], group[j - 1])
        push(cour.at[levels], got_c.at[lon], group[j - 1])
    for j in (2, 1, 3, 0):
        levels = pl.ds(2 * turns[j], 2)
        push(tr_top.at[turns[j]], south.at[lon], above[j])
        push(tr_low.at[turns[j]], north_t.at[lon], under[j])
        push(cour_low.at[turns[j]], north_c.at[lon], under[j])
    mine = pl.ds(2 * lon, 2)
    keep_t = pltpu.make_async_copy(tr.at[:, mine], got_t.at[lon], local.at[0])
    keep_c = pltpu.make_async_copy(cour.at[mine], got_c.at[lon], local.at[1])
    keep_t.start()
    keep_c.start()
    for copy in copies:
        copy.wait()
    keep_t.wait()
    keep_c.wait()


def gather(tracers, courant, lat_count, lon_count):
    tracer_count, level_count, row_count, columns = tracers.shape
    per = level_count // lon_count

    def by_owner(edge):
        edge = edge.reshape(edge.shape[:-2] + (lon_count, per, columns))
        return jnp.moveaxis(edge, -3, 0)

    operands = (
        tracers, courant, by_owner(tracers[:, :, row_count - 1]),
        by_owner(tracers[:, :, 0]), by_owner(courant[:, 0]),
    )
    shapes = [
        (lon_count, tracer_count, per, row_count, columns),
        (lon_count, per, row_count, columns),
        (lon_count, tracer_count, per, columns),
        (lon_count, tracer_count, per, columns),
        (lon_count, per, columns),
    ]
    any_space = pl.BlockSpec(memory_space=pl.ANY)
    count = 2 * (lon_count - 1) + 3 * lon_count
    return pl.pallas_call(
        functools.partial(gather_kernel, lat_count, lon_count),
        out_shape=[jax.ShapeDtypeStruct(s, jnp.float32) for s in shapes],
        in_specs=[any_space] * len(operands),
        out_specs=[any_space] * len(shapes),
        scratch_shapes=[
            pltpu.SemaphoreType.DMA((count,)),
            pltpu.SemaphoreType.DMA((count,)),
            pltpu.SemaphoreType.DMA((2,)),
        ],
        compiler_params=pltpu.CompilerParams(collective_id=0, has_side_effects=True),
    )(*operands)


def return_kernel(lon_count, parts, out, send, recv, local):
    lon = lax.axis_index("lon")
    turns = [lax.rem(lon + j, lon_count) for j in range(lon_count)]
    greet([{"lon": d} for d in turns[1:]])
    mine = pl.ds(2 * lon, 2)
    copies = []
    for j in (2, 1, 3):
        copy = pltpu.make_async_remote_copy(
            src_ref=parts.at[turns[j]], dst_ref=out.at[:, mine],
            send_sem=send.at[j - 1], recv_sem=recv.at[j - 1],
            device_id={"lon": turns[j]}, device_id_type=MESH,
        )
        copy.start()
        copies.append(copy)
    keep = pltpu.make_async_copy(parts.at[lon], out.at[:, mine], local.at[0])
    keep.start()
    for copy in copies:
        copy.wait()
    keep.wait()


def send_back(parts, lon_count):
    _, tracer_count, per, row_count, columns = parts.shape
    any_space = pl.BlockSpec(memory_space=pl.ANY)
    return pl.pallas_call(
        functools.partial(return_kernel, lon_count),
        out_shape=jax.ShapeDtypeStruct((tracer_count, per * lon_count, row_count, columns), jnp.float32),
        in_specs=[any_space],
        out_specs=any_space,
        scratch_shapes=[
            pltpu.SemaphoreType.DMA((lon_count - 1,)),
            pltpu.SemaphoreType.DMA((lon_count - 1,)),
            pltpu.SemaphoreType.DMA((1,)),
        ],
        compiler_params=pltpu.CompilerParams(collective_id=1, has_side_effects=True),
    )(parts)


def body(tracers, merid_courant, zonal_shift, zonal_fraction, cutoff, damping):
    tracer_count, level_count, row_count, column_count = tracers.shape
    lat_count = lax.axis_size("lat")
    lat_index = lax.axis_index("lat")
    lon_count = lax.axis_size("lon")
    lon_index = lax.axis_index("lon")
    per = level_count // lon_count
    twid, kabs, scale, fwd, inv = tables(column_count * lon_count)
    pieces = gather(tracers, merid_courant, lat_count, lon_count)

    def own(levels):
        mine = lax.dynamic_slice_in_dim(levels, lon_index * per, per, axis=0)
        return mine.reshape(per * row_count, 1)

    def rows_of(values):
        mine = lax.dynamic_slice_in_dim(values, lat_index * row_count, row_count)
        return jnp.tile(mine, per).reshape(per * row_count, 1)

    row = jnp.tile(jnp.arange(row_count, dtype=jnp.int32), per).reshape(-1, 1)
    face = lat_index * row_count + row
    open_s = (face > 0).astype(jnp.int32)
    open_n = (face + 1 < lat_count * row_count).astype(jnp.int32)
    quarter = lat_count // 4
    is_cap = (lat_index < quarter) | (lat_index >= lat_count - quarter)
    cap = jnp.full((per * row_count, 1), is_cap, jnp.int32)
    parts = compute(
        *pieces, own(zonal_shift), own(zonal_fraction), rows_of(cutoff), rows_of(damping),
        open_s, open_n, cap, jnp.asarray(twid), jnp.asarray(kabs), jnp.asarray(scale),
        *halves(fwd), *halves(inv),
        lon_count=lon_count, tracer_count=tracer_count, columns=column_count,
    )
    return send_back(parts, lon_count)


def solution(mesh):
    placed = (
        P(None, None, "lat", "lon"),
        P(None, "lat", "lon"),
        P(None, "lat"),
        P(None, "lat"),
        P(),
        P(),
    )
    return jax.shard_map(
        body, mesh=mesh, in_specs=placed, out_specs=P(None, None, "lat", "lon"), check_vma=False
    )
```

```python
import functools
import math

import jax
import jax.numpy as jnp
import numpy as np
from jax import lax
from jax.experimental import pallas as pl
from jax.experimental.pallas import tpu as pltpu
from jax.sharding import PartitionSpec as P

MODES = 1024
LANES = 128
PTS = 45
HALF = 23
SPAN = 23
MESH = pl.DeviceIdType.MESH


def residues():
    found = []
    for k5 in range(3):
        for k9 in range(5 if k5 == 0 else 9):
            kk = next(k for k in range(PTS) if k % 5 == k5 and k % 9 == k9)
            found.append(kk if kk <= PTS // 2 else kk - PTS)
    return found


def tables(lon_cells):
    res = np.array(residues(), np.int64)
    lane = np.arange(LANES, dtype=np.int64)
    ang = (res[:, None] * lane[None, :] % lon_cells) * (2 * math.pi / lon_cells)
    twid = np.stack([np.cos(ang), np.sin(ang)]).astype(np.float32)
    half = LANES // 2
    k2 = np.zeros(LANES, np.int64)
    valid = np.zeros(LANES, bool)
    for part in range(2):
        k2[part * half : part * half + 2 * SPAN + 1] = np.arange(-SPAN, SPAN + 1)
        valid[part * half : part * half + 2 * SPAN + 1] = True
    mode = res[:, None] + PTS * k2[None, :]
    kabs = np.abs(mode)
    keep = valid[None, :] & (kabs < MODES) & ~((res[:, None] == 0) & (mode < 0))
    kabs = np.where(keep, kabs, 1 << 20).astype(np.int32)
    scale = np.where(mode == 0, 1.0, 2.0) / lon_cells
    scale = np.where(keep, scale, 0.0).astype(np.float32)
    ang2 = (k2[None, :] * lane[:, None] % LANES) * (2 * math.pi / LANES)
    c2 = np.cos(ang2) * valid[None, :]
    s2 = np.sin(ang2) * valid[None, :]
    first = np.arange(LANES) < half
    fwd = np.concatenate(
        [np.where(first, c2, -s2), np.where(first, s2, c2)], axis=0
    )
    inv = np.concatenate(
        [np.where(first, c2, -s2), np.where(first, s2, c2)], axis=0
    ).T
    return twid, kabs, scale, fwd.astype(np.float32), inv.astype(np.float32)


def halves(table):
    high = jnp.asarray(table).astype(jnp.bfloat16)
    low = (jnp.asarray(table) - high.astype(jnp.float32)).astype(jnp.bfloat16)
    return high, low


def split_dot(value, high, low):
    vh = value.astype(jnp.bfloat16)
    vl = (value - vh.astype(jnp.float32)).astype(jnp.bfloat16)
    dot = functools.partial(jnp.dot, preferred_element_type=jnp.float32)
    return dot(vh, high) + (dot(vl, high) + dot(vh, low))


def cs(count, turn):
    return math.cos(2 * math.pi * turn / count), math.sin(2 * math.pi * turn / count)


def real5(x):
    e1, o1, e2, o2 = x[1] + x[4], x[1] - x[4], x[2] + x[3], x[2] - x[3]
    c1, s1 = cs(5, 1)
    c2, s2 = cs(5, 2)
    return (
        x[0] + (e1 + e2),
        (x[0] + (c1 * e1 + c2 * e2), -(s1 * o1 + s2 * o2)),
        (x[0] + (c2 * e1 + c1 * e2), s1 * o2 - s2 * o1),
    )


def total(terms):
    while len(terms) > 1:
        terms = [sum(terms[i : i + 2][1:], terms[i]) for i in range(0, len(terms), 2)]
    return terms[0]


def real9(x):
    e = [x[j] + x[9 - j] for j in range(1, 5)]
    o = [x[j] - x[9 - j] for j in range(1, 5)]
    out = [(total([x[0]] + e), None)]
    for k in range(1, 5):
        re = total([x[0]] + [cs(9, j * k)[0] * e[j - 1] for j in range(1, 5)])
        im = total([-cs(9, j * k)[1] * o[j - 1] for j in range(1, 5)])
        out.append((re, im))
    return out


def complex9(re, im, sign):
    er = [re[j] + re[9 - j] for j in range(1, 5)]
    ei = [im[j] + im[9 - j] for j in range(1, 5)]
    dr = [re[j] - re[9 - j] for j in range(1, 5)]
    di = [im[j] - im[9 - j] for j in range(1, 5)]
    out = [None] * 9
    out[0] = (total([re[0]] + er), total([im[0]] + ei))
    for k in range(1, 5):
        c = [cs(9, j * k)[0] for j in range(1, 5)]
        s = [sign * cs(9, j * k)[1] for j in range(1, 5)]
        pr = total([re[0]] + [c[j] * er[j] for j in range(4)])
        pi = total([im[0]] + [c[j] * ei[j] for j in range(4)])
        qr = total([s[j] * di[j] for j in range(4)])
        qi = total([s[j] * dr[j] for j in range(4)])
        out[k] = (pr - qr, pi + qi)
        out[9 - k] = (pr + qr, pi - qi)
    return out


def forward45(x):
    zero, one, two = [], [], []
    for p9 in range(9):
        a0, a1, a2 = real5([x[(9 * p5 + 5 * p9) % PTS] for p5 in range(5)])
        zero.append(a0)
        one.append(a1)
        two.append(a2)
    out = real9(zero)
    for part in (one, two):
        out += complex9([a[0] for a in part], [a[1] for a in part], -1.0)
    return out


def inverse45(v):
    zero, one, two = v[:5], v[5:14], v[14:]
    b0 = [None] * 9
    b0[0] = total([z[0] for z in zero])
    for p in range(1, 5):
        pr = total([zero[0][0]] + [cs(9, p * k)[0] * zero[k][0] for k in range(1, 5)])
        qr = total([cs(9, p * k)[1] * zero[k][1] for k in range(1, 5)])
        b0[p] = pr - qr
        b0[9 - p] = pr + qr
    b1 = complex9([a[0] for a in one], [a[1] for a in one], 1.0)
    b2 = complex9([a[0] for a in two], [a[1] for a in two], 1.0)
    c1, s1 = cs(5, 1)
    c2, s2 = cs(5, 2)
    out = [None] * PTS
    for p9 in range(9):
        (r1, i1), (r2, i2), base = b1[p9], b2[p9], b0[p9]
        ca = base + (c1 * r1 + c2 * r2)
        sa = s1 * i1 + s2 * i2
        cb = base + (c2 * r1 + c1 * r2)
        sb = s2 * i1 - s1 * i2
        vals = [base + (r1 + r2), ca - sa, cb - sb, cb + sb, ca + sa]
        for p5 in range(5):
            out[(9 * p5 + 5 * p9) % PTS] = vals[p5]
    return out


def fused_kernel(
    lat_count, lon_count,
    tr, cour, zs_in, zf_in, cut_in, damp_in,
    twid_in, kabs_in, scale_in, fwd_h_in, fwd_l_in, inv_h_in, inv_l_in,
    out,
    got_t, got_c, halo_t, halo_c, parts,
    zs, zf, cut, damp, twid, kabs, scale, fwd_h, fwd_l, inv_h, inv_l,
    line, moved, spec, wave,
    t_send, t_recv, c_send, c_recv, h_send, h_recv, hc_send, hc_recv, b_send, b_recv, b_local, local,
):
    tracer_count, _, row_count, columns = tr.shape
    lat = lax.axis_index("lat")
    lon = lax.axis_index("lon")
    up = lax.rem(lat + 1, lat_count)
    down = lax.rem(lat + lat_count - 1, lat_count)
    flip = 2 * lax.rem(lat, 2)
    peers = [lon + 1 - 2 * lax.rem(lon, 2), lax.rem(lon + 2, lon_count), lon_count - 1 - lon]
    levels = [pl.ds(2 * lax.rem(peer + flip, lon_count), 2) for peer in peers]
    mine = pl.ds(2 * lax.rem(lon + flip, lon_count), 2)
    across = peers[1]
    near = 2 * (lon // 2)
    pairs = [near, 2 - near]

    staged = [
        (tr.at[:, mine], got_t.at[lon]), (cour.at[mine], got_c.at[lon]),
        (zs_in, zs), (zf_in, zf), (cut_in, cut), (damp_in, damp),
        (twid_in, twid), (kabs_in, kabs), (scale_in, scale),
        (fwd_h_in, fwd_h), (fwd_l_in, fwd_l), (inv_h_in, inv_h), (inv_l_in, inv_l),
    ]
    staged = [
        pltpu.make_async_copy(a, b, local.at[i]) for i, (a, b) in enumerate(staged)
    ]
    for copy in staged:
        copy.start()

    def remote(src, dst, send, recv, device):
        return pltpu.make_async_remote_copy(
            src_ref=src, dst_ref=dst, send_sem=send, recv_sem=recv,
            device_id=device, device_id_type=MESH,
        )

    def cells(t, m):
        return remote(
            tr.at[t, levels[m]], got_t.at[lon, t], t_send.at[t, m], t_recv.at[t, m],
            {"lat": lat, "lon": peers[m]},
        )

    def speeds(m):
        return remote(
            cour.at[levels[m]], got_c.at[lon], c_send.at[m], c_recv.at[m],
            {"lat": lat, "lon": peers[m]},
        )

    def rims(t, k):
        both = pl.ds(pairs[k], 2)
        north = remote(
            got_t.at[both, t, :, pl.ds(row_count - 1, 1)],
            halo_t.at[both, t, :, pl.ds(row_count - 1, 1)],
            h_send.at[t, k], h_recv.at[t, k], {"lat": up, "lon": across},
        )
        south = remote(
            got_t.at[both, t, :, pl.ds(0, 1)],
            halo_t.at[both, t, :, pl.ds(0, 1)],
            h_send.at[t, k + 2], h_recv.at[t, k + 2], {"lat": down, "lon": across},
        )
        return north, south

    def rim_speed(k):
        both = pl.ds(pairs[k], 2)
        return remote(
            got_c.at[both, :, pl.ds(0, 1)], halo_c.at[both, :, pl.ds(0, 1)],
            hc_send.at[k], hc_recv.at[k], {"lat": down, "lon": across},
        )

    def reply(t, m):
        return remote(
            parts.at[peers[m], t], out.at[t, mine], b_send.at[t, m], b_recv.at[t, m],
            {"lat": lat, "lon": peers[m]},
        )

    def keep(t):
        return pltpu.make_async_copy(parts.at[lon, t], out.at[t, mine], b_local.at[t])

    barrier = pltpu.get_barrier_semaphore()
    friends = [{"lat": lat, "lon": peer} for peer in peers]
    friends += [{"lat": up, "lon": across}, {"lat": down, "lon": across}]
    for friend in friends:
        pl.semaphore_signal(barrier, inc=1, device_id=friend, device_id_type=MESH)
    pl.semaphore_wait(barrier, len(friends))

    for m in (1, 2, 0):
        speeds(m).start()
    for t in range(tracer_count):
        for m in (1, 2, 0):
            cells(t, m).start()
    for copy in staged:
        copy.wait()

    def relay(t):
        cells(t, 0).wait_recv()
        for copy in rims(t, 0):
            copy.start()
        cells(t, 1).wait_recv()
        cells(t, 2).wait_recv()
        for copy in rims(t, 1):
            copy.start()

    speeds(0).wait_recv()
    rim_speed(0).start()
    speeds(1).wait_recv()
    speeds(2).wait_recv()
    rim_speed(1).start()
    relay(0)

    shape = (8, LANES)
    sub = lax.broadcasted_iota(jnp.int32, (8, columns), 0)
    sub1 = lax.broadcasted_iota(jnp.int32, shape, 0)
    lane = lax.broadcasted_iota(jnp.int32, shape, 1)

    def own_levels(ref):
        rows = ref[mine].astype(jnp.float32)
        wide = jnp.concatenate(
            [jnp.broadcast_to(rows[i : i + 1], (4, row_count)) for i in range(2)], axis=0
        )
        a = lax.broadcasted_iota(jnp.int32, wide.shape, 0)
        b = lax.broadcasted_iota(jnp.int32, wide.shape, 1)
        value = jnp.sum(jnp.where(b == (a & 3), wide, 0.0), axis=1, keepdims=True)
        return jnp.broadcast_to(value, shape)

    def own_rows(ref):
        rows = ref[pl.ds(lat * row_count // LANES, 1)].astype(jnp.float32)
        wide = jnp.broadcast_to(rows, shape)
        at = lax.rem(lat * row_count, LANES) + (sub1 & 3)
        value = jnp.sum(jnp.where(lane == at, wide, 0.0), axis=1, keepdims=True)
        return jnp.broadcast_to(value, shape)

    s0 = own_levels(zs).astype(jnp.int32)
    s1 = s0 + 1
    here = own_levels(zf)
    cut8 = own_rows(cut).astype(jnp.int32)
    damp8 = own_rows(damp)
    face = lat * row_count + (sub & 3)
    open_s8 = face > 0
    open_n8 = face + 1 < lat_count * row_count
    band = lat + 0 * lane
    quarter = lat_count // 4
    cap8 = (band < quarter) | (band >= lat_count - quarter)
    fold0, fold1 = (lane - s0) & (LANES - 1), (lane - s1) & (LANES - 1)
    own0, own1 = lane >= s0, lane >= s1

    def stacked(ref, *at):
        return jnp.concatenate([ref[(*at, 0)], ref[(*at, 1)]], axis=0)

    def tracer(t, carry):
        @pl.when(t < tracer_count - 1)
        def _():
            relay(t + 1)

        for k in range(2):
            for copy in rims(t, k):
                copy.wait_recv()
        for seg in range(lon_count):
            x = stacked(got_t, seg, t)
            c = stacked(got_c, seg)
            rim = stacked(halo_t, seg, t)
            rim_c = stacked(halo_c, seg)
            below = jnp.where((sub & 3) == 0, pltpu.roll(rim, 5, 0), pltpu.roll(x, 1, 0))
            flux = jnp.maximum(c, 0.0) * below + jnp.minimum(c, 0.0) * x
            flux = jnp.where(open_s8, flux, 0.0)
            hi, ch = pltpu.roll(rim, 3, 0), pltpu.roll(rim_c, 3, 0)
            edge = jnp.maximum(ch, 0.0) * x + jnp.minimum(ch, 0.0) * hi
            top = jnp.where((sub & 3) == 3, edge, pltpu.roll(flux, 7, 0))
            top = jnp.where(open_n8, top, 0.0)
            line[:, seg * columns : (seg + 1) * columns] = x + flux - top

        def gathered(p):
            tile = line[:, p * LANES : (p + 1) * LANES]
            return (
                jnp.take_along_axis(tile, fold0, axis=1),
                jnp.take_along_axis(tile, fold1, axis=1),
            )

        previous = gathered(PTS - 1)
        x = []
        for p in range(PTS):
            now = gathered(p)
            current = jnp.where(own0, now[0], previous[0])
            earlier = jnp.where(own1, now[1], previous[1])
            value = (1.0 - here) * current + here * earlier
            moved[:, p * LANES : (p + 1) * LANES] = value
            x.append(value)
            previous = now
        for r, (re, im) in enumerate(forward45(x)):
            tc, ts = twid[0, r : r + 1], twid[1, r : r + 1]
            if im is None:
                spec[8 * r : 8 * r + 8, :LANES] = re * tc
                spec[8 * r : 8 * r + 8, LANES:] = -(re * ts)
            else:
                spec[8 * r : 8 * r + 8, :LANES] = re * tc + im * ts
                spec[8 * r : 8 * r + 8, LANES:] = im * tc - re * ts
        wave[...] = split_dot(spec[...], fwd_h[...], fwd_l[...])
        for r in range(HALF):
            weight = jnp.where(kabs[r : r + 1] <= cut8, scale[r : r + 1], 0.0)
            wave[8 * r : 8 * r + 8, :] = wave[8 * r : 8 * r + 8, :] * weight
        spec[...] = split_dot(wave[...], inv_h[...], inv_l[...])
        v = []
        for r in range(HALF):
            tc, ts = twid[0, r : r + 1], twid[1, r : r + 1]
            re, im = spec[8 * r : 8 * r + 8, :LANES], spec[8 * r : 8 * r + 8, LANES:]
            v.append((re * tc - im * ts, re * ts + im * tc))
        for p, low in enumerate(inverse45(v)):
            cols = slice(p * LANES, (p + 1) * LANES)
            shifted = moved[:, cols]
            filtered = damp8 * shifted + (1.0 - damp8) * low
            line[:, cols] = jnp.where(cap8, filtered, shifted)
        for seg in range(lon_count):
            value = line[:, seg * columns : (seg + 1) * columns]
            parts[seg, t, 0] = value[:4]
            parts[seg, t, 1] = value[4:]
        for m in (1, 2, 0):
            reply(t, m).start()
        keep(t).start()
        return carry

    for k in range(2):
        rim_speed(k).wait_recv()
    lax.fori_loop(0, tracer_count, tracer, 0)

    for m in range(3):
        speeds(m).wait_send()
    for k in range(2):
        rim_speed(k).wait_send()
    for t in range(tracer_count):
        for m in range(3):
            cells(t, m).wait_send()
        for k in range(2):
            for copy in rims(t, k):
                copy.wait_send()
        for m in range(3):
            reply(t, m).wait_send()
            back = reply(t, m)
            back.wait_recv()
        keep(t).wait()


def body(tracers, merid_courant, zonal_shift, zonal_fraction, cutoff, damping):
    tracer_count, level_count, row_count, columns = tracers.shape
    lat_count = lax.axis_size("lat")
    lon_count = lax.axis_size("lon")
    per = level_count // lon_count
    twid, kabs, scale, fwd, inv = tables(columns * lon_count)
    operands = (
        tracers, merid_courant, zonal_shift, zonal_fraction,
        cutoff.reshape(-1, LANES), damping.reshape(-1, LANES),
        jnp.asarray(twid), jnp.asarray(kabs), jnp.asarray(scale), *halves(fwd), *halves(inv),
    )
    any_space = pl.BlockSpec(memory_space=pl.ANY)
    tile = (per, row_count, columns)
    f32 = jnp.float32
    small = [pltpu.VMEM(a.shape, a.dtype) for a in operands[2:]]
    dma = pltpu.SemaphoreType.DMA
    return pl.pallas_call(
        functools.partial(fused_kernel, lat_count, lon_count),
        out_shape=jax.ShapeDtypeStruct(tracers.shape, f32),
        in_specs=[any_space] * len(operands),
        out_specs=any_space,
        scratch_shapes=[
            pltpu.VMEM((lon_count, tracer_count) + tile, f32),
            pltpu.VMEM((lon_count,) + tile, f32),
            pltpu.VMEM((lon_count, tracer_count) + tile, f32),
            pltpu.VMEM((lon_count,) + tile, f32),
            pltpu.VMEM((lon_count, tracer_count) + tile, f32),
            *small,
            pltpu.VMEM((8, columns * lon_count), f32),
            pltpu.VMEM((8, columns * lon_count), f32),
            pltpu.VMEM((HALF * 8, 2 * LANES), f32),
            pltpu.VMEM((HALF * 8, LANES), f32),
            dma((tracer_count, 3)), dma((tracer_count, 3)),
            dma((3,)), dma((3,)),
            dma((tracer_count, 4)), dma((tracer_count, 4)),
            dma((2,)), dma((2,)),
            dma((tracer_count, 3)), dma((tracer_count, 3)),
            dma((tracer_count,)),
            dma((len(operands),)),
        ],
        compiler_params=pltpu.CompilerParams(collective_id=0, has_side_effects=True),
    )(*operands)


def solution(mesh):
    placed = (
        P(None, None, "lat", "lon"),
        P(None, "lat", "lon"),
        P(None, "lat"),
        P(None, "lat"),
        P(),
        P(),
    )
    return jax.shard_map(
        body, mesh=mesh, in_specs=placed, out_specs=P(None, None, "lat", "lon"), check_vma=False
    )
```

```python
import functools
import math

import jax
import jax.numpy as jnp
import numpy as np
from jax import lax
from jax.experimental import pallas as pl
from jax.experimental.pallas import tpu as pltpu
from jax.sharding import PartitionSpec as P

MODES = 1024
LANES = 128
PTS = 45
HALF = 23
SPAN = 23
MESH = pl.DeviceIdType.MESH


def residues():
    found = []
    for k5 in range(3):
        for k9 in range(5 if k5 == 0 else 9):
            kk = next(k for k in range(PTS) if k % 5 == k5 and k % 9 == k9)
            found.append(kk if kk <= PTS // 2 else kk - PTS)
    return found


def tables(lon_cells):
    res = np.array(residues(), np.int64)
    lane = np.arange(LANES, dtype=np.int64)
    ang = (res[:, None] * lane[None, :] % lon_cells) * (2 * math.pi / lon_cells)
    twid = np.stack([np.cos(ang), np.sin(ang)]).astype(np.float32)
    half = LANES // 2
    k2 = np.zeros(LANES, np.int64)
    valid = np.zeros(LANES, bool)
    for part in range(2):
        k2[part * half : part * half + 2 * SPAN + 1] = np.arange(-SPAN, SPAN + 1)
        valid[part * half : part * half + 2 * SPAN + 1] = True
    mode = res[:, None] + PTS * k2[None, :]
    kabs = np.abs(mode)
    keep = valid[None, :] & (kabs < MODES) & ~((res[:, None] == 0) & (mode < 0))
    kabs = np.where(keep, kabs, 1 << 20).astype(np.int32)
    scale = np.where(mode == 0, 1.0, 2.0) / lon_cells
    scale = np.where(keep, scale, 0.0).astype(np.float32)
    ang2 = (k2[None, :] * lane[:, None] % LANES) * (2 * math.pi / LANES)
    c2 = np.cos(ang2) * valid[None, :]
    s2 = np.sin(ang2) * valid[None, :]
    first = np.arange(LANES) < half
    fwd = np.concatenate(
        [np.where(first, c2, -s2), np.where(first, s2, c2)], axis=0
    )
    inv = np.concatenate(
        [np.where(first, c2, -s2), np.where(first, s2, c2)], axis=0
    ).T
    return twid, kabs, scale, fwd.astype(np.float32), inv.astype(np.float32)


def halves(table):
    high = jnp.asarray(table).astype(jnp.bfloat16)
    low = (jnp.asarray(table) - high.astype(jnp.float32)).astype(jnp.bfloat16)
    return high, low


def split_dot(value, high, low):
    vh = value.astype(jnp.bfloat16)
    vl = (value - vh.astype(jnp.float32)).astype(jnp.bfloat16)
    dot = functools.partial(jnp.dot, preferred_element_type=jnp.float32)
    return dot(vh, high) + (dot(vl, high) + dot(vh, low))


def cs(count, turn):
    return math.cos(2 * math.pi * turn / count), math.sin(2 * math.pi * turn / count)


def real5(x):
    e1, o1, e2, o2 = x[1] + x[4], x[1] - x[4], x[2] + x[3], x[2] - x[3]
    c1, s1 = cs(5, 1)
    c2, s2 = cs(5, 2)
    return (
        x[0] + (e1 + e2),
        (x[0] + (c1 * e1 + c2 * e2), -(s1 * o1 + s2 * o2)),
        (x[0] + (c2 * e1 + c1 * e2), s1 * o2 - s2 * o1),
    )


def total(terms):
    while len(terms) > 1:
        terms = [sum(terms[i : i + 2][1:], terms[i]) for i in range(0, len(terms), 2)]
    return terms[0]


def real9(x):
    e = [x[j] + x[9 - j] for j in range(1, 5)]
    o = [x[j] - x[9 - j] for j in range(1, 5)]
    out = [(total([x[0]] + e), None)]
    for k in range(1, 5):
        re = total([x[0]] + [cs(9, j * k)[0] * e[j - 1] for j in range(1, 5)])
        im = total([-cs(9, j * k)[1] * o[j - 1] for j in range(1, 5)])
        out.append((re, im))
    return out


def complex9(re, im, sign):
    er = [re[j] + re[9 - j] for j in range(1, 5)]
    ei = [im[j] + im[9 - j] for j in range(1, 5)]
    dr = [re[j] - re[9 - j] for j in range(1, 5)]
    di = [im[j] - im[9 - j] for j in range(1, 5)]
    out = [None] * 9
    out[0] = (total([re[0]] + er), total([im[0]] + ei))
    for k in range(1, 5):
        c = [cs(9, j * k)[0] for j in range(1, 5)]
        s = [sign * cs(9, j * k)[1] for j in range(1, 5)]
        pr = total([re[0]] + [c[j] * er[j] for j in range(4)])
        pi = total([im[0]] + [c[j] * ei[j] for j in range(4)])
        qr = total([s[j] * di[j] for j in range(4)])
        qi = total([s[j] * dr[j] for j in range(4)])
        out[k] = (pr - qr, pi + qi)
        out[9 - k] = (pr + qr, pi - qi)
    return out


def forward45(x):
    zero, one, two = [], [], []
    for p9 in range(9):
        a0, a1, a2 = real5([x[(9 * p5 + 5 * p9) % PTS] for p5 in range(5)])
        zero.append(a0)
        one.append(a1)
        two.append(a2)
    out = real9(zero)
    for part in (one, two):
        out += complex9([a[0] for a in part], [a[1] for a in part], -1.0)
    return out


def inverse45(v):
    zero, one, two = v[:5], v[5:14], v[14:]
    b0 = [None] * 9
    b0[0] = total([z[0] for z in zero])
    for p in range(1, 5):
        pr = total([zero[0][0]] + [cs(9, p * k)[0] * zero[k][0] for k in range(1, 5)])
        qr = total([cs(9, p * k)[1] * zero[k][1] for k in range(1, 5)])
        b0[p] = pr - qr
        b0[9 - p] = pr + qr
    b1 = complex9([a[0] for a in one], [a[1] for a in one], 1.0)
    b2 = complex9([a[0] for a in two], [a[1] for a in two], 1.0)
    c1, s1 = cs(5, 1)
    c2, s2 = cs(5, 2)
    out = [None] * PTS
    for p9 in range(9):
        (r1, i1), (r2, i2), base = b1[p9], b2[p9], b0[p9]
        ca = base + (c1 * r1 + c2 * r2)
        sa = s1 * i1 + s2 * i2
        cb = base + (c2 * r1 + c1 * r2)
        sb = s2 * i1 - s1 * i2
        vals = [base + (r1 + r2), ca - sa, cb - sb, cb + sb, ca + sa]
        for p5 in range(5):
            out[(9 * p5 + 5 * p9) % PTS] = vals[p5]
    return out


def fused_kernel(
    lat_count, lon_count,
    tr, cour, zs_in, zf_in, cut_in, damp_in,
    twid_in, kabs_in, scale_in, fwd_h_in, fwd_l_in, inv_h_in, inv_l_in,
    out,
    got_t, got_c, halo_t, halo_c, parts,
    zs, zf, cut, damp, twid, kabs, scale, fwd_h, fwd_l, inv_h, inv_l,
    line, moved, spec, wave,
    t_send, t_recv, c_send, c_recv, h_send, h_recv, hc_send, hc_recv, b_send, b_recv, b_local, local,
):
    tracer_count, _, row_count, columns = tr.shape
    lat = lax.axis_index("lat")
    lon = lax.axis_index("lon")
    up = lax.rem(lat + 1, lat_count)
    down = lax.rem(lat + lat_count - 1, lat_count)
    flip = 2 * lax.rem(lat, 2)
    peers = [lon + 1 - 2 * lax.rem(lon, 2), lax.rem(lon + 2, lon_count), lon_count - 1 - lon]
    levels = [pl.ds(2 * lax.rem(peer + flip, lon_count), 2) for peer in peers]
    mine = pl.ds(2 * lax.rem(lon + flip, lon_count), 2)
    across = peers[1]
    near = 2 * (lon // 2)
    pairs = [near, 2 - near]

    staged = [
        (tr.at[:, mine], got_t.at[lon]), (cour.at[mine], got_c.at[lon]),
        (zs_in, zs), (zf_in, zf), (cut_in, cut), (damp_in, damp),
        (twid_in, twid), (kabs_in, kabs), (scale_in, scale),
        (fwd_h_in, fwd_h), (fwd_l_in, fwd_l), (inv_h_in, inv_h), (inv_l_in, inv_l),
    ]
    staged = [
        pltpu.make_async_copy(a, b, local.at[i]) for i, (a, b) in enumerate(staged)
    ]
    for copy in staged:
        copy.start()

    def remote(src, dst, send, recv, device):
        return pltpu.make_async_remote_copy(
            src_ref=src, dst_ref=dst, send_sem=send, recv_sem=recv,
            device_id=device, device_id_type=MESH,
        )

    def cells(t, m):
        return remote(
            tr.at[t, levels[m]], got_t.at[lon, t], t_send.at[t, m], t_recv.at[t, m],
            {"lat": lat, "lon": peers[m]},
        )

    def speeds(m):
        return remote(
            cour.at[levels[m]], got_c.at[lon], c_send.at[m], c_recv.at[m],
            {"lat": lat, "lon": peers[m]},
        )

    def rims(t, k):
        both = pl.ds(pairs[k], 2)
        north = remote(
            got_t.at[both, t, :, pl.ds(row_count - 1, 1)],
            halo_t.at[both, t, :, pl.ds(row_count - 1, 1)],
            h_send.at[t, k], h_recv.at[t, k], {"lat": up, "lon": across},
        )
        south = remote(
            got_t.at[both, t, :, pl.ds(0, 1)],
            halo_t.at[both, t, :, pl.ds(0, 1)],
            h_send.at[t, k + 2], h_recv.at[t, k + 2], {"lat": down, "lon": across},
        )
        return north, south

    def rim_speed(k):
        both = pl.ds(pairs[k], 2)
        return remote(
            got_c.at[both, :, pl.ds(0, 1)], halo_c.at[both, :, pl.ds(0, 1)],
            hc_send.at[k], hc_recv.at[k], {"lat": down, "lon": across},
        )

    def reply(t, m):
        return remote(
            parts.at[peers[m], t], out.at[t, mine], b_send.at[t, m], b_recv.at[t, m],
            {"lat": lat, "lon": peers[m]},
        )

    def keep(t):
        return pltpu.make_async_copy(parts.at[lon, t], out.at[t, mine], b_local.at[t])

    barrier = pltpu.get_barrier_semaphore()
    has_north = (2 * lat_count - 3 - lat) // (lat_count - 1)
    has_south = (lat + lat_count - 2) // (lat_count - 1)
    sides = [(has_north == 1, {"lat": up, "lon": across}), (has_south == 1, {"lat": down, "lon": across})]

    def signal(friend):
        pl.semaphore_signal(barrier, inc=1, device_id=friend, device_id_type=MESH)

    for peer in peers:
        signal({"lat": lat, "lon": peer})
    for there, friend in sides:
        pl.when(there)(functools.partial(signal, friend))
    pl.semaphore_wait(barrier, len(peers) + has_north + has_south)
    north_there, south_there = sides[0][0], sides[1][0]

    def start_rims(t, k):
        north, south = rims(t, k)
        pl.when(north_there)(north.start)
        pl.when(south_there)(south.start)

    def start_rim_speed(k):
        pl.when(south_there)(rim_speed(k).start)

    for m in (1, 2, 0):
        speeds(m).start()
    for t in range(tracer_count):
        for m in (1, 2, 0):
            cells(t, m).start()
    for copy in staged:
        copy.wait()

    def relay(t):
        cells(t, 0).wait_recv()
        start_rims(t, 0)
        cells(t, 1).wait_recv()
        cells(t, 2).wait_recv()
        start_rims(t, 1)

    speeds(0).wait_recv()
    start_rim_speed(0)
    speeds(1).wait_recv()
    speeds(2).wait_recv()
    start_rim_speed(1)
    relay(0)

    shape = (8, LANES)
    sub = lax.broadcasted_iota(jnp.int32, (8, columns), 0)
    sub1 = lax.broadcasted_iota(jnp.int32, shape, 0)
    lane = lax.broadcasted_iota(jnp.int32, shape, 1)

    def own_levels(ref):
        rows = ref[...].astype(jnp.float32)
        wide = jnp.concatenate([rows, rows], axis=0)
        a = lax.broadcasted_iota(jnp.int32, wide.shape, 0)
        b = lax.broadcasted_iota(jnp.int32, wide.shape, 1)
        at = 2 * lax.rem(lon + flip, lon_count) + (a // 4)
        value = jnp.sum(jnp.where(b == at, wide, 0.0), axis=1, keepdims=True)
        return jnp.broadcast_to(value, shape)

    def own_rows(ref):
        rows = ref[pl.ds(lat * row_count // LANES, 1)].astype(jnp.float32)
        wide = jnp.broadcast_to(rows, shape)
        at = lax.rem(lat * row_count, LANES) + (sub1 & 3)
        value = jnp.sum(jnp.where(lane == at, wide, 0.0), axis=1, keepdims=True)
        return jnp.broadcast_to(value, shape)

    s0 = own_levels(zs).astype(jnp.int32)
    s1 = s0 + 1
    here = own_levels(zf)
    cut8 = own_rows(cut).astype(jnp.int32)
    damp8 = own_rows(damp)
    face = lat * row_count + (sub & 3)
    open_s8 = face > 0
    open_n8 = face + 1 < lat_count * row_count
    band = lat + 0 * lane
    quarter = lat_count // 4
    cap8 = (band < quarter) | (band >= lat_count - quarter)
    fold0, fold1 = (lane - s0) & (LANES - 1), (lane - s1) & (LANES - 1)
    own0, own1 = lane >= s0, lane >= s1

    def stacked(ref, *at):
        return jnp.concatenate([ref[(*at, 0)], ref[(*at, 1)]], axis=0)

    def tracer(t, carry):
        @pl.when(t < tracer_count - 1)
        def _():
            relay(t + 1)

        for k in range(2):
            north, south = rims(t, k)
            pl.when(south_there)(north.wait_recv)
            pl.when(north_there)(south.wait_recv)
        for seg in range(lon_count):
            x = stacked(got_t, seg, t)
            c = stacked(got_c, seg)
            rim = stacked(halo_t, seg, t)
            rim_c = stacked(halo_c, seg)
            below = jnp.where((sub & 3) == 0, pltpu.roll(rim, 5, 0), pltpu.roll(x, 1, 0))
            flux = jnp.maximum(c, 0.0) * below + jnp.minimum(c, 0.0) * x
            flux = jnp.where(open_s8, flux, 0.0)
            hi, ch = pltpu.roll(rim, 3, 0), pltpu.roll(rim_c, 3, 0)
            edge = jnp.maximum(ch, 0.0) * x + jnp.minimum(ch, 0.0) * hi
            top = jnp.where((sub & 3) == 3, edge, pltpu.roll(flux, 7, 0))
            top = jnp.where(open_n8, top, 0.0)
            line[:, seg * columns : (seg + 1) * columns] = x + flux - top

        def gathered(p):
            tile = line[:, p * LANES : (p + 1) * LANES]
            return (
                jnp.take_along_axis(tile, fold0, axis=1),
                jnp.take_along_axis(tile, fold1, axis=1),
            )

        previous = gathered(PTS - 1)
        x = []
        for p in range(PTS):
            now = gathered(p)
            current = jnp.where(own0, now[0], previous[0])
            earlier = jnp.where(own1, now[1], previous[1])
            value = (1.0 - here) * current + here * earlier
            moved[:, p * LANES : (p + 1) * LANES] = value
            x.append(value)
            previous = now
        for r, (re, im) in enumerate(forward45(x)):
            tc, ts = twid[0, r : r + 1], twid[1, r : r + 1]
            if im is None:
                spec[8 * r : 8 * r + 8, :LANES] = re * tc
                spec[8 * r : 8 * r + 8, LANES:] = -(re * ts)
            else:
                spec[8 * r : 8 * r + 8, :LANES] = re * tc + im * ts
                spec[8 * r : 8 * r + 8, LANES:] = im * tc - re * ts
        wave[...] = split_dot(spec[...], fwd_h[...], fwd_l[...])
        for r in range(HALF):
            weight = jnp.where(kabs[r : r + 1] <= cut8, scale[r : r + 1], 0.0)
            wave[8 * r : 8 * r + 8, :] = wave[8 * r : 8 * r + 8, :] * weight
        spec[...] = split_dot(wave[...], inv_h[...], inv_l[...])
        v = []
        for r in range(HALF):
            tc, ts = twid[0, r : r + 1], twid[1, r : r + 1]
            re, im = spec[8 * r : 8 * r + 8, :LANES], spec[8 * r : 8 * r + 8, LANES:]
            v.append((re * tc - im * ts, re * ts + im * tc))
        for p, low in enumerate(inverse45(v)):
            cols = slice(p * LANES, (p + 1) * LANES)
            shifted = moved[:, cols]
            filtered = damp8 * shifted + (1.0 - damp8) * low
            line[:, cols] = jnp.where(cap8, filtered, shifted)
        for seg in range(lon_count):
            value = line[:, seg * columns : (seg + 1) * columns]
            parts[seg, t, 0] = value[:4]
            parts[seg, t, 1] = value[4:]
        for m in (1, 2, 0):
            reply(t, m).start()
        keep(t).start()
        return carry

    for k in range(2):
        pl.when(north_there)(rim_speed(k).wait_recv)
    lax.fori_loop(0, tracer_count, tracer, 0)

    for m in range(3):
        speeds(m).wait_send()
    for k in range(2):
        pl.when(south_there)(rim_speed(k).wait_send)
    for t in range(tracer_count):
        for m in range(3):
            cells(t, m).wait_send()
        for k in range(2):
            north, south = rims(t, k)
            pl.when(north_there)(north.wait_send)
            pl.when(south_there)(south.wait_send)
        for m in range(3):
            reply(t, m).wait_send()
            back = reply(t, m)
            back.wait_recv()
        keep(t).wait()


def deliver_kernel(held, out, room, sems):
    count = held.shape[0]
    reads = [pltpu.make_async_copy(held.at[t], room.at[t], sems.at[0, t]) for t in range(count)]
    writes = [pltpu.make_async_copy(room.at[t], out.at[t], sems.at[1, t]) for t in range(count)]
    for read in reads:
        read.start()
    for read, write in zip(reads, writes):
        read.wait()
        write.start()
    for write in writes:
        write.wait()


def body(tracers, merid_courant, zonal_shift, zonal_fraction, cutoff, damping):
    tracer_count, level_count, row_count, columns = tracers.shape
    lat_count = lax.axis_size("lat")
    lon_count = lax.axis_size("lon")
    per = level_count // lon_count
    twid, kabs, scale, fwd, inv = tables(columns * lon_count)
    operands = (
        tracers, merid_courant, zonal_shift.T, zonal_fraction.T,
        cutoff.reshape(-1, LANES), damping.reshape(-1, LANES),
        jnp.asarray(twid), jnp.asarray(kabs), jnp.asarray(scale), *halves(fwd), *halves(inv),
    )
    any_space = pl.BlockSpec(memory_space=pl.ANY)
    tile = (per, row_count, columns)
    f32 = jnp.float32
    small = [pltpu.VMEM(a.shape, a.dtype) for a in operands[2:]]
    dma = pltpu.SemaphoreType.DMA
    result = pl.pallas_call(
        functools.partial(fused_kernel, lat_count, lon_count),
        out_shape=jax.ShapeDtypeStruct(tracers.shape, f32),
        in_specs=[any_space] * len(operands),
        out_specs=any_space,
        scratch_shapes=[
            pltpu.VMEM((lon_count, tracer_count) + tile, f32),
            pltpu.VMEM((lon_count,) + tile, f32),
            pltpu.VMEM((lon_count, tracer_count) + tile, f32),
            pltpu.VMEM((lon_count,) + tile, f32),
            pltpu.VMEM((lon_count, tracer_count) + tile, f32),
            *small,
            pltpu.VMEM((8, columns * lon_count), f32),
            pltpu.VMEM((8, columns * lon_count), f32),
            pltpu.VMEM((HALF * 8, 2 * LANES), f32),
            pltpu.VMEM((HALF * 8, LANES), f32),
            dma((tracer_count, 3)), dma((tracer_count, 3)),
            dma((3,)), dma((3,)),
            dma((tracer_count, 4)), dma((tracer_count, 4)),
            dma((2,)), dma((2,)),
            dma((tracer_count, 3)), dma((tracer_count, 3)),
            dma((tracer_count,)),
            dma((len(operands),)),
        ],
        compiler_params=pltpu.CompilerParams(collective_id=0, has_side_effects=True),
    )(*operands)
    return pl.pallas_call(
        deliver_kernel,
        out_shape=jax.ShapeDtypeStruct(tracers.shape, f32),
        in_specs=[any_space],
        out_specs=any_space,
        scratch_shapes=[pltpu.VMEM(tracers.shape, f32), dma((2, tracer_count))],
    )(result)


def solution(mesh):
    placed = (
        P(None, None, "lat", "lon"),
        P(None, "lat", "lon"),
        P(None, "lat"),
        P(None, "lat"),
        P(),
        P(),
    )
    return jax.shard_map(
        body, mesh=mesh, in_specs=placed, out_specs=P(None, None, "lat", "lon"), check_vma=False
    )
```

```python
import functools
import math

import jax
import jax.numpy as jnp
import numpy as np
from jax import lax
from jax.experimental import pallas as pl
from jax.experimental.pallas import tpu as pltpu
from jax.sharding import PartitionSpec as P

MODES = 1024
LANES = 128
PTS = 45
HALF = 23
SPAN = 23
MESH = pl.DeviceIdType.MESH


def residues():
    found = []
    for k5 in range(3):
        for k9 in range(5 if k5 == 0 else 9):
            kk = next(k for k in range(PTS) if k % 5 == k5 and k % 9 == k9)
            found.append(kk if kk <= PTS // 2 else kk - PTS)
    return found


def tables(lon_cells):
    res = np.array(residues(), np.int64)
    lane = np.arange(LANES, dtype=np.int64)
    ang = (res[:, None] * lane[None, :] % lon_cells) * (2 * math.pi / lon_cells)
    twid = np.stack([np.cos(ang), np.sin(ang)]).astype(np.float32)
    half = LANES // 2
    k2 = np.zeros(LANES, np.int64)
    valid = np.zeros(LANES, bool)
    for part in range(2):
        k2[part * half : part * half + 2 * SPAN + 1] = np.arange(-SPAN, SPAN + 1)
        valid[part * half : part * half + 2 * SPAN + 1] = True
    mode = res[:, None] + PTS * k2[None, :]
    kabs = np.abs(mode)
    keep = valid[None, :] & (kabs < MODES) & ~((res[:, None] == 0) & (mode < 0))
    kabs = np.where(keep, kabs, 1 << 20).astype(np.int32)
    scale = np.where(mode == 0, 1.0, 2.0) / lon_cells
    scale = np.where(keep, scale, 0.0).astype(np.float32)
    ang2 = (k2[None, :] * lane[:, None] % LANES) * (2 * math.pi / LANES)
    c2 = np.cos(ang2) * valid[None, :]
    s2 = np.sin(ang2) * valid[None, :]
    first = np.arange(LANES) < half
    fwd = np.concatenate(
        [np.where(first, c2, -s2), np.where(first, s2, c2)], axis=0
    )
    inv = np.concatenate(
        [np.where(first, c2, -s2), np.where(first, s2, c2)], axis=0
    ).T
    return twid, kabs, scale, fwd.astype(np.float32), inv.astype(np.float32)


def halves(table):
    high = jnp.asarray(table).astype(jnp.bfloat16)
    low = (jnp.asarray(table) - high.astype(jnp.float32)).astype(jnp.bfloat16)
    return high, low


def split_dot(value, high, low):
    vh = value.astype(jnp.bfloat16)
    vl = (value - vh.astype(jnp.float32)).astype(jnp.bfloat16)
    dot = functools.partial(jnp.dot, preferred_element_type=jnp.float32)
    return dot(vh, high) + (dot(vl, high) + dot(vh, low))


def cs(count, turn):
    return math.cos(2 * math.pi * turn / count), math.sin(2 * math.pi * turn / count)


def real5(x):
    e1, o1, e2, o2 = x[1] + x[4], x[1] - x[4], x[2] + x[3], x[2] - x[3]
    c1, s1 = cs(5, 1)
    c2, s2 = cs(5, 2)
    return (
        x[0] + (e1 + e2),
        (x[0] + (c1 * e1 + c2 * e2), -(s1 * o1 + s2 * o2)),
        (x[0] + (c2 * e1 + c1 * e2), s1 * o2 - s2 * o1),
    )


def total(terms):
    while len(terms) > 1:
        terms = [sum(terms[i : i + 2][1:], terms[i]) for i in range(0, len(terms), 2)]
    return terms[0]


def real9(x):
    e = [x[j] + x[9 - j] for j in range(1, 5)]
    o = [x[j] - x[9 - j] for j in range(1, 5)]
    out = [(total([x[0]] + e), None)]
    for k in range(1, 5):
        re = total([x[0]] + [cs(9, j * k)[0] * e[j - 1] for j in range(1, 5)])
        im = total([-cs(9, j * k)[1] * o[j - 1] for j in range(1, 5)])
        out.append((re, im))
    return out


def complex9(re, im, sign):
    er = [re[j] + re[9 - j] for j in range(1, 5)]
    ei = [im[j] + im[9 - j] for j in range(1, 5)]
    dr = [re[j] - re[9 - j] for j in range(1, 5)]
    di = [im[j] - im[9 - j] for j in range(1, 5)]
    out = [None] * 9
    out[0] = (total([re[0]] + er), total([im[0]] + ei))
    for k in range(1, 5):
        c = [cs(9, j * k)[0] for j in range(1, 5)]
        s = [sign * cs(9, j * k)[1] for j in range(1, 5)]
        pr = total([re[0]] + [c[j] * er[j] for j in range(4)])
        pi = total([im[0]] + [c[j] * ei[j] for j in range(4)])
        qr = total([s[j] * di[j] for j in range(4)])
        qi = total([s[j] * dr[j] for j in range(4)])
        out[k] = (pr - qr, pi + qi)
        out[9 - k] = (pr + qr, pi - qi)
    return out


def forward45(x):
    zero, one, two = [], [], []
    for p9 in range(9):
        a0, a1, a2 = real5([x[(9 * p5 + 5 * p9) % PTS] for p5 in range(5)])
        zero.append(a0)
        one.append(a1)
        two.append(a2)
    out = real9(zero)
    for part in (one, two):
        out += complex9([a[0] for a in part], [a[1] for a in part], -1.0)
    return out


def inverse45(v):
    zero, one, two = v[:5], v[5:14], v[14:]
    b0 = [None] * 9
    b0[0] = total([z[0] for z in zero])
    for p in range(1, 5):
        pr = total([zero[0][0]] + [cs(9, p * k)[0] * zero[k][0] for k in range(1, 5)])
        qr = total([cs(9, p * k)[1] * zero[k][1] for k in range(1, 5)])
        b0[p] = pr - qr
        b0[9 - p] = pr + qr
    b1 = complex9([a[0] for a in one], [a[1] for a in one], 1.0)
    b2 = complex9([a[0] for a in two], [a[1] for a in two], 1.0)
    c1, s1 = cs(5, 1)
    c2, s2 = cs(5, 2)
    out = [None] * PTS
    for p9 in range(9):
        (r1, i1), (r2, i2), base = b1[p9], b2[p9], b0[p9]
        ca = base + (c1 * r1 + c2 * r2)
        sa = s1 * i1 + s2 * i2
        cb = base + (c2 * r1 + c1 * r2)
        sb = s2 * i1 - s1 * i2
        vals = [base + (r1 + r2), ca - sa, cb - sb, cb + sb, ca + sa]
        for p5 in range(5):
            out[(9 * p5 + 5 * p9) % PTS] = vals[p5]
    return out


def fused_kernel(
    lat_count, lon_count,
    tr, cour, zs_in, zf_in, cut_in, damp_in,
    twid_in, kabs_in, scale_in, fwd_h_in, fwd_l_in, inv_h_in, inv_l_in,
    out,
    got_t, got_c, halo_t, halo_c, parts,
    zs, zf, cut, damp, twid, kabs, scale, fwd_h, fwd_l, inv_h, inv_l,
    line, moved, spec, wave,
    t_send, t_recv, c_send, c_recv, h_send, h_recv, hc_send, hc_recv, b_send, b_recv, b_local, local,
):
    tracer_count, _, row_count, columns = tr.shape
    lat = lax.axis_index("lat")
    lon = lax.axis_index("lon")
    up = lax.rem(lat + 1, lat_count)
    down = lax.rem(lat + lat_count - 1, lat_count)
    flip = 2 * lax.rem(lat, 2)
    peers = [lon + 1 - 2 * lax.rem(lon, 2), lax.rem(lon + 2, lon_count), lon_count - 1 - lon]
    levels = [pl.ds(2 * lax.rem(peer + flip, lon_count), 2) for peer in peers]
    mine = pl.ds(2 * lax.rem(lon + flip, lon_count), 2)
    across = peers[1]
    near = 2 * (lon // 2)
    pairs = [near, 2 - near]

    staged = [
        (tr.at[:, mine], got_t.at[lon]), (cour.at[mine], got_c.at[lon]),
        (zs_in, zs), (zf_in, zf), (cut_in, cut), (damp_in, damp),
        (twid_in, twid), (kabs_in, kabs), (scale_in, scale),
        (fwd_h_in, fwd_h), (fwd_l_in, fwd_l), (inv_h_in, inv_h), (inv_l_in, inv_l),
    ]
    staged = [
        pltpu.make_async_copy(a, b, local.at[i]) for i, (a, b) in enumerate(staged)
    ]
    for copy in staged:
        copy.start()

    def remote(src, dst, send, recv, device):
        return pltpu.make_async_remote_copy(
            src_ref=src, dst_ref=dst, send_sem=send, recv_sem=recv,
            device_id=device, device_id_type=MESH,
        )

    def cells(t, m):
        return remote(
            tr.at[t, levels[m]], got_t.at[lon, t], t_send.at[t, m], t_recv.at[t, m],
            {"lat": lat, "lon": peers[m]},
        )

    def speeds(m):
        return remote(
            cour.at[levels[m]], got_c.at[lon], c_send.at[m], c_recv.at[m],
            {"lat": lat, "lon": peers[m]},
        )

    def rims(t, k):
        both = pl.ds(pairs[k], 2)
        north = remote(
            got_t.at[both, t, :, pl.ds(row_count - 1, 1)],
            halo_t.at[both, t, :, pl.ds(row_count - 1, 1)],
            h_send.at[t, k], h_recv.at[t, k], {"lat": up, "lon": across},
        )
        south = remote(
            got_t.at[both, t, :, pl.ds(0, 1)],
            halo_t.at[both, t, :, pl.ds(0, 1)],
            h_send.at[t, k + 2], h_recv.at[t, k + 2], {"lat": down, "lon": across},
        )
        return north, south

    def rim_speed(k):
        both = pl.ds(pairs[k], 2)
        return remote(
            got_c.at[both, :, pl.ds(0, 1)], halo_c.at[both, :, pl.ds(0, 1)],
            hc_send.at[k], hc_recv.at[k], {"lat": down, "lon": across},
        )

    def reply(t, m):
        return remote(
            parts.at[peers[m], t], out.at[t, mine], b_send.at[t, m], b_recv.at[t, m],
            {"lat": lat, "lon": peers[m]},
        )

    def keep(t):
        return pltpu.make_async_copy(parts.at[lon, t], out.at[t, mine], b_local.at[t])

    barrier = pltpu.get_barrier_semaphore()
    has_north = (2 * lat_count - 3 - lat) // (lat_count - 1)
    has_south = (lat + lat_count - 2) // (lat_count - 1)
    sides = [(has_north == 1, {"lat": up, "lon": across}), (has_south == 1, {"lat": down, "lon": across})]

    def signal(friend):
        pl.semaphore_signal(barrier, inc=1, device_id=friend, device_id_type=MESH)

    for peer in peers:
        signal({"lat": lat, "lon": peer})
    for there, friend in sides:
        pl.when(there)(functools.partial(signal, friend))
    pl.semaphore_wait(barrier, len(peers) + has_north + has_south)
    north_there, south_there = sides[0][0], sides[1][0]

    def start_rims(t, k):
        north, south = rims(t, k)
        pl.when(north_there)(north.start)
        pl.when(south_there)(south.start)

    def start_rim_speed(k):
        pl.when(south_there)(rim_speed(k).start)

    for m in (1, 2, 0):
        speeds(m).start()
    for t in range(tracer_count):
        for m in (1, 2, 0):
            cells(t, m).start()
    for copy in staged:
        copy.wait()

    def relay(t):
        cells(t, 0).wait_recv()
        start_rims(t, 0)
        cells(t, 1).wait_recv()
        cells(t, 2).wait_recv()
        start_rims(t, 1)

    speeds(0).wait_recv()
    start_rim_speed(0)
    speeds(1).wait_recv()
    speeds(2).wait_recv()
    start_rim_speed(1)
    relay(0)

    shape = (8, LANES)
    sub = lax.broadcasted_iota(jnp.int32, (8, columns), 0)
    sub1 = lax.broadcasted_iota(jnp.int32, shape, 0)
    lane = lax.broadcasted_iota(jnp.int32, shape, 1)

    def own_levels(ref):
        rows = ref[...].astype(jnp.float32)
        wide = jnp.concatenate([rows, rows], axis=0)
        a = lax.broadcasted_iota(jnp.int32, wide.shape, 0)
        b = lax.broadcasted_iota(jnp.int32, wide.shape, 1)
        at = 2 * lax.rem(lon + flip, lon_count) + (a // 4)
        value = jnp.sum(jnp.where(b == at, wide, 0.0), axis=1, keepdims=True)
        return jnp.broadcast_to(value, shape)

    def own_rows(ref):
        rows = ref[pl.ds(lat * row_count // LANES, 1)].astype(jnp.float32)
        wide = jnp.broadcast_to(rows, shape)
        at = lax.rem(lat * row_count, LANES) + (sub1 & 3)
        value = jnp.sum(jnp.where(lane == at, wide, 0.0), axis=1, keepdims=True)
        return jnp.broadcast_to(value, shape)

    s0 = own_levels(zs).astype(jnp.int32)
    s1 = s0 + 1
    here = own_levels(zf)
    cut8 = own_rows(cut).astype(jnp.int32)
    damp8 = own_rows(damp)
    face = lat * row_count + (sub & 3)
    open_s8 = face > 0
    open_n8 = face + 1 < lat_count * row_count
    band = lat + 0 * lane
    quarter = lat_count // 4
    cap8 = (band < quarter) | (band >= lat_count - quarter)
    fold0, fold1 = (lane - s0) & (LANES - 1), (lane - s1) & (LANES - 1)
    own0, own1 = lane >= s0, lane >= s1

    def stacked(ref, *at):
        return jnp.concatenate([ref[(*at, 0)], ref[(*at, 1)]], axis=0)

    def tracer(t, carry):
        @pl.when(t < tracer_count - 1)
        def _():
            relay(t + 1)

        for k in range(2):
            north, south = rims(t, k)
            pl.when(south_there)(north.wait_recv)
            pl.when(north_there)(south.wait_recv)
        for seg in range(lon_count):
            x = stacked(got_t, seg, t)
            c = stacked(got_c, seg)
            rim = stacked(halo_t, seg, t)
            rim_c = stacked(halo_c, seg)
            below = jnp.where((sub & 3) == 0, pltpu.roll(rim, 5, 0), pltpu.roll(x, 1, 0))
            flux = jnp.maximum(c, 0.0) * below + jnp.minimum(c, 0.0) * x
            flux = jnp.where(open_s8, flux, 0.0)
            hi, ch = pltpu.roll(rim, 3, 0), pltpu.roll(rim_c, 3, 0)
            edge = jnp.maximum(ch, 0.0) * x + jnp.minimum(ch, 0.0) * hi
            top = jnp.where((sub & 3) == 3, edge, pltpu.roll(flux, 7, 0))
            top = jnp.where(open_n8, top, 0.0)
            line[:, seg * columns : (seg + 1) * columns] = x + flux - top

        def gathered(p):
            tile = line[:, p * LANES : (p + 1) * LANES]
            return (
                jnp.take_along_axis(tile, fold0, axis=1),
                jnp.take_along_axis(tile, fold1, axis=1),
            )

        previous = gathered(PTS - 1)
        x = []
        for p in range(PTS):
            now = gathered(p)
            current = jnp.where(own0, now[0], previous[0])
            earlier = jnp.where(own1, now[1], previous[1])
            value = (1.0 - here) * current + here * earlier
            moved[:, p * LANES : (p + 1) * LANES] = value
            x.append(value)
            previous = now
        for r, (re, im) in enumerate(forward45(x)):
            tc, ts = twid[0, r : r + 1], twid[1, r : r + 1]
            if im is None:
                spec[8 * r : 8 * r + 8, :LANES] = re * tc
                spec[8 * r : 8 * r + 8, LANES:] = -(re * ts)
            else:
                spec[8 * r : 8 * r + 8, :LANES] = re * tc + im * ts
                spec[8 * r : 8 * r + 8, LANES:] = im * tc - re * ts
        wave[...] = split_dot(spec[...], fwd_h[...], fwd_l[...])
        for r in range(HALF):
            weight = jnp.where(kabs[r : r + 1] <= cut8, scale[r : r + 1], 0.0)
            wave[8 * r : 8 * r + 8, :] = wave[8 * r : 8 * r + 8, :] * weight
        spec[...] = split_dot(wave[...], inv_h[...], inv_l[...])
        v = []
        for r in range(HALF):
            tc, ts = twid[0, r : r + 1], twid[1, r : r + 1]
            re, im = spec[8 * r : 8 * r + 8, :LANES], spec[8 * r : 8 * r + 8, LANES:]
            v.append((re * tc - im * ts, re * ts + im * tc))
        for p, low in enumerate(inverse45(v)):
            cols = slice(p * LANES, (p + 1) * LANES)
            shifted = moved[:, cols]
            filtered = damp8 * shifted + (1.0 - damp8) * low
            line[:, cols] = jnp.where(cap8, filtered, shifted)
        for seg in range(lon_count):
            value = line[:, seg * columns : (seg + 1) * columns]
            parts[seg, t, 0] = value[:4]
            parts[seg, t, 1] = value[4:]
        for m in (1, 2, 0):
            reply(t, m).start()
        keep(t).start()
        return carry

    for k in range(2):
        pl.when(north_there)(rim_speed(k).wait_recv)
    lax.fori_loop(0, tracer_count, tracer, 0)

    for m in range(3):
        speeds(m).wait_send()
    for k in range(2):
        pl.when(south_there)(rim_speed(k).wait_send)
    for t in range(tracer_count):
        for m in range(3):
            cells(t, m).wait_send()
        for k in range(2):
            north, south = rims(t, k)
            pl.when(north_there)(north.wait_send)
            pl.when(south_there)(south.wait_send)
        for m in range(3):
            reply(t, m).wait_send()
            back = reply(t, m)
            back.wait_recv()
        keep(t).wait()


def deliver_kernel(held, out, sem):
    copy = pltpu.make_async_copy(held, out, sem.at[0])
    copy.start()
    copy.wait()


def body(tracers, merid_courant, zonal_shift, zonal_fraction, cutoff, damping):
    tracer_count, level_count, row_count, columns = tracers.shape
    lat_count = lax.axis_size("lat")
    lon_count = lax.axis_size("lon")
    per = level_count // lon_count
    twid, kabs, scale, fwd, inv = tables(columns * lon_count)
    operands = (
        tracers, merid_courant, zonal_shift.T, zonal_fraction.T,
        cutoff.reshape(-1, LANES), damping.reshape(-1, LANES),
        jnp.asarray(twid), jnp.asarray(kabs), jnp.asarray(scale), *halves(fwd), *halves(inv),
    )
    any_space = pl.BlockSpec(memory_space=pl.ANY)
    operands = tuple(pltpu.with_memory_space_constraint(a, pltpu.HBM) for a in operands)
    tile = (per, row_count, columns)
    f32 = jnp.float32
    small = [pltpu.VMEM(a.shape, a.dtype) for a in operands[2:]]
    dma = pltpu.SemaphoreType.DMA
    result = pl.pallas_call(
        functools.partial(fused_kernel, lat_count, lon_count),
        out_shape=jax.ShapeDtypeStruct(tracers.shape, f32),
        in_specs=[any_space] * len(operands),
        out_specs=pl.BlockSpec(memory_space=pltpu.VMEM),
        scratch_shapes=[
            pltpu.VMEM((lon_count, tracer_count) + tile, f32),
            pltpu.VMEM((lon_count,) + tile, f32),
            pltpu.VMEM((lon_count, tracer_count) + tile, f32),
            pltpu.VMEM((lon_count,) + tile, f32),
            pltpu.VMEM((lon_count, tracer_count) + tile, f32),
            *small,
            pltpu.VMEM((8, columns * lon_count), f32),
            pltpu.VMEM((8, columns * lon_count), f32),
            pltpu.VMEM((HALF * 8, 2 * LANES), f32),
            pltpu.VMEM((HALF * 8, LANES), f32),
            dma((tracer_count, 3)), dma((tracer_count, 3)),
            dma((3,)), dma((3,)),
            dma((tracer_count, 4)), dma((tracer_count, 4)),
            dma((2,)), dma((2,)),
            dma((tracer_count, 3)), dma((tracer_count, 3)),
            dma((tracer_count,)),
            dma((len(operands),)),
        ],
        compiler_params=pltpu.CompilerParams(
            collective_id=0, has_side_effects=True, vmem_limit_bytes=16 << 20
        ),
    )(*operands)
    return pl.pallas_call(
        deliver_kernel,
        out_shape=jax.ShapeDtypeStruct(tracers.shape, f32),
        in_specs=[pl.BlockSpec(memory_space=pltpu.VMEM)],
        out_specs=any_space,
        scratch_shapes=[dma((1,))],
        compiler_params=pltpu.CompilerParams(vmem_limit_bytes=4 << 20),
    )(result)


def solution(mesh):
    placed = (
        P(None, None, "lat", "lon"),
        P(None, "lat", "lon"),
        P(None, "lat"),
        P(None, "lat"),
        P(),
        P(),
    )
    return jax.shard_map(
        body, mesh=mesh, in_specs=placed, out_specs=P(None, None, "lat", "lon"), check_vma=False
    )
```

```python
import functools
import math

import jax
import jax.numpy as jnp
import numpy as np
from jax import lax
from jax.experimental import pallas as pl
from jax.experimental.pallas import tpu as pltpu
from jax.sharding import PartitionSpec as P

MODES = 1024
LANES = 128
PTS = 45
HALF = 23
SPAN = 23
MESH = pl.DeviceIdType.MESH


def residues():
    found = []
    for k5 in range(3):
        for k9 in range(5 if k5 == 0 else 9):
            kk = next(k for k in range(PTS) if k % 5 == k5 and k % 9 == k9)
            found.append(kk if kk <= PTS // 2 else kk - PTS)
    return found


def tables(lon_cells):
    res = np.array(residues(), np.int64)
    lane = np.arange(LANES, dtype=np.int64)
    ang = (res[:, None] * lane[None, :] % lon_cells) * (2 * math.pi / lon_cells)
    twid = np.stack([np.cos(ang), np.sin(ang)]).astype(np.float32)
    half = LANES // 2
    k2 = np.zeros(LANES, np.int64)
    valid = np.zeros(LANES, bool)
    for part in range(2):
        k2[part * half : part * half + 2 * SPAN + 1] = np.arange(-SPAN, SPAN + 1)
        valid[part * half : part * half + 2 * SPAN + 1] = True
    mode = res[:, None] + PTS * k2[None, :]
    kabs = np.abs(mode)
    keep = valid[None, :] & (kabs < MODES) & ~((res[:, None] == 0) & (mode < 0))
    kabs = np.where(keep, kabs, 1 << 20).astype(np.int32)
    scale = np.where(mode == 0, 1.0, 2.0) / lon_cells
    scale = np.where(keep, scale, 0.0).astype(np.float32)
    ang2 = (k2[None, :] * lane[:, None] % LANES) * (2 * math.pi / LANES)
    c2 = np.cos(ang2) * valid[None, :]
    s2 = np.sin(ang2) * valid[None, :]
    first = np.arange(LANES) < half
    fwd = np.concatenate(
        [np.where(first, c2, -s2), np.where(first, s2, c2)], axis=0
    )
    inv = np.concatenate(
        [np.where(first, c2, -s2), np.where(first, s2, c2)], axis=0
    ).T
    return twid, kabs, scale, fwd.astype(np.float32), inv.astype(np.float32)


def halves(table):
    high = jnp.asarray(table).astype(jnp.bfloat16)
    low = (jnp.asarray(table) - high.astype(jnp.float32)).astype(jnp.bfloat16)
    return high, low


def split_dot(value, high, low):
    vh = value.astype(jnp.bfloat16)
    vl = (value - vh.astype(jnp.float32)).astype(jnp.bfloat16)
    dot = functools.partial(jnp.dot, preferred_element_type=jnp.float32)
    return dot(vh, high) + (dot(vl, high) + dot(vh, low))


def cs(count, turn):
    return math.cos(2 * math.pi * turn / count), math.sin(2 * math.pi * turn / count)


def real5(x):
    e1, o1, e2, o2 = x[1] + x[4], x[1] - x[4], x[2] + x[3], x[2] - x[3]
    c1, s1 = cs(5, 1)
    c2, s2 = cs(5, 2)
    return (
        x[0] + (e1 + e2),
        (x[0] + (c1 * e1 + c2 * e2), -(s1 * o1 + s2 * o2)),
        (x[0] + (c2 * e1 + c1 * e2), s1 * o2 - s2 * o1),
    )


def total(terms):
    while len(terms) > 1:
        terms = [sum(terms[i : i + 2][1:], terms[i]) for i in range(0, len(terms), 2)]
    return terms[0]


def real9(x):
    e = [x[j] + x[9 - j] for j in range(1, 5)]
    o = [x[j] - x[9 - j] for j in range(1, 5)]
    out = [(total([x[0]] + e), None)]
    for k in range(1, 5):
        re = total([x[0]] + [cs(9, j * k)[0] * e[j - 1] for j in range(1, 5)])
        im = total([-cs(9, j * k)[1] * o[j - 1] for j in range(1, 5)])
        out.append((re, im))
    return out


def complex9(re, im, sign):
    er = [re[j] + re[9 - j] for j in range(1, 5)]
    ei = [im[j] + im[9 - j] for j in range(1, 5)]
    dr = [re[j] - re[9 - j] for j in range(1, 5)]
    di = [im[j] - im[9 - j] for j in range(1, 5)]
    out = [None] * 9
    out[0] = (total([re[0]] + er), total([im[0]] + ei))
    for k in range(1, 5):
        c = [cs(9, j * k)[0] for j in range(1, 5)]
        s = [sign * cs(9, j * k)[1] for j in range(1, 5)]
        pr = total([re[0]] + [c[j] * er[j] for j in range(4)])
        pi = total([im[0]] + [c[j] * ei[j] for j in range(4)])
        qr = total([s[j] * di[j] for j in range(4)])
        qi = total([s[j] * dr[j] for j in range(4)])
        out[k] = (pr - qr, pi + qi)
        out[9 - k] = (pr + qr, pi - qi)
    return out


def forward45(x):
    zero, one, two = [], [], []
    for p9 in range(9):
        a0, a1, a2 = real5([x[(9 * p5 + 5 * p9) % PTS] for p5 in range(5)])
        zero.append(a0)
        one.append(a1)
        two.append(a2)
    out = real9(zero)
    for part in (one, two):
        out += complex9([a[0] for a in part], [a[1] for a in part], -1.0)
    return out


def inverse45(v):
    zero, one, two = v[:5], v[5:14], v[14:]
    b0 = [None] * 9
    b0[0] = total([z[0] for z in zero])
    for p in range(1, 5):
        pr = total([zero[0][0]] + [cs(9, p * k)[0] * zero[k][0] for k in range(1, 5)])
        qr = total([cs(9, p * k)[1] * zero[k][1] for k in range(1, 5)])
        b0[p] = pr - qr
        b0[9 - p] = pr + qr
    b1 = complex9([a[0] for a in one], [a[1] for a in one], 1.0)
    b2 = complex9([a[0] for a in two], [a[1] for a in two], 1.0)
    c1, s1 = cs(5, 1)
    c2, s2 = cs(5, 2)
    out = [None] * PTS
    for p9 in range(9):
        (r1, i1), (r2, i2), base = b1[p9], b2[p9], b0[p9]
        ca = base + (c1 * r1 + c2 * r2)
        sa = s1 * i1 + s2 * i2
        cb = base + (c2 * r1 + c1 * r2)
        sb = s2 * i1 - s1 * i2
        vals = [base + (r1 + r2), ca - sa, cb - sb, cb + sb, ca + sa]
        for p5 in range(5):
            out[(9 * p5 + 5 * p9) % PTS] = vals[p5]
    return out


def fused_kernel(
    lat_count, lon_count,
    tr, cour, zs_in, zf_in, cut_in, damp_in,
    twid_in, kabs_in, scale_in, fwd_h_in, fwd_l_in, inv_h_in, inv_l_in,
    out,
    got_t, got_c, halo_t, halo_c, parts,
    zs, zf, cut, damp, twid, kabs, scale, fwd_h, fwd_l, inv_h, inv_l,
    line, moved, spec, wave,
    t_send, t_recv, c_send, c_recv, h_send, h_recv, hc_send, hc_recv, b_send, b_recv, b_local, local,
):
    tracer_count, _, row_count, columns = tr.shape
    lat = lax.axis_index("lat")
    lon = lax.axis_index("lon")
    up = lax.rem(lat + 1, lat_count)
    down = lax.rem(lat + lat_count - 1, lat_count)
    flip = 2 * lax.rem(lat, 2)
    peers = [lon + 1 - 2 * lax.rem(lon, 2), lax.rem(lon + 2, lon_count), lon_count - 1 - lon]
    levels = [pl.ds(2 * lax.rem(peer + flip, lon_count), 2) for peer in peers]
    mine = pl.ds(2 * lax.rem(lon + flip, lon_count), 2)

    staged = [
        (tr.at[:, mine], got_t.at[lon]), (cour.at[mine], got_c.at[lon]),
        (zs_in, zs), (zf_in, zf), (cut_in, cut), (damp_in, damp),
        (twid_in, twid), (kabs_in, kabs), (scale_in, scale),
        (fwd_h_in, fwd_h), (fwd_l_in, fwd_l), (inv_h_in, inv_h), (inv_l_in, inv_l),
    ]
    staged = [
        pltpu.make_async_copy(a, b, local.at[i]) for i, (a, b) in enumerate(staged)
    ]
    for copy in staged:
        copy.start()

    def remote(src, dst, send, recv, device):
        return pltpu.make_async_remote_copy(
            src_ref=src, dst_ref=dst, send_sem=send, recv_sem=recv,
            device_id=device, device_id_type=MESH,
        )

    def cells(t, m):
        return remote(
            tr.at[t, levels[m]], got_t.at[lon, t], t_send.at[t, m], t_recv.at[t, m],
            {"lat": lat, "lon": peers[m]},
        )

    def speeds(m):
        return remote(
            cour.at[levels[m]], got_c.at[lon], c_send.at[m], c_recv.at[m],
            {"lat": lat, "lon": peers[m]},
        )

    last = pl.ds(row_count - 1, 1)
    first = pl.ds(0, 1)
    far = pl.ds(2 - 2 * (lon // 2), 2)
    direct = [(mine, peers[1]), (levels[0], peers[2])]

    def rims(t):
        copies = []
        for j, (owned, owner) in enumerate(direct):
            copies.append((
                remote(tr.at[t, owned, last], halo_t.at[lon, t, :, last],
                       h_send.at[t, j], h_recv.at[t, j], {"lat": up, "lon": owner}),
                remote(tr.at[t, owned, first], halo_t.at[lon, t, :, first],
                       h_send.at[t, j + 3], h_recv.at[t, j + 3], {"lat": down, "lon": owner}),
            ))
        copies.append((
            remote(got_t.at[far, t, :, last], halo_t.at[far, t, :, last],
                   h_send.at[t, 2], h_recv.at[t, 2], {"lat": up, "lon": peers[1]}),
            remote(got_t.at[far, t, :, first], halo_t.at[far, t, :, first],
                   h_send.at[t, 5], h_recv.at[t, 5], {"lat": down, "lon": peers[1]}),
        ))
        return copies

    def rim_speeds():
        copies = [
            remote(cour.at[owned, first], halo_c.at[lon, :, first],
                   hc_send.at[j], hc_recv.at[j], {"lat": down, "lon": owner})
            for j, (owned, owner) in enumerate(direct)
        ]
        copies.append(
            remote(got_c.at[far, :, first], halo_c.at[far, :, first],
                   hc_send.at[2], hc_recv.at[2], {"lat": down, "lon": peers[1]})
        )
        return copies

    def reply(t, m):
        return remote(
            parts.at[peers[m], t], out.at[t, mine], b_send.at[t, m], b_recv.at[t, m],
            {"lat": lat, "lon": peers[m]},
        )

    def keep(t):
        return pltpu.make_async_copy(parts.at[lon, t], out.at[t, mine], b_local.at[t])

    barrier = pltpu.get_barrier_semaphore()
    has_north = (2 * lat_count - 3 - lat) // (lat_count - 1)
    has_south = (lat + lat_count - 2) // (lat_count - 1)
    north_there, south_there = has_north == 1, has_south == 1

    def signal(friend):
        pl.semaphore_signal(barrier, inc=1, device_id=friend, device_id_type=MESH)

    for peer in peers:
        signal({"lat": lat, "lon": peer})
    for owner in peers[1:]:
        pl.when(north_there)(functools.partial(signal, {"lat": up, "lon": owner}))
        pl.when(south_there)(functools.partial(signal, {"lat": down, "lon": owner}))
    pl.semaphore_wait(barrier, len(peers) + 2 * has_north + 2 * has_south)

    def each_rim(north_act, south_act, copies):
        @pl.when(north_act[0])
        def _():
            for north, _ in copies:
                getattr(north, north_act[1])()

        @pl.when(south_act[0])
        def _():
            for _, south in copies:
                getattr(south, south_act[1])()

    def start_rims(copies):
        each_rim((north_there, "start"), (south_there, "start"), copies)

    @pl.when(south_there)
    def _():
        for copy in rim_speeds()[:2]:
            copy.start()

    for m in (1, 2, 0):
        speeds(m).start()
    for t in range(tracer_count):
        start_rims(rims(t)[:2])
        for m in (1, 2, 0):
            cells(t, m).start()
    for copy in staged:
        copy.wait()

    def relay(t):
        cells(t, 1).wait_recv()
        cells(t, 2).wait_recv()
        start_rims(rims(t)[2:])

    speeds(1).wait_recv()
    speeds(2).wait_recv()
    pl.when(south_there)(rim_speeds()[2].start)
    relay(0)
    speeds(0).wait_recv()

    shape = (8, LANES)
    sub = lax.broadcasted_iota(jnp.int32, (8, columns), 0)
    sub1 = lax.broadcasted_iota(jnp.int32, shape, 0)
    lane = lax.broadcasted_iota(jnp.int32, shape, 1)

    def own_levels(ref):
        rows = ref[...].astype(jnp.float32)
        wide = jnp.concatenate([rows, rows], axis=0)
        a = lax.broadcasted_iota(jnp.int32, wide.shape, 0)
        b = lax.broadcasted_iota(jnp.int32, wide.shape, 1)
        at = 2 * lax.rem(lon + flip, lon_count) + (a // 4)
        value = jnp.sum(jnp.where(b == at, wide, 0.0), axis=1, keepdims=True)
        return jnp.broadcast_to(value, shape)

    def own_rows(ref):
        rows = ref[pl.ds(lat * row_count // LANES, 1)].astype(jnp.float32)
        wide = jnp.broadcast_to(rows, shape)
        at = lax.rem(lat * row_count, LANES) + (sub1 & 3)
        value = jnp.sum(jnp.where(lane == at, wide, 0.0), axis=1, keepdims=True)
        return jnp.broadcast_to(value, shape)

    s0 = own_levels(zs).astype(jnp.int32)
    s1 = s0 + 1
    here = own_levels(zf)
    cut8 = own_rows(cut).astype(jnp.int32)
    damp8 = own_rows(damp)
    face = lat * row_count + (sub & 3)
    open_s8 = face > 0
    open_n8 = face + 1 < lat_count * row_count
    quarter = lat_count // 4
    in_cap = (lat < quarter) | (lat >= lat_count - quarter)
    fold0, fold1 = (lane - s0) & (LANES - 1), (lane - s1) & (LANES - 1)
    own0, own1 = lane >= s0, lane >= s1

    def stacked(ref, *at):
        return jnp.concatenate([ref[(*at, 0)], ref[(*at, 1)]], axis=0)

    def tracer(t, carry):
        @pl.when(t < tracer_count - 1)
        def _():
            relay(t + 1)

        cells(t, 0).wait_recv()
        each_rim((south_there, "wait_recv"), (north_there, "wait_recv"), rims(t))
        for seg in range(lon_count):
            x = stacked(got_t, seg, t)
            c = stacked(got_c, seg)
            rim = stacked(halo_t, seg, t)
            rim_c = stacked(halo_c, seg)
            below = jnp.where((sub & 3) == 0, pltpu.roll(rim, 5, 0), pltpu.roll(x, 1, 0))
            flux = jnp.maximum(c, 0.0) * below + jnp.minimum(c, 0.0) * x
            flux = jnp.where(open_s8, flux, 0.0)
            hi, ch = pltpu.roll(rim, 3, 0), pltpu.roll(rim_c, 3, 0)
            edge = jnp.maximum(ch, 0.0) * x + jnp.minimum(ch, 0.0) * hi
            top = jnp.where((sub & 3) == 3, edge, pltpu.roll(flux, 7, 0))
            top = jnp.where(open_n8, top, 0.0)
            line[:, seg * columns : (seg + 1) * columns] = x + flux - top

        def gathered(p):
            tile = line[:, p * LANES : (p + 1) * LANES]
            return (
                jnp.take_along_axis(tile, fold0, axis=1),
                jnp.take_along_axis(tile, fold1, axis=1),
            )

        @pl.when(in_cap)
        def _():
            previous = gathered(PTS - 1)
            x = []
            for p in range(PTS):
                now = gathered(p)
                current = jnp.where(own0, now[0], previous[0])
                earlier = jnp.where(own1, now[1], previous[1])
                value = (1.0 - here) * current + here * earlier
                moved[:, p * LANES : (p + 1) * LANES] = value
                x.append(value)
                previous = now
            for r, (re, im) in enumerate(forward45(x)):
                tc, ts = twid[0, r : r + 1], twid[1, r : r + 1]
                if im is None:
                    spec[8 * r : 8 * r + 8, :LANES] = re * tc
                    spec[8 * r : 8 * r + 8, LANES:] = -(re * ts)
                else:
                    spec[8 * r : 8 * r + 8, :LANES] = re * tc + im * ts
                    spec[8 * r : 8 * r + 8, LANES:] = im * tc - re * ts
            wave[...] = split_dot(spec[...], fwd_h[...], fwd_l[...])
            for r in range(HALF):
                weight = jnp.where(kabs[r : r + 1] <= cut8, scale[r : r + 1], 0.0)
                wave[8 * r : 8 * r + 8, :] = wave[8 * r : 8 * r + 8, :] * weight
            spec[...] = split_dot(wave[...], inv_h[...], inv_l[...])
            v = []
            for r in range(HALF):
                tc, ts = twid[0, r : r + 1], twid[1, r : r + 1]
                re, im = spec[8 * r : 8 * r + 8, :LANES], spec[8 * r : 8 * r + 8, LANES:]
                v.append((re * tc - im * ts, re * ts + im * tc))
            for p, low in enumerate(inverse45(v)):
                cols = slice(p * LANES, (p + 1) * LANES)
                shifted = moved[:, cols]
                filtered = damp8 * shifted + (1.0 - damp8) * low
                line[:, cols] = filtered

        @pl.when(jnp.logical_not(in_cap))
        def _():
            previous = gathered(PTS - 1)
            for p in range(PTS):
                now = gathered(p)
                current = jnp.where(own0, now[0], previous[0])
                earlier = jnp.where(own1, now[1], previous[1])
                moved[:, p * LANES : (p + 1) * LANES] = (1.0 - here) * current + here * earlier
                previous = now
            line[...] = moved[...]

        for seg in range(lon_count):
            value = line[:, seg * columns : (seg + 1) * columns]
            parts[seg, t, 0] = value[:4]
            parts[seg, t, 1] = value[4:]
        for m in (1, 2, 0):
            reply(t, m).start()
        keep(t).start()
        return carry

    @pl.when(north_there)
    def _():
        for copy in rim_speeds():
            copy.wait_recv()

    lax.fori_loop(0, tracer_count, tracer, 0)

    for m in range(3):
        speeds(m).wait_send()

    @pl.when(south_there)
    def _():
        for copy in rim_speeds():
            copy.wait_send()

    for t in range(tracer_count):
        for m in range(3):
            cells(t, m).wait_send()
        each_rim((north_there, "wait_send"), (south_there, "wait_send"), rims(t))
        for m in range(3):
            reply(t, m).wait_send()
            back = reply(t, m)
            back.wait_recv()
        keep(t).wait()


def deliver_kernel(held, out, sem):
    copy = pltpu.make_async_copy(held, out, sem.at[0])
    copy.start()
    copy.wait()


def body(tracers, merid_courant, zonal_shift, zonal_fraction, cutoff, damping):
    tracer_count, level_count, row_count, columns = tracers.shape
    lat_count = lax.axis_size("lat")
    lon_count = lax.axis_size("lon")
    per = level_count // lon_count
    twid, kabs, scale, fwd, inv = tables(columns * lon_count)
    operands = (
        tracers, merid_courant, zonal_shift.T, zonal_fraction.T,
        cutoff.reshape(-1, LANES), damping.reshape(-1, LANES),
        jnp.asarray(twid), jnp.asarray(kabs), jnp.asarray(scale), *halves(fwd), *halves(inv),
    )
    any_space = pl.BlockSpec(memory_space=pl.ANY)
    operands = tuple(pltpu.with_memory_space_constraint(a, pltpu.HBM) for a in operands)
    tile = (per, row_count, columns)
    f32 = jnp.float32
    small = [pltpu.VMEM(a.shape, a.dtype) for a in operands[2:]]
    dma = pltpu.SemaphoreType.DMA
    result = pl.pallas_call(
        functools.partial(fused_kernel, lat_count, lon_count),
        out_shape=jax.ShapeDtypeStruct(tracers.shape, f32),
        in_specs=[any_space] * len(operands),
        out_specs=pl.BlockSpec(memory_space=pltpu.VMEM),
        scratch_shapes=[
            pltpu.VMEM((lon_count, tracer_count) + tile, f32),
            pltpu.VMEM((lon_count,) + tile, f32),
            pltpu.VMEM((lon_count, tracer_count) + tile, f32),
            pltpu.VMEM((lon_count,) + tile, f32),
            pltpu.VMEM((lon_count, tracer_count) + tile, f32),
            *small,
            pltpu.VMEM((8, columns * lon_count), f32),
            pltpu.VMEM((8, columns * lon_count), f32),
            pltpu.VMEM((HALF * 8, 2 * LANES), f32),
            pltpu.VMEM((HALF * 8, LANES), f32),
            dma((tracer_count, 3)), dma((tracer_count, 3)),
            dma((3,)), dma((3,)),
            dma((tracer_count, 6)), dma((tracer_count, 6)),
            dma((3,)), dma((3,)),
            dma((tracer_count, 3)), dma((tracer_count, 3)),
            dma((tracer_count,)),
            dma((len(operands),)),
        ],
        compiler_params=pltpu.CompilerParams(
            collective_id=0, has_side_effects=True, vmem_limit_bytes=16 << 20
        ),
    )(*operands)
    return pl.pallas_call(
        deliver_kernel,
        out_shape=jax.ShapeDtypeStruct(tracers.shape, f32),
        in_specs=[pl.BlockSpec(memory_space=pltpu.VMEM)],
        out_specs=any_space,
        scratch_shapes=[dma((1,))],
        compiler_params=pltpu.CompilerParams(vmem_limit_bytes=4 << 20),
    )(result)


def solution(mesh):
    placed = (
        P(None, None, "lat", "lon"),
        P(None, "lat", "lon"),
        P(None, "lat"),
        P(None, "lat"),
        P(),
        P(),
    )
    return jax.shard_map(
        body, mesh=mesh, in_specs=placed, out_specs=P(None, None, "lat", "lon"), check_vma=False
    )
```

```python
import functools
import math

import jax
import jax.numpy as jnp
import numpy as np
from jax import lax
from jax.experimental import pallas as pl
from jax.experimental.pallas import tpu as pltpu
from jax.sharding import PartitionSpec as P

MODES = 1024
LANES = 128
PTS = 45
HALF = 23
SPAN = 23
MESH = pl.DeviceIdType.MESH


def residues():
    found = []
    for k5 in range(3):
        for k9 in range(5 if k5 == 0 else 9):
            kk = next(k for k in range(PTS) if k % 5 == k5 and k % 9 == k9)
            found.append(kk if kk <= PTS // 2 else kk - PTS)
    return found


def tables(lon_cells):
    res = np.array(residues(), np.int64)
    lane = np.arange(LANES, dtype=np.int64)
    ang = (res[:, None] * lane[None, :] % lon_cells) * (2 * math.pi / lon_cells)
    twid = np.stack([np.cos(ang), np.sin(ang)]).astype(np.float32)
    half = LANES // 2
    k2 = np.zeros(LANES, np.int64)
    valid = np.zeros(LANES, bool)
    for part in range(2):
        k2[part * half : part * half + 2 * SPAN + 1] = np.arange(-SPAN, SPAN + 1)
        valid[part * half : part * half + 2 * SPAN + 1] = True
    mode = res[:, None] + PTS * k2[None, :]
    kabs = np.abs(mode)
    keep = valid[None, :] & (kabs < MODES) & ~((res[:, None] == 0) & (mode < 0))
    kabs = np.where(keep, kabs, 1 << 20).astype(np.int32)
    scale = np.where(mode == 0, 1.0, 2.0) / lon_cells
    scale = np.where(keep, scale, 0.0).astype(np.float32)
    ang2 = (k2[None, :] * lane[:, None] % LANES) * (2 * math.pi / LANES)
    c2 = np.cos(ang2) * valid[None, :]
    s2 = np.sin(ang2) * valid[None, :]
    first = np.arange(LANES) < half
    fwd = np.concatenate(
        [np.where(first, c2, -s2), np.where(first, s2, c2)], axis=0
    )
    inv = np.concatenate(
        [np.where(first, c2, -s2), np.where(first, s2, c2)], axis=0
    ).T
    return twid, kabs, scale, fwd.astype(np.float32), inv.astype(np.float32)


def halves(table):
    high = jnp.asarray(table).astype(jnp.bfloat16)
    low = (jnp.asarray(table) - high.astype(jnp.float32)).astype(jnp.bfloat16)
    return high, low


def split_dot(value, high, low):
    vh = value.astype(jnp.bfloat16)
    vl = (value - vh.astype(jnp.float32)).astype(jnp.bfloat16)
    dot = functools.partial(jnp.dot, preferred_element_type=jnp.float32)
    return dot(vh, high) + (dot(vl, high) + dot(vh, low))


def cs(count, turn):
    return math.cos(2 * math.pi * turn / count), math.sin(2 * math.pi * turn / count)


def real5(x):
    e1, o1, e2, o2 = x[1] + x[4], x[1] - x[4], x[2] + x[3], x[2] - x[3]
    c1, s1 = cs(5, 1)
    c2, s2 = cs(5, 2)
    return (
        x[0] + (e1 + e2),
        (x[0] + (c1 * e1 + c2 * e2), -(s1 * o1 + s2 * o2)),
        (x[0] + (c2 * e1 + c1 * e2), s1 * o2 - s2 * o1),
    )


def total(terms):
    while len(terms) > 1:
        terms = [sum(terms[i : i + 2][1:], terms[i]) for i in range(0, len(terms), 2)]
    return terms[0]


def real9(x):
    e = [x[j] + x[9 - j] for j in range(1, 5)]
    o = [x[j] - x[9 - j] for j in range(1, 5)]
    out = [(total([x[0]] + e), None)]
    for k in range(1, 5):
        re = total([x[0]] + [cs(9, j * k)[0] * e[j - 1] for j in range(1, 5)])
        im = total([-cs(9, j * k)[1] * o[j - 1] for j in range(1, 5)])
        out.append((re, im))
    return out


def complex9(re, im, sign):
    er = [re[j] + re[9 - j] for j in range(1, 5)]
    ei = [im[j] + im[9 - j] for j in range(1, 5)]
    dr = [re[j] - re[9 - j] for j in range(1, 5)]
    di = [im[j] - im[9 - j] for j in range(1, 5)]
    out = [None] * 9
    out[0] = (total([re[0]] + er), total([im[0]] + ei))
    for k in range(1, 5):
        c = [cs(9, j * k)[0] for j in range(1, 5)]
        s = [sign * cs(9, j * k)[1] for j in range(1, 5)]
        pr = total([re[0]] + [c[j] * er[j] for j in range(4)])
        pi = total([im[0]] + [c[j] * ei[j] for j in range(4)])
        qr = total([s[j] * di[j] for j in range(4)])
        qi = total([s[j] * dr[j] for j in range(4)])
        out[k] = (pr - qr, pi + qi)
        out[9 - k] = (pr + qr, pi - qi)
    return out


def forward45(x):
    zero, one, two = [], [], []
    for p9 in range(9):
        a0, a1, a2 = real5([x[(9 * p5 + 5 * p9) % PTS] for p5 in range(5)])
        zero.append(a0)
        one.append(a1)
        two.append(a2)
    out = real9(zero)
    for part in (one, two):
        out += complex9([a[0] for a in part], [a[1] for a in part], -1.0)
    return out


def inverse45(v):
    zero, one, two = v[:5], v[5:14], v[14:]
    b0 = [None] * 9
    b0[0] = total([z[0] for z in zero])
    for p in range(1, 5):
        pr = total([zero[0][0]] + [cs(9, p * k)[0] * zero[k][0] for k in range(1, 5)])
        qr = total([cs(9, p * k)[1] * zero[k][1] for k in range(1, 5)])
        b0[p] = pr - qr
        b0[9 - p] = pr + qr
    b1 = complex9([a[0] for a in one], [a[1] for a in one], 1.0)
    b2 = complex9([a[0] for a in two], [a[1] for a in two], 1.0)
    c1, s1 = cs(5, 1)
    c2, s2 = cs(5, 2)
    out = [None] * PTS
    for p9 in range(9):
        (r1, i1), (r2, i2), base = b1[p9], b2[p9], b0[p9]
        ca = base + (c1 * r1 + c2 * r2)
        sa = s1 * i1 + s2 * i2
        cb = base + (c2 * r1 + c1 * r2)
        sb = s2 * i1 - s1 * i2
        vals = [base + (r1 + r2), ca - sa, cb - sb, cb + sb, ca + sa]
        for p5 in range(5):
            out[(9 * p5 + 5 * p9) % PTS] = vals[p5]
    return out


def fused_kernel(
    lat_count, lon_count,
    tr, cour, zs_in, zf_in, cut_in, damp_in,
    twid_in, kabs_in, scale_in, fwd_h_in, fwd_l_in, inv_h_in, inv_l_in,
    out,
    got_t, got_c, halo_t, halo_c, parts,
    zs, zf, cut, damp, twid, kabs, scale, fwd_h, fwd_l, inv_h, inv_l,
    line, moved, spec, wave,
    t_send, t_recv, c_send, c_recv, h_send, h_recv, hc_send, hc_recv, b_send, b_recv, b_local, local, ready,
):
    tracer_count, _, row_count, columns = tr.shape
    lat = lax.axis_index("lat")
    lon = lax.axis_index("lon")
    up = lax.rem(lat + 1, lat_count)
    down = lax.rem(lat + lat_count - 1, lat_count)
    flip = 2 * lax.rem(lat, 2)
    peers = [lon + 1 - 2 * lax.rem(lon, 2), lax.rem(lon + 2, lon_count), lon_count - 1 - lon]
    levels = [pl.ds(2 * lax.rem(peer + flip, lon_count), 2) for peer in peers]
    mine = pl.ds(2 * lax.rem(lon + flip, lon_count), 2)

    staged = [
        (tr.at[:, mine], got_t.at[lon]), (cour.at[mine], got_c.at[lon]),
        (zs_in, zs), (zf_in, zf), (cut_in, cut), (damp_in, damp),
        (twid_in, twid), (kabs_in, kabs), (scale_in, scale),
        (fwd_h_in, fwd_h), (fwd_l_in, fwd_l), (inv_h_in, inv_h), (inv_l_in, inv_l),
    ]
    staged = [
        pltpu.make_async_copy(a, b, local.at[i]) for i, (a, b) in enumerate(staged)
    ]
    for copy in staged:
        copy.start()

    def remote(src, dst, send, recv, device):
        return pltpu.make_async_remote_copy(
            src_ref=src, dst_ref=dst, send_sem=send, recv_sem=recv,
            device_id=device, device_id_type=MESH,
        )

    def cells(t, m):
        return remote(
            tr.at[t, levels[m]], got_t.at[lon, t], t_send.at[t, m], t_recv.at[t, m],
            {"lat": lat, "lon": peers[m]},
        )

    def speeds(m):
        return remote(
            cour.at[levels[m]], got_c.at[lon], c_send.at[m], c_recv.at[m],
            {"lat": lat, "lon": peers[m]},
        )

    last = pl.ds(row_count - 1, 1)
    first = pl.ds(0, 1)
    far = pl.ds(2 - 2 * (lon // 2), 2)
    direct = [(mine, peers[1]), (levels[0], peers[2])]

    def rims(t):
        copies = []
        for j, (owned, owner) in enumerate(direct):
            copies.append((
                remote(tr.at[t, owned, last], halo_t.at[lon, t, :, last],
                       h_send.at[t, j], h_recv.at[t, j], {"lat": up, "lon": owner}),
                remote(tr.at[t, owned, first], halo_t.at[lon, t, :, first],
                       h_send.at[t, j + 3], h_recv.at[t, j + 3], {"lat": down, "lon": owner}),
            ))
        copies.append((
            remote(got_t.at[far, t, :, last], halo_t.at[far, t, :, last],
                   h_send.at[t, 2], h_recv.at[t, 2], {"lat": up, "lon": peers[1]}),
            remote(got_t.at[far, t, :, first], halo_t.at[far, t, :, first],
                   h_send.at[t, 5], h_recv.at[t, 5], {"lat": down, "lon": peers[1]}),
        ))
        return copies

    def rim_speeds():
        copies = [
            remote(cour.at[owned, first], halo_c.at[lon, :, first],
                   hc_send.at[j], hc_recv.at[j], {"lat": down, "lon": owner})
            for j, (owned, owner) in enumerate(direct)
        ]
        copies.append(
            remote(got_c.at[far, :, first], halo_c.at[far, :, first],
                   hc_send.at[2], hc_recv.at[2], {"lat": down, "lon": peers[1]})
        )
        return copies

    def reply(t, m, piece):
        rows = (pl.ds(1, row_count - 2), first, last)[piece]
        return remote(
            parts.at[peers[m], t, :, rows], out.at[t, mine, rows],
            b_send.at[t, 3 * m + piece], b_recv.at[t, 3 * m + piece],
            {"lat": lat, "lon": peers[m]},
        )

    def keep(t):
        return pltpu.make_async_copy(parts.at[lon, t], out.at[t, mine], b_local.at[t])

    barrier = pltpu.get_barrier_semaphore()
    has_north = (2 * lat_count - 3 - lat) // (lat_count - 1)
    has_south = (lat + lat_count - 2) // (lat_count - 1)
    north_there, south_there = has_north == 1, has_south == 1

    def signal(friend):
        pl.semaphore_signal(barrier, inc=1, device_id=friend, device_id_type=MESH)

    for peer in peers:
        signal({"lat": lat, "lon": peer})
    core = lax.rem(lon, 2)
    keeper = peers[1] + 1 - core
    pl.when(north_there)(functools.partial(signal, {"lat": up, "lon": keeper}))
    pl.when(south_there)(functools.partial(signal, {"lat": down, "lon": keeper}))
    pl.semaphore_wait(barrier, len(peers) + core * (2 * has_north + 2 * has_south))
    for m in (1, 2, 0):
        speeds(m).start()
    for t in range(tracer_count):
        for m in (1, 2, 0):
            cells(t, m).start()

    @pl.when(core == 1)
    def _():
        pl.semaphore_signal(ready, inc=1, device_id={"lat": lat, "lon": peers[0]}, device_id_type=MESH)

    @pl.when(core == 0)
    def _():
        pl.semaphore_wait(ready, 1)

    def each_rim(north_act, south_act, copies):
        @pl.when(north_act[0])
        def _():
            for north, _ in copies:
                getattr(north, north_act[1])()

        @pl.when(south_act[0])
        def _():
            for _, south in copies:
                getattr(south, south_act[1])()

    def start_rims(copies):
        each_rim((north_there, "start"), (south_there, "start"), copies)

    @pl.when(south_there)
    def _():
        for copy in rim_speeds()[:2]:
            copy.start()

    for t in range(tracer_count):
        start_rims(rims(t)[:2])
    for copy in staged:
        copy.wait()

    def relay(t):
        cells(t, 1).wait_recv()
        cells(t, 2).wait_recv()
        start_rims(rims(t)[2:])

    speeds(1).wait_recv()
    speeds(2).wait_recv()
    pl.when(south_there)(rim_speeds()[2].start)
    speeds(0).wait_recv()

    shape = (8, LANES)
    sub = lax.broadcasted_iota(jnp.int32, (8, columns), 0)
    sub1 = lax.broadcasted_iota(jnp.int32, shape, 0)
    lane = lax.broadcasted_iota(jnp.int32, shape, 1)

    def own_levels(ref):
        rows = ref[...].astype(jnp.float32)
        wide = jnp.concatenate([rows, rows], axis=0)
        a = lax.broadcasted_iota(jnp.int32, wide.shape, 0)
        b = lax.broadcasted_iota(jnp.int32, wide.shape, 1)
        at = 2 * lax.rem(lon + flip, lon_count) + (a // 4)
        value = jnp.sum(jnp.where(b == at, wide, 0.0), axis=1, keepdims=True)
        return jnp.broadcast_to(value, shape)

    def own_rows(ref):
        rows = ref[pl.ds(lat * row_count // LANES, 1)].astype(jnp.float32)
        wide = jnp.broadcast_to(rows, shape)
        at = lax.rem(lat * row_count, LANES) + (sub1 & 3)
        value = jnp.sum(jnp.where(lane == at, wide, 0.0), axis=1, keepdims=True)
        return jnp.broadcast_to(value, shape)

    face = lat * row_count + (sub & 3)
    open_s8 = face > 0
    open_n8 = face + 1 < lat_count * row_count
    quarter = lat_count // 4
    in_cap = (lat < quarter) | (lat >= lat_count - quarter)
    given = (own_levels(zs), own_levels(zf), own_rows(cut), own_rows(damp))

    def joined(edge, one, two):
        inner = (lax.broadcasted_iota(jnp.int32, one.shape, 0) + 1) & 2
        return jnp.where(inner == (0 if edge else 2), one, pltpu.roll(two, 2, 0))

    def stacked(ref, *at):
        return jnp.concatenate([ref[(*at, 0)], ref[(*at, 1)]], axis=0)

    def advected(seg, t, edge):
        x = stacked(got_t, seg, t)
        c = stacked(got_c, seg)
        below = pltpu.roll(x, 1, 0)
        if edge:
            rim = stacked(halo_t, seg, t)
            rim_c = stacked(halo_c, seg)
            below = jnp.where((sub & 3) == 0, pltpu.roll(rim, 5, 0), below)
        flux = jnp.maximum(c, 0.0) * below + jnp.minimum(c, 0.0) * x
        if edge:
            flux = jnp.where(open_s8, flux, 0.0)
        top = pltpu.roll(flux, 7, 0)
        if edge:
            hi, ch = pltpu.roll(rim, 3, 0), pltpu.roll(rim_c, 3, 0)
            top = jnp.where(
                (sub & 3) == 3, jnp.maximum(ch, 0.0) * x + jnp.minimum(ch, 0.0) * hi, top
            )
            top = jnp.where(open_n8, top, 0.0)
        return x + flux - top

    def group(edge, pair, carry):
        both = [2 * pair, 2 * pair + 1]
        for t in both:
            if edge:
                each_rim((south_there, "wait_recv"), (north_there, "wait_recv"), rims(t))
            else:
                relay(t)
                cells(t, 0).wait_recv()
        s0, here, cut8, damp8 = [joined(edge, value, value) for value in given]
        s0, cut8 = s0.astype(jnp.int32), cut8.astype(jnp.int32)
        s1 = s0 + 1
        fold0, fold1 = (lane - s0) & (LANES - 1), (lane - s1) & (LANES - 1)
        own0, own1 = lane >= s0, lane >= s1
        for seg in range(lon_count):
            line[:, seg * columns : (seg + 1) * columns] = joined(
                edge, advected(seg, both[0], edge), advected(seg, both[1], edge)
            )

        def gathered(p):
            tile = line[:, p * LANES : (p + 1) * LANES]
            return (
                jnp.take_along_axis(tile, fold0, axis=1),
                jnp.take_along_axis(tile, fold1, axis=1),
            )

        @pl.when(in_cap)
        def _():
            previous = gathered(PTS - 1)
            x = []
            for p in range(PTS):
                now = gathered(p)
                current = jnp.where(own0, now[0], previous[0])
                earlier = jnp.where(own1, now[1], previous[1])
                value = (1.0 - here) * current + here * earlier
                moved[:, p * LANES : (p + 1) * LANES] = value
                x.append(value)
                previous = now
            for r, (re, im) in enumerate(forward45(x)):
                tc, ts = twid[0, r : r + 1], twid[1, r : r + 1]
                if im is None:
                    spec[8 * r : 8 * r + 8, :LANES] = re * tc
                    spec[8 * r : 8 * r + 8, LANES:] = -(re * ts)
                else:
                    spec[8 * r : 8 * r + 8, :LANES] = re * tc + im * ts
                    spec[8 * r : 8 * r + 8, LANES:] = im * tc - re * ts
            wave[...] = split_dot(spec[...], fwd_h[...], fwd_l[...])
            for r in range(HALF):
                weight = jnp.where(kabs[r : r + 1] <= cut8, scale[r : r + 1], 0.0)
                wave[8 * r : 8 * r + 8, :] = wave[8 * r : 8 * r + 8, :] * weight
            spec[...] = split_dot(wave[...], inv_h[...], inv_l[...])
            v = []
            for r in range(HALF):
                tc, ts = twid[0, r : r + 1], twid[1, r : r + 1]
                re, im = spec[8 * r : 8 * r + 8, :LANES], spec[8 * r : 8 * r + 8, LANES:]
                v.append((re * tc - im * ts, re * ts + im * tc))
            for p, low in enumerate(inverse45(v)):
                cols = slice(p * LANES, (p + 1) * LANES)
                shifted = moved[:, cols]
                filtered = damp8 * shifted + (1.0 - damp8) * low
                line[:, cols] = filtered

        @pl.when(jnp.logical_not(in_cap))
        def _():
            previous = gathered(PTS - 1)
            for p in range(PTS):
                now = gathered(p)
                current = jnp.where(own0, now[0], previous[0])
                earlier = jnp.where(own1, now[1], previous[1])
                moved[:, p * LANES : (p + 1) * LANES] = (1.0 - here) * current + here * earlier
                previous = now
            line[...] = moved[...]

        for seg in range(lon_count):
            value = line[:, seg * columns : (seg + 1) * columns]
            for t, rows in zip(both, (value, pltpu.roll(value, 6, 0))):
                for level in range(2):
                    tile = rows[4 * level : 4 * level + 4]
                    if edge:
                        parts[seg, t, level, 0:1] = tile[0:1]
                        parts[seg, t, level, 3:4] = tile[3:4]
                    else:
                        parts[seg, t, level] = tile
        for t in both:
            for piece in ((1, 2) if edge else (0,)):
                for m in (1, 2, 0):
                    reply(t, m, piece).start()
            if edge:
                keep(t).start()
        return carry

    lax.fori_loop(0, tracer_count // 2, functools.partial(group, False), 0)

    @pl.when(north_there)
    def _():
        for copy in rim_speeds():
            copy.wait_recv()

    lax.fori_loop(0, tracer_count // 2, functools.partial(group, True), 0)

    for m in range(3):
        speeds(m).wait_send()

    @pl.when(south_there)
    def _():
        for copy in rim_speeds():
            copy.wait_send()

    for t in range(tracer_count):
        for m in range(3):
            cells(t, m).wait_send()
        each_rim((north_there, "wait_send"), (south_there, "wait_send"), rims(t))
        for m in range(3):
            for piece in range(3):
                back = reply(t, m, piece)
                back.wait_send()
                back.wait_recv()
        keep(t).wait()


def deliver_kernel(held, out, sem):
    copy = pltpu.make_async_copy(held, out, sem.at[0])
    copy.start()
    copy.wait()


def body(tracers, merid_courant, zonal_shift, zonal_fraction, cutoff, damping):
    tracer_count, level_count, row_count, columns = tracers.shape
    lat_count = lax.axis_size("lat")
    lon_count = lax.axis_size("lon")
    per = level_count // lon_count
    twid, kabs, scale, fwd, inv = tables(columns * lon_count)
    operands = (
        tracers, merid_courant, zonal_shift.T, zonal_fraction.T,
        cutoff.reshape(-1, LANES), damping.reshape(-1, LANES),
        jnp.asarray(twid), jnp.asarray(kabs), jnp.asarray(scale), *halves(fwd), *halves(inv),
    )
    any_space = pl.BlockSpec(memory_space=pl.ANY)
    operands = tuple(pltpu.with_memory_space_constraint(a, pltpu.HBM) for a in operands)
    tile = (per, row_count, columns)
    f32 = jnp.float32
    small = [pltpu.VMEM(a.shape, a.dtype) for a in operands[2:]]
    dma = pltpu.SemaphoreType.DMA
    result = pl.pallas_call(
        functools.partial(fused_kernel, lat_count, lon_count),
        out_shape=jax.ShapeDtypeStruct(tracers.shape, f32),
        in_specs=[any_space] * len(operands),
        out_specs=pl.BlockSpec(memory_space=pltpu.VMEM),
        scratch_shapes=[
            pltpu.VMEM((lon_count, tracer_count) + tile, f32),
            pltpu.VMEM((lon_count,) + tile, f32),
            pltpu.VMEM((lon_count, tracer_count) + tile, f32),
            pltpu.VMEM((lon_count,) + tile, f32),
            pltpu.VMEM((lon_count, tracer_count) + tile, f32),
            *small,
            pltpu.VMEM((8, columns * lon_count), f32),
            pltpu.VMEM((8, columns * lon_count), f32),
            pltpu.VMEM((HALF * 8, 2 * LANES), f32),
            pltpu.VMEM((HALF * 8, LANES), f32),
            dma((tracer_count, 3)), dma((tracer_count, 3)),
            dma((3,)), dma((3,)),
            dma((tracer_count, 6)), dma((tracer_count, 6)),
            dma((3,)), dma((3,)),
            dma((tracer_count, 9)), dma((tracer_count, 9)),
            dma((tracer_count,)),
            dma((len(operands),)),
            pltpu.SemaphoreType.REGULAR,
        ],
        compiler_params=pltpu.CompilerParams(
            collective_id=0, has_side_effects=True, vmem_limit_bytes=16 << 20
        ),
    )(*operands)
    return pl.pallas_call(
        deliver_kernel,
        out_shape=jax.ShapeDtypeStruct(tracers.shape, f32),
        in_specs=[pl.BlockSpec(memory_space=pltpu.VMEM)],
        out_specs=any_space,
        scratch_shapes=[dma((1,))],
        compiler_params=pltpu.CompilerParams(vmem_limit_bytes=4 << 20),
    )(result)


def solution(mesh):
    placed = (
        P(None, None, "lat", "lon"),
        P(None, "lat", "lon"),
        P(None, "lat"),
        P(None, "lat"),
        P(),
        P(),
    )
    return jax.shard_map(
        body, mesh=mesh, in_specs=placed, out_specs=P(None, None, "lat", "lon"), check_vma=False
    )
```

```python
import functools
import math

import jax
import jax.numpy as jnp
import numpy as np
from jax import lax
from jax.experimental import pallas as pl
from jax.experimental.pallas import tpu as pltpu
from jax.sharding import PartitionSpec as P

MODES = 1024
LANES = 128
PTS = 45
HALF = 23
SPAN = 23
MESH = pl.DeviceIdType.MESH


def residues():
    found = []
    for k5 in range(3):
        for k9 in range(5 if k5 == 0 else 9):
            kk = next(k for k in range(PTS) if k % 5 == k5 and k % 9 == k9)
            found.append(kk if kk <= PTS // 2 else kk - PTS)
    return found


def tables(lon_cells):
    res = np.array(residues(), np.int64)
    lane = np.arange(LANES, dtype=np.int64)
    ang = (res[:, None] * lane[None, :] % lon_cells) * (2 * math.pi / lon_cells)
    twid = np.stack([np.cos(ang), np.sin(ang)]).astype(np.float32)
    half = LANES // 2
    k2 = np.zeros(LANES, np.int64)
    valid = np.zeros(LANES, bool)
    for part in range(2):
        k2[part * half : part * half + 2 * SPAN + 1] = np.arange(-SPAN, SPAN + 1)
        valid[part * half : part * half + 2 * SPAN + 1] = True
    mode = res[:, None] + PTS * k2[None, :]
    kabs = np.abs(mode)
    keep = valid[None, :] & (kabs < MODES) & ~((res[:, None] == 0) & (mode < 0))
    kabs = np.where(keep, kabs, 1 << 20).astype(np.int32)
    scale = np.where(mode == 0, 1.0, 2.0) / lon_cells
    scale = np.where(keep, scale, 0.0).astype(np.float32)
    ang2 = (k2[None, :] * lane[:, None] % LANES) * (2 * math.pi / LANES)
    c2 = np.cos(ang2) * valid[None, :]
    s2 = np.sin(ang2) * valid[None, :]
    first = np.arange(LANES) < half
    fwd = np.concatenate(
        [np.where(first, c2, -s2), np.where(first, s2, c2)], axis=0
    )
    inv = np.concatenate(
        [np.where(first, c2, -s2), np.where(first, s2, c2)], axis=0
    ).T
    return twid, kabs, scale, fwd.astype(np.float32), inv.astype(np.float32)


def halves(table):
    high = jnp.asarray(table).astype(jnp.bfloat16)
    low = (jnp.asarray(table) - high.astype(jnp.float32)).astype(jnp.bfloat16)
    return high, low


def split_dot(value, high, low):
    vh = value.astype(jnp.bfloat16)
    vl = (value - vh.astype(jnp.float32)).astype(jnp.bfloat16)
    dot = functools.partial(jnp.dot, preferred_element_type=jnp.float32)
    return dot(vh, high) + (dot(vl, high) + dot(vh, low))


def cs(count, turn):
    return math.cos(2 * math.pi * turn / count), math.sin(2 * math.pi * turn / count)


def real5(x):
    e1, o1, e2, o2 = x[1] + x[4], x[1] - x[4], x[2] + x[3], x[2] - x[3]
    c1, s1 = cs(5, 1)
    c2, s2 = cs(5, 2)
    return (
        x[0] + (e1 + e2),
        (x[0] + (c1 * e1 + c2 * e2), -(s1 * o1 + s2 * o2)),
        (x[0] + (c2 * e1 + c1 * e2), s1 * o2 - s2 * o1),
    )


def total(terms):
    while len(terms) > 1:
        terms = [sum(terms[i : i + 2][1:], terms[i]) for i in range(0, len(terms), 2)]
    return terms[0]


def real9(x):
    e = [x[j] + x[9 - j] for j in range(1, 5)]
    o = [x[j] - x[9 - j] for j in range(1, 5)]
    out = [(total([x[0]] + e), None)]
    for k in range(1, 5):
        re = total([x[0]] + [cs(9, j * k)[0] * e[j - 1] for j in range(1, 5)])
        im = total([-cs(9, j * k)[1] * o[j - 1] for j in range(1, 5)])
        out.append((re, im))
    return out


def complex9(re, im, sign):
    er = [re[j] + re[9 - j] for j in range(1, 5)]
    ei = [im[j] + im[9 - j] for j in range(1, 5)]
    dr = [re[j] - re[9 - j] for j in range(1, 5)]
    di = [im[j] - im[9 - j] for j in range(1, 5)]
    out = [None] * 9
    out[0] = (total([re[0]] + er), total([im[0]] + ei))
    for k in range(1, 5):
        c = [cs(9, j * k)[0] for j in range(1, 5)]
        s = [sign * cs(9, j * k)[1] for j in range(1, 5)]
        pr = total([re[0]] + [c[j] * er[j] for j in range(4)])
        pi = total([im[0]] + [c[j] * ei[j] for j in range(4)])
        qr = total([s[j] * di[j] for j in range(4)])
        qi = total([s[j] * dr[j] for j in range(4)])
        out[k] = (pr - qr, pi + qi)
        out[9 - k] = (pr + qr, pi - qi)
    return out


def forward45(x):
    zero, one, two = [], [], []
    for p9 in range(9):
        a0, a1, a2 = real5([x[(9 * p5 + 5 * p9) % PTS] for p5 in range(5)])
        zero.append(a0)
        one.append(a1)
        two.append(a2)
    out = real9(zero)
    for part in (one, two):
        out += complex9([a[0] for a in part], [a[1] for a in part], -1.0)
    return out


def inverse45(v):
    zero, one, two = v[:5], v[5:14], v[14:]
    b0 = [None] * 9
    b0[0] = total([z[0] for z in zero])
    for p in range(1, 5):
        pr = total([zero[0][0]] + [cs(9, p * k)[0] * zero[k][0] for k in range(1, 5)])
        qr = total([cs(9, p * k)[1] * zero[k][1] for k in range(1, 5)])
        b0[p] = pr - qr
        b0[9 - p] = pr + qr
    b1 = complex9([a[0] for a in one], [a[1] for a in one], 1.0)
    b2 = complex9([a[0] for a in two], [a[1] for a in two], 1.0)
    c1, s1 = cs(5, 1)
    c2, s2 = cs(5, 2)
    out = [None] * PTS
    for p9 in range(9):
        (r1, i1), (r2, i2), base = b1[p9], b2[p9], b0[p9]
        ca = base + (c1 * r1 + c2 * r2)
        sa = s1 * i1 + s2 * i2
        cb = base + (c2 * r1 + c1 * r2)
        sb = s2 * i1 - s1 * i2
        vals = [base + (r1 + r2), ca - sa, cb - sb, cb + sb, ca + sa]
        for p5 in range(5):
            out[(9 * p5 + 5 * p9) % PTS] = vals[p5]
    return out


def fused_kernel(
    lat_count, lon_count,
    tr, cour, zs_in, zf_in, cut_in, damp_in,
    twid_in, kabs_in, scale_in, fwd_h_in, fwd_l_in, inv_h_in, inv_l_in,
    out,
    got_t, got_c, halo_t, halo_c, parts,
    zs, zf, cut, damp, twid, kabs, scale, fwd_h, fwd_l, inv_h, inv_l,
    line, moved, spec, wave,
    t_send, t_recv, c_send, c_recv, h_send, h_recv, hc_send, hc_recv, b_send, b_recv, b_local, local, ready,
):
    tracer_count, _, row_count, columns = tr.shape
    lat = lax.axis_index("lat")
    lon = lax.axis_index("lon")
    up = lax.rem(lat + 1, lat_count)
    down = lax.rem(lat + lat_count - 1, lat_count)
    flip = 2 * lax.rem(lat, 2)
    peers = [lon + 1 - 2 * lax.rem(lon, 2), lax.rem(lon + 2, lon_count), lon_count - 1 - lon]
    levels = [pl.ds(2 * lax.rem(peer + flip, lon_count), 2) for peer in peers]
    mine = pl.ds(2 * lax.rem(lon + flip, lon_count), 2)

    staged = [
        (tr.at[:, mine], got_t.at[lon]), (cour.at[mine], got_c.at[lon]),
        (zs_in, zs), (zf_in, zf), (cut_in, cut), (damp_in, damp),
        (twid_in, twid), (kabs_in, kabs), (scale_in, scale),
        (fwd_h_in, fwd_h), (fwd_l_in, fwd_l), (inv_h_in, inv_h), (inv_l_in, inv_l),
    ]
    staged = [
        pltpu.make_async_copy(a, b, local.at[i]) for i, (a, b) in enumerate(staged)
    ]
    for copy in staged:
        copy.start()

    def remote(src, dst, send, recv, device):
        return pltpu.make_async_remote_copy(
            src_ref=src, dst_ref=dst, send_sem=send, recv_sem=recv,
            device_id=device, device_id_type=MESH,
        )

    last = pl.ds(row_count - 1, 1)
    first = pl.ds(0, 1)
    pieces = (pl.ds(1, row_count - 2), first, last)

    def cells(t, m, piece):
        return remote(
            tr.at[t, levels[m], pieces[piece]], got_t.at[lon, t, :, pieces[piece]],
            t_send.at[t, 3 * m + piece], t_recv.at[t, 3 * m + piece],
            {"lat": lat, "lon": peers[m]},
        )

    def speeds(m):
        return remote(
            cour.at[levels[m]], got_c.at[lon], c_send.at[m], c_recv.at[m],
            {"lat": lat, "lon": peers[m]},
        )

    far = pl.ds(2 - 2 * (lon // 2), 2)
    direct = [(mine, peers[1]), (levels[0], peers[2])]

    def rims(t):
        copies = []
        for j, (owned, owner) in enumerate(direct):
            copies.append((
                remote(tr.at[t, owned, last], halo_t.at[lon, t, :, last],
                       h_send.at[t, j], h_recv.at[t, j], {"lat": up, "lon": owner}),
                remote(tr.at[t, owned, first], halo_t.at[lon, t, :, first],
                       h_send.at[t, j + 3], h_recv.at[t, j + 3], {"lat": down, "lon": owner}),
            ))
        copies.append((
            remote(got_t.at[far, t, :, last], halo_t.at[far, t, :, last],
                   h_send.at[t, 2], h_recv.at[t, 2], {"lat": up, "lon": peers[1]}),
            remote(got_t.at[far, t, :, first], halo_t.at[far, t, :, first],
                   h_send.at[t, 5], h_recv.at[t, 5], {"lat": down, "lon": peers[1]}),
        ))
        return copies

    def rim_speeds():
        copies = [
            remote(cour.at[owned, first], halo_c.at[lon, :, first],
                   hc_send.at[j], hc_recv.at[j], {"lat": down, "lon": owner})
            for j, (owned, owner) in enumerate(direct)
        ]
        copies.append(
            remote(got_c.at[far, :, first], halo_c.at[far, :, first],
                   hc_send.at[2], hc_recv.at[2], {"lat": down, "lon": peers[1]})
        )
        return copies

    def reply(t, m, piece):
        rows = pieces[piece]
        return remote(
            parts.at[peers[m], t, :, rows], out.at[t, mine, rows],
            b_send.at[t, 3 * m + piece], b_recv.at[t, 3 * m + piece],
            {"lat": lat, "lon": peers[m]},
        )

    def keep(t):
        return pltpu.make_async_copy(parts.at[lon, t], out.at[t, mine], b_local.at[t])

    barrier = pltpu.get_barrier_semaphore()
    has_north = (2 * lat_count - 3 - lat) // (lat_count - 1)
    has_south = (lat + lat_count - 2) // (lat_count - 1)
    north_there, south_there = has_north == 1, has_south == 1

    def signal(friend):
        pl.semaphore_signal(barrier, inc=1, device_id=friend, device_id_type=MESH)

    for peer in peers:
        signal({"lat": lat, "lon": peer})
    core = lax.rem(lon, 2)
    keeper = peers[1] + 1 - core
    pl.when(north_there)(functools.partial(signal, {"lat": up, "lon": keeper}))
    pl.when(south_there)(functools.partial(signal, {"lat": down, "lon": keeper}))
    pl.semaphore_wait(barrier, len(peers) + core * (2 * has_north + 2 * has_south))
    for m in (1, 2, 0):
        speeds(m).start()
    for group_of in ((0,), (1,), (2, 3)):
        for piece in (1, 2, 0):
            for t in group_of:
                for m in (1, 2, 0):
                    cells(t, m, piece).start()

    @pl.when(core == 1)
    def _():
        pl.semaphore_signal(ready, inc=1, device_id={"lat": lat, "lon": peers[0]}, device_id_type=MESH)

    @pl.when(core == 0)
    def _():
        pl.semaphore_wait(ready, 1)

    def each_rim(north_act, south_act, copies):
        @pl.when(north_act[0])
        def _():
            for north, _ in copies:
                getattr(north, north_act[1])()

        @pl.when(south_act[0])
        def _():
            for _, south in copies:
                getattr(south, south_act[1])()

    def start_rims(copies):
        each_rim((north_there, "start"), (south_there, "start"), copies)

    @pl.when(south_there)
    def _():
        for copy in rim_speeds()[:2]:
            copy.start()

    for t in range(tracer_count):
        start_rims(rims(t)[:2])
    for copy in staged:
        copy.wait()

    def relay(t):
        for m in (1, 2):
            for piece in (1, 2):
                cells(t, m, piece).wait_recv()
        start_rims(rims(t)[2:])

    speeds(1).wait_recv()
    speeds(2).wait_recv()
    pl.when(south_there)(rim_speeds()[2].start)
    speeds(0).wait_recv()

    shape = (8, LANES)
    sub = lax.broadcasted_iota(jnp.int32, (8, columns), 0)
    sub1 = lax.broadcasted_iota(jnp.int32, shape, 0)
    lane = lax.broadcasted_iota(jnp.int32, shape, 1)

    def own_levels(ref):
        rows = ref[...].astype(jnp.float32)
        wide = jnp.concatenate([rows, rows], axis=0)
        a = lax.broadcasted_iota(jnp.int32, wide.shape, 0)
        b = lax.broadcasted_iota(jnp.int32, wide.shape, 1)
        at = 2 * lax.rem(lon + flip, lon_count) + (a // 4)
        value = jnp.sum(jnp.where(b == at, wide, 0.0), axis=1, keepdims=True)
        return jnp.broadcast_to(value, shape)

    def own_rows(ref):
        rows = ref[pl.ds(lat * row_count // LANES, 1)].astype(jnp.float32)
        wide = jnp.broadcast_to(rows, shape)
        at = lax.rem(lat * row_count, LANES) + (sub1 & 3)
        value = jnp.sum(jnp.where(lane == at, wide, 0.0), axis=1, keepdims=True)
        return jnp.broadcast_to(value, shape)

    face = lat * row_count + (sub & 3)
    open_s8 = face > 0
    open_n8 = face + 1 < lat_count * row_count
    quarter = lat_count // 4
    in_cap = (lat < quarter) | (lat >= lat_count - quarter)
    given = (own_levels(zs), own_levels(zf), own_rows(cut), own_rows(damp))

    def joined(edge, one, two):
        inner = (lax.broadcasted_iota(jnp.int32, one.shape, 0) + 1) & 2
        return jnp.where(inner == (0 if edge else 2), one, pltpu.roll(two, 2, 0))

    def stacked(ref, *at):
        return jnp.concatenate([ref[(*at, 0)], ref[(*at, 1)]], axis=0)

    def advected(seg, t, edge):
        x = stacked(got_t, seg, t)
        c = stacked(got_c, seg)
        below = pltpu.roll(x, 1, 0)
        if edge:
            rim = stacked(halo_t, seg, t)
            rim_c = stacked(halo_c, seg)
            below = jnp.where((sub & 3) == 0, pltpu.roll(rim, 5, 0), below)
        flux = jnp.maximum(c, 0.0) * below + jnp.minimum(c, 0.0) * x
        if edge:
            flux = jnp.where(open_s8, flux, 0.0)
        top = pltpu.roll(flux, 7, 0)
        if edge:
            hi, ch = pltpu.roll(rim, 3, 0), pltpu.roll(rim_c, 3, 0)
            top = jnp.where(
                (sub & 3) == 3, jnp.maximum(ch, 0.0) * x + jnp.minimum(ch, 0.0) * hi, top
            )
            top = jnp.where(open_n8, top, 0.0)
        return x + flux - top

    def group(edge, pair, carry):
        both = [2 * pair, 2 * pair + 1]
        if not edge:
            for t in both:
                relay(t)
        for t in both:
            if edge:
                each_rim((south_there, "wait_recv"), (north_there, "wait_recv"), rims(t))
            else:
                for m in range(3):
                    cells(t, m, 0).wait_recv()
                for piece in (1, 2):
                    cells(t, 0, piece).wait_recv()
        s0, here, cut8, damp8 = [joined(edge, value, value) for value in given]
        s0, cut8 = s0.astype(jnp.int32), cut8.astype(jnp.int32)
        s1 = s0 + 1
        fold0, fold1 = (lane - s0) & (LANES - 1), (lane - s1) & (LANES - 1)
        own0, own1 = lane >= s0, lane >= s1
        for seg in range(lon_count):
            line[:, seg * columns : (seg + 1) * columns] = joined(
                edge, advected(seg, both[0], edge), advected(seg, both[1], edge)
            )

        def gathered(p):
            tile = line[:, p * LANES : (p + 1) * LANES]
            return (
                jnp.take_along_axis(tile, fold0, axis=1),
                jnp.take_along_axis(tile, fold1, axis=1),
            )

        @pl.when(in_cap)
        def _():
            previous = gathered(PTS - 1)
            x = []
            for p in range(PTS):
                now = gathered(p)
                current = jnp.where(own0, now[0], previous[0])
                earlier = jnp.where(own1, now[1], previous[1])
                value = (1.0 - here) * current + here * earlier
                moved[:, p * LANES : (p + 1) * LANES] = value
                x.append(value)
                previous = now
            for r, (re, im) in enumerate(forward45(x)):
                tc, ts = twid[0, r : r + 1], twid[1, r : r + 1]
                if im is None:
                    spec[8 * r : 8 * r + 8, :LANES] = re * tc
                    spec[8 * r : 8 * r + 8, LANES:] = -(re * ts)
                else:
                    spec[8 * r : 8 * r + 8, :LANES] = re * tc + im * ts
                    spec[8 * r : 8 * r + 8, LANES:] = im * tc - re * ts
            wave[...] = split_dot(spec[...], fwd_h[...], fwd_l[...])
            for r in range(HALF):
                weight = jnp.where(kabs[r : r + 1] <= cut8, scale[r : r + 1], 0.0)
                wave[8 * r : 8 * r + 8, :] = wave[8 * r : 8 * r + 8, :] * weight
            spec[...] = split_dot(wave[...], inv_h[...], inv_l[...])
            v = []
            for r in range(HALF):
                tc, ts = twid[0, r : r + 1], twid[1, r : r + 1]
                re, im = spec[8 * r : 8 * r + 8, :LANES], spec[8 * r : 8 * r + 8, LANES:]
                v.append((re * tc - im * ts, re * ts + im * tc))
            for p, low in enumerate(inverse45(v)):
                cols = slice(p * LANES, (p + 1) * LANES)
                shifted = moved[:, cols]
                filtered = damp8 * shifted + (1.0 - damp8) * low
                line[:, cols] = filtered

        @pl.when(jnp.logical_not(in_cap))
        def _():
            previous = gathered(PTS - 1)
            for p in range(PTS):
                now = gathered(p)
                current = jnp.where(own0, now[0], previous[0])
                earlier = jnp.where(own1, now[1], previous[1])
                moved[:, p * LANES : (p + 1) * LANES] = (1.0 - here) * current + here * earlier
                previous = now
            line[...] = moved[...]

        for seg in range(lon_count):
            value = line[:, seg * columns : (seg + 1) * columns]
            for t, rows in zip(both, (value, pltpu.roll(value, 6, 0))):
                for level in range(2):
                    tile = rows[4 * level : 4 * level + 4]
                    if edge:
                        parts[seg, t, level, 0:1] = tile[0:1]
                        parts[seg, t, level, 3:4] = tile[3:4]
                    else:
                        parts[seg, t, level] = tile
        for t in both:
            for piece in ((1, 2) if edge else (0,)):
                for m in (1, 2, 0):
                    reply(t, m, piece).start()
            if edge:
                keep(t).start()
        return carry

    lax.fori_loop(0, tracer_count // 2, functools.partial(group, False), 0)

    @pl.when(north_there)
    def _():
        for copy in rim_speeds():
            copy.wait_recv()

    lax.fori_loop(0, tracer_count // 2, functools.partial(group, True), 0)

    for m in range(3):
        speeds(m).wait_send()

    @pl.when(south_there)
    def _():
        for copy in rim_speeds():
            copy.wait_send()

    for t in range(tracer_count):
        for m in range(3):
            for piece in range(3):
                cells(t, m, piece).wait_send()
        each_rim((north_there, "wait_send"), (south_there, "wait_send"), rims(t))
        for m in range(3):
            for piece in range(3):
                back = reply(t, m, piece)
                back.wait_send()
                back.wait_recv()
        keep(t).wait()


def deliver_kernel(held, out, sem):
    copy = pltpu.make_async_copy(held, out, sem.at[0])
    copy.start()
    copy.wait()


def body(tracers, merid_courant, zonal_shift, zonal_fraction, cutoff, damping):
    tracer_count, level_count, row_count, columns = tracers.shape
    lat_count = lax.axis_size("lat")
    lon_count = lax.axis_size("lon")
    per = level_count // lon_count
    twid, kabs, scale, fwd, inv = tables(columns * lon_count)
    operands = (
        tracers, merid_courant, zonal_shift.T, zonal_fraction.T,
        cutoff.reshape(-1, LANES), damping.reshape(-1, LANES),
        jnp.asarray(twid), jnp.asarray(kabs), jnp.asarray(scale), *halves(fwd), *halves(inv),
    )
    any_space = pl.BlockSpec(memory_space=pl.ANY)
    operands = tuple(pltpu.with_memory_space_constraint(a, pltpu.HBM) for a in operands)
    tile = (per, row_count, columns)
    f32 = jnp.float32
    small = [pltpu.VMEM(a.shape, a.dtype) for a in operands[2:]]
    dma = pltpu.SemaphoreType.DMA
    result = pl.pallas_call(
        functools.partial(fused_kernel, lat_count, lon_count),
        out_shape=jax.ShapeDtypeStruct(tracers.shape, f32),
        in_specs=[any_space] * len(operands),
        out_specs=pl.BlockSpec(memory_space=pltpu.VMEM),
        scratch_shapes=[
            pltpu.VMEM((lon_count, tracer_count) + tile, f32),
            pltpu.VMEM((lon_count,) + tile, f32),
            pltpu.VMEM((lon_count, tracer_count) + tile, f32),
            pltpu.VMEM((lon_count,) + tile, f32),
            pltpu.VMEM((lon_count, tracer_count) + tile, f32),
            *small,
            pltpu.VMEM((8, columns * lon_count), f32),
            pltpu.VMEM((8, columns * lon_count), f32),
            pltpu.VMEM((HALF * 8, 2 * LANES), f32),
            pltpu.VMEM((HALF * 8, LANES), f32),
            dma((tracer_count, 9)), dma((tracer_count, 9)),
            dma((3,)), dma((3,)),
            dma((tracer_count, 6)), dma((tracer_count, 6)),
            dma((3,)), dma((3,)),
            dma((tracer_count, 9)), dma((tracer_count, 9)),
            dma((tracer_count,)),
            dma((len(operands),)),
            pltpu.SemaphoreType.REGULAR,
        ],
        compiler_params=pltpu.CompilerParams(
            collective_id=0, has_side_effects=True, vmem_limit_bytes=16 << 20
        ),
    )(*operands)
    return pl.pallas_call(
        deliver_kernel,
        out_shape=jax.ShapeDtypeStruct(tracers.shape, f32),
        in_specs=[pl.BlockSpec(memory_space=pltpu.VMEM)],
        out_specs=any_space,
        scratch_shapes=[dma((1,))],
        compiler_params=pltpu.CompilerParams(vmem_limit_bytes=4 << 20),
    )(result)


def solution(mesh):
    placed = (
        P(None, None, "lat", "lon"),
        P(None, "lat", "lon"),
        P(None, "lat"),
        P(None, "lat"),
        P(),
        P(),
    )
    return jax.shard_map(
        body, mesh=mesh, in_specs=placed, out_specs=P(None, None, "lat", "lon"), check_vma=False
    )
```

```python
import functools
import math

import jax
import jax.numpy as jnp
import numpy as np
from jax import lax
from jax.experimental import pallas as pl
from jax.experimental.pallas import tpu as pltpu
from jax.sharding import PartitionSpec as P

MODES = 1024
LANES = 128
PTS = 45
HALF = 23
SPAN = 23
MESH = pl.DeviceIdType.MESH


def residues():
    found = []
    for k5 in range(3):
        for k9 in range(5 if k5 == 0 else 9):
            kk = next(k for k in range(PTS) if k % 5 == k5 and k % 9 == k9)
            found.append(kk if kk <= PTS // 2 else kk - PTS)
    return found


def tables(lon_cells):
    res = np.array(residues(), np.int64)
    lane = np.arange(LANES, dtype=np.int64)
    ang = (res[:, None] * lane[None, :] % lon_cells) * (2 * math.pi / lon_cells)
    twid = np.stack([np.cos(ang), np.sin(ang)]).astype(np.float32)
    half = LANES // 2
    k2 = np.zeros(LANES, np.int64)
    valid = np.zeros(LANES, bool)
    for part in range(2):
        k2[part * half : part * half + 2 * SPAN + 1] = np.arange(-SPAN, SPAN + 1)
        valid[part * half : part * half + 2 * SPAN + 1] = True
    mode = res[:, None] + PTS * k2[None, :]
    kabs = np.abs(mode)
    keep = valid[None, :] & (kabs < MODES) & ~((res[:, None] == 0) & (mode < 0))
    kabs = np.where(keep, kabs, 1 << 20).astype(np.int32)
    scale = np.where(mode == 0, 1.0, 2.0) / lon_cells
    scale = np.where(keep, scale, 0.0).astype(np.float32)
    ang2 = (k2[None, :] * lane[:, None] % LANES) * (2 * math.pi / LANES)
    c2 = np.cos(ang2) * valid[None, :]
    s2 = np.sin(ang2) * valid[None, :]
    first = np.arange(LANES) < half
    fwd = np.concatenate(
        [np.where(first, c2, -s2), np.where(first, s2, c2)], axis=0
    )
    inv = np.concatenate(
        [np.where(first, c2, -s2), np.where(first, s2, c2)], axis=0
    ).T
    return twid, kabs, scale, fwd.astype(np.float32), inv.astype(np.float32)


def halves(table):
    high = jnp.asarray(table).astype(jnp.bfloat16)
    low = (jnp.asarray(table) - high.astype(jnp.float32)).astype(jnp.bfloat16)
    return high, low


def split_dot(value, high, low):
    vh = value.astype(jnp.bfloat16)
    vl = (value - vh.astype(jnp.float32)).astype(jnp.bfloat16)
    dot = functools.partial(jnp.dot, preferred_element_type=jnp.float32)
    return dot(vh, high) + (dot(vl, high) + dot(vh, low))


def cs(count, turn):
    return math.cos(2 * math.pi * turn / count), math.sin(2 * math.pi * turn / count)


def real5(x):
    e1, o1, e2, o2 = x[1] + x[4], x[1] - x[4], x[2] + x[3], x[2] - x[3]
    c1, s1 = cs(5, 1)
    c2, s2 = cs(5, 2)
    return (
        x[0] + (e1 + e2),
        (x[0] + (c1 * e1 + c2 * e2), -(s1 * o1 + s2 * o2)),
        (x[0] + (c2 * e1 + c1 * e2), s1 * o2 - s2 * o1),
    )


def total(terms):
    while len(terms) > 1:
        terms = [sum(terms[i : i + 2][1:], terms[i]) for i in range(0, len(terms), 2)]
    return terms[0]


def real9(x):
    e = [x[j] + x[9 - j] for j in range(1, 5)]
    o = [x[j] - x[9 - j] for j in range(1, 5)]
    out = [(total([x[0]] + e), None)]
    for k in range(1, 5):
        re = total([x[0]] + [cs(9, j * k)[0] * e[j - 1] for j in range(1, 5)])
        im = total([-cs(9, j * k)[1] * o[j - 1] for j in range(1, 5)])
        out.append((re, im))
    return out


def complex9(re, im, sign):
    er = [re[j] + re[9 - j] for j in range(1, 5)]
    ei = [im[j] + im[9 - j] for j in range(1, 5)]
    dr = [re[j] - re[9 - j] for j in range(1, 5)]
    di = [im[j] - im[9 - j] for j in range(1, 5)]
    out = [None] * 9
    out[0] = (total([re[0]] + er), total([im[0]] + ei))
    for k in range(1, 5):
        c = [cs(9, j * k)[0] for j in range(1, 5)]
        s = [sign * cs(9, j * k)[1] for j in range(1, 5)]
        pr = total([re[0]] + [c[j] * er[j] for j in range(4)])
        pi = total([im[0]] + [c[j] * ei[j] for j in range(4)])
        qr = total([s[j] * di[j] for j in range(4)])
        qi = total([s[j] * dr[j] for j in range(4)])
        out[k] = (pr - qr, pi + qi)
        out[9 - k] = (pr + qr, pi - qi)
    return out


def forward45(x):
    zero, one, two = [], [], []
    for p9 in range(9):
        a0, a1, a2 = real5([x[(9 * p5 + 5 * p9) % PTS] for p5 in range(5)])
        zero.append(a0)
        one.append(a1)
        two.append(a2)
    out = real9(zero)
    for part in (one, two):
        out += complex9([a[0] for a in part], [a[1] for a in part], -1.0)
    return out


def inverse45(v):
    zero, one, two = v[:5], v[5:14], v[14:]
    b0 = [None] * 9
    b0[0] = total([z[0] for z in zero])
    for p in range(1, 5):
        pr = total([zero[0][0]] + [cs(9, p * k)[0] * zero[k][0] for k in range(1, 5)])
        qr = total([cs(9, p * k)[1] * zero[k][1] for k in range(1, 5)])
        b0[p] = pr - qr
        b0[9 - p] = pr + qr
    b1 = complex9([a[0] for a in one], [a[1] for a in one], 1.0)
    b2 = complex9([a[0] for a in two], [a[1] for a in two], 1.0)
    c1, s1 = cs(5, 1)
    c2, s2 = cs(5, 2)
    out = [None] * PTS
    for p9 in range(9):
        (r1, i1), (r2, i2), base = b1[p9], b2[p9], b0[p9]
        ca = base + (c1 * r1 + c2 * r2)
        sa = s1 * i1 + s2 * i2
        cb = base + (c2 * r1 + c1 * r2)
        sb = s2 * i1 - s1 * i2
        vals = [base + (r1 + r2), ca - sa, cb - sb, cb + sb, ca + sa]
        for p5 in range(5):
            out[(9 * p5 + 5 * p9) % PTS] = vals[p5]
    return out


def fused_kernel(
    lat_count, lon_count,
    tr, cour, zs_in, zf_in, cut_in, damp_in,
    twid_in, kabs_in, scale_in, fwd_h_in, fwd_l_in, inv_h_in, inv_l_in,
    out,
    got_t, got_c, halo_t, halo_c, parts,
    zs, zf, cut, damp, twid, kabs, scale, fwd_h, fwd_l, inv_h, inv_l,
    line, moved, spec, wave,
    t_send, t_recv, c_send, c_recv, h_send, h_recv, hc_send, hc_recv, b_send, b_recv, b_local, local, ready,
):
    tracer_count, _, row_count, columns = tr.shape
    lat = lax.axis_index("lat")
    lon = lax.axis_index("lon")
    up = lax.rem(lat + 1, lat_count)
    down = lax.rem(lat + lat_count - 1, lat_count)
    flip = 2 * lax.rem(lat, 2)
    peers = [lon + 1 - 2 * lax.rem(lon, 2), lax.rem(lon + 2, lon_count), lon_count - 1 - lon]
    levels = [pl.ds(2 * lax.rem(peer + flip, lon_count), 2) for peer in peers]
    mine = pl.ds(2 * lax.rem(lon + flip, lon_count), 2)

    staged = [
        (tr.at[:, mine], got_t.at[lon]), (cour.at[mine], got_c.at[lon]),
        (zs_in, zs), (zf_in, zf), (cut_in, cut), (damp_in, damp),
        (twid_in, twid), (kabs_in, kabs), (scale_in, scale),
        (fwd_h_in, fwd_h), (fwd_l_in, fwd_l), (inv_h_in, inv_h), (inv_l_in, inv_l),
    ]
    staged = [
        pltpu.make_async_copy(a, b, local.at[i]) for i, (a, b) in enumerate(staged)
    ]
    for copy in staged:
        copy.start()

    def remote(src, dst, send, recv, device):
        return pltpu.make_async_remote_copy(
            src_ref=src, dst_ref=dst, send_sem=send, recv_sem=recv,
            device_id=device, device_id_type=MESH,
        )

    last = pl.ds(row_count - 1, 1)
    first = pl.ds(0, 1)
    pieces = (pl.ds(1, row_count - 2), first, last)

    def cells(t, m, piece):
        return remote(
            tr.at[t, levels[m], pieces[piece]], got_t.at[lon, t, :, pieces[piece]],
            t_send.at[t, 3 * m + piece], t_recv.at[t, 3 * m + piece],
            {"lat": lat, "lon": peers[m]},
        )

    def speeds(m):
        return remote(
            cour.at[levels[m]], got_c.at[lon], c_send.at[m], c_recv.at[m],
            {"lat": lat, "lon": peers[m]},
        )

    far = pl.ds(2 - 2 * (lon // 2), 2)
    direct = [(mine, peers[1]), (levels[0], peers[2])]

    def rims(t):
        copies = []
        for j, (owned, owner) in enumerate(direct):
            copies.append((
                remote(tr.at[t, owned, last], halo_t.at[lon, t, :, last],
                       h_send.at[t, j], h_recv.at[t, j], {"lat": up, "lon": owner}),
                remote(tr.at[t, owned, first], halo_t.at[lon, t, :, first],
                       h_send.at[t, j + 3], h_recv.at[t, j + 3], {"lat": down, "lon": owner}),
            ))
        copies.append((
            remote(got_t.at[far, t, :, last], halo_t.at[far, t, :, last],
                   h_send.at[t, 2], h_recv.at[t, 2], {"lat": up, "lon": peers[1]}),
            remote(got_t.at[far, t, :, first], halo_t.at[far, t, :, first],
                   h_send.at[t, 5], h_recv.at[t, 5], {"lat": down, "lon": peers[1]}),
        ))
        return copies

    def rim_speeds():
        copies = [
            remote(cour.at[owned, first], halo_c.at[lon, :, first],
                   hc_send.at[j], hc_recv.at[j], {"lat": down, "lon": owner})
            for j, (owned, owner) in enumerate(direct)
        ]
        copies.append(
            remote(got_c.at[far, :, first], halo_c.at[far, :, first],
                   hc_send.at[2], hc_recv.at[2], {"lat": down, "lon": peers[1]})
        )
        return copies

    def reply(t, m, piece):
        rows = pieces[piece]
        return remote(
            parts.at[peers[m], t, :, rows], out.at[t, mine, rows],
            b_send.at[t, 3 * m + piece], b_recv.at[t, 3 * m + piece],
            {"lat": lat, "lon": peers[m]},
        )

    def keep(t):
        return pltpu.make_async_copy(parts.at[lon, t], out.at[t, mine], b_local.at[t])

    barrier = pltpu.get_barrier_semaphore()
    has_north = (2 * lat_count - 3 - lat) // (lat_count - 1)
    has_south = (lat + lat_count - 2) // (lat_count - 1)
    north_there, south_there = has_north == 1, has_south == 1

    def signal(friend):
        pl.semaphore_signal(barrier, inc=1, device_id=friend, device_id_type=MESH)

    for peer in peers:
        signal({"lat": lat, "lon": peer})
    core = lax.rem(lon, 2)
    keeper = peers[1] + 1 - core
    pl.when(north_there)(functools.partial(signal, {"lat": up, "lon": keeper}))
    pl.when(south_there)(functools.partial(signal, {"lat": down, "lon": keeper}))
    pl.semaphore_wait(barrier, len(peers) + core * (2 * has_north + 2 * has_south))
    for m in (1, 2, 0):
        speeds(m).start()
    for group_of in ((0,), (1,), (2, 3)):
        for piece in (1, 2, 0):
            for t in group_of:
                for m in (1, 2, 0):
                    cells(t, m, piece).start()

    @pl.when(core == 1)
    def _():
        pl.semaphore_signal(ready, inc=1, device_id={"lat": lat, "lon": peers[0]}, device_id_type=MESH)

    @pl.when(core == 0)
    def _():
        pl.semaphore_wait(ready, 1)

    def each_rim(north_act, south_act, copies):
        @pl.when(north_act[0])
        def _():
            for north, _ in copies:
                getattr(north, north_act[1])()

        @pl.when(south_act[0])
        def _():
            for _, south in copies:
                getattr(south, south_act[1])()

    def start_rims(copies):
        each_rim((north_there, "start"), (south_there, "start"), copies)

    @pl.when(south_there)
    def _():
        for copy in rim_speeds()[:2]:
            copy.start()

    for t in range(tracer_count):
        start_rims(rims(t)[:2])
    for copy in staged:
        copy.wait()

    def relay(t):
        for m in (1, 2):
            for piece in (1, 2):
                cells(t, m, piece).wait_recv()
        start_rims(rims(t)[2:])

    speeds(1).wait_recv()
    speeds(2).wait_recv()
    pl.when(south_there)(rim_speeds()[2].start)
    speeds(0).wait_recv()

    shape = (8, LANES)
    sub = lax.broadcasted_iota(jnp.int32, (8, columns), 0)
    sub1 = lax.broadcasted_iota(jnp.int32, shape, 0)
    lane = lax.broadcasted_iota(jnp.int32, shape, 1)

    def own_levels(ref):
        rows = ref[...].astype(jnp.float32)
        wide = jnp.concatenate([rows, rows], axis=0)
        a = lax.broadcasted_iota(jnp.int32, wide.shape, 0)
        b = lax.broadcasted_iota(jnp.int32, wide.shape, 1)
        at = 2 * lax.rem(lon + flip, lon_count) + (a // 4)
        value = jnp.sum(jnp.where(b == at, wide, 0.0), axis=1, keepdims=True)
        return jnp.broadcast_to(value, shape)

    def own_rows(ref):
        rows = ref[pl.ds(lat * row_count // LANES, 1)].astype(jnp.float32)
        wide = jnp.broadcast_to(rows, shape)
        at = lax.rem(lat * row_count, LANES) + (sub1 & 3)
        value = jnp.sum(jnp.where(lane == at, wide, 0.0), axis=1, keepdims=True)
        return jnp.broadcast_to(value, shape)

    face = lat * row_count + (sub & 3)
    open_s8 = face > 0
    open_n8 = face + 1 < lat_count * row_count
    quarter = lat_count // 4
    in_cap = (lat < quarter) | (lat >= lat_count - quarter)
    given = (own_levels(zs), own_levels(zf), own_rows(cut), own_rows(damp))

    def joined(edge, one, two):
        inner = (lax.broadcasted_iota(jnp.int32, one.shape, 0) + 1) & 2
        return jnp.where(inner == (0 if edge else 2), one, pltpu.roll(two, 2, 0))

    def stacked(ref, *at):
        return jnp.concatenate([ref[(*at, 0)], ref[(*at, 1)]], axis=0)

    def advected(seg, t, edge):
        x = stacked(got_t, seg, t)
        c = stacked(got_c, seg)
        below = pltpu.roll(x, 1, 0)
        if edge:
            rim = stacked(halo_t, seg, t)
            rim_c = stacked(halo_c, seg)
            below = jnp.where((sub & 3) == 0, pltpu.roll(rim, 5, 0), below)
        flux = jnp.maximum(c, 0.0) * below + jnp.minimum(c, 0.0) * x
        if edge:
            flux = jnp.where(open_s8, flux, 0.0)
        top = pltpu.roll(flux, 7, 0)
        if edge:
            hi, ch = pltpu.roll(rim, 3, 0), pltpu.roll(rim_c, 3, 0)
            top = jnp.where(
                (sub & 3) == 3, jnp.maximum(ch, 0.0) * x + jnp.minimum(ch, 0.0) * hi, top
            )
            top = jnp.where(open_n8, top, 0.0)
        return x + flux - top

    def group(edge, both):
        for t in both:
            if edge:
                each_rim((south_there, "wait_recv"), (north_there, "wait_recv"), rims(t))
            else:
                for m in range(3):
                    cells(t, m, 0).wait_recv()
                for piece in (1, 2):
                    cells(t, 0, piece).wait_recv()
        alone = len(both) == 1
        s0, here, cut8, damp8 = [value if alone else joined(edge, value, value) for value in given]
        s0, cut8 = s0.astype(jnp.int32), cut8.astype(jnp.int32)
        s1 = s0 + 1
        fold0, fold1 = (lane - s0) & (LANES - 1), (lane - s1) & (LANES - 1)
        own0, own1 = lane >= s0, lane >= s1
        for seg in range(lon_count):
            tiles = [advected(seg, t, edge) for t in both]
            line[:, seg * columns : (seg + 1) * columns] = tiles[0] if alone else joined(edge, *tiles)

        def gathered(p):
            tile = line[:, p * LANES : (p + 1) * LANES]
            return (
                jnp.take_along_axis(tile, fold0, axis=1),
                jnp.take_along_axis(tile, fold1, axis=1),
            )

        @pl.when(in_cap)
        def _():
            previous = gathered(PTS - 1)
            x = []
            for p in range(PTS):
                now = gathered(p)
                current = jnp.where(own0, now[0], previous[0])
                earlier = jnp.where(own1, now[1], previous[1])
                value = (1.0 - here) * current + here * earlier
                moved[:, p * LANES : (p + 1) * LANES] = value
                x.append(value)
                previous = now
            for r, (re, im) in enumerate(forward45(x)):
                tc, ts = twid[0, r : r + 1], twid[1, r : r + 1]
                if im is None:
                    spec[8 * r : 8 * r + 8, :LANES] = re * tc
                    spec[8 * r : 8 * r + 8, LANES:] = -(re * ts)
                else:
                    spec[8 * r : 8 * r + 8, :LANES] = re * tc + im * ts
                    spec[8 * r : 8 * r + 8, LANES:] = im * tc - re * ts
            wave[...] = split_dot(spec[...], fwd_h[...], fwd_l[...])
            for r in range(HALF):
                weight = jnp.where(kabs[r : r + 1] <= cut8, scale[r : r + 1], 0.0)
                wave[8 * r : 8 * r + 8, :] = wave[8 * r : 8 * r + 8, :] * weight
            spec[...] = split_dot(wave[...], inv_h[...], inv_l[...])
            v = []
            for r in range(HALF):
                tc, ts = twid[0, r : r + 1], twid[1, r : r + 1]
                re, im = spec[8 * r : 8 * r + 8, :LANES], spec[8 * r : 8 * r + 8, LANES:]
                v.append((re * tc - im * ts, re * ts + im * tc))
            for p, low in enumerate(inverse45(v)):
                cols = slice(p * LANES, (p + 1) * LANES)
                shifted = moved[:, cols]
                filtered = damp8 * shifted + (1.0 - damp8) * low
                line[:, cols] = filtered

        @pl.when(jnp.logical_not(in_cap))
        def _():
            previous = gathered(PTS - 1)
            for p in range(PTS):
                now = gathered(p)
                current = jnp.where(own0, now[0], previous[0])
                earlier = jnp.where(own1, now[1], previous[1])
                moved[:, p * LANES : (p + 1) * LANES] = (1.0 - here) * current + here * earlier
                previous = now
            line[...] = moved[...]

        for seg in range(lon_count):
            value = line[:, seg * columns : (seg + 1) * columns]
            for t, rows in zip(both, (value, None if alone else pltpu.roll(value, 6, 0))):
                for level in range(2):
                    tile = rows[4 * level : 4 * level + 4]
                    if edge:
                        parts[seg, t, level, 0:1] = tile[0:1]
                        parts[seg, t, level, 3:4] = tile[3:4]
                    else:
                        parts[seg, t, level] = tile
        for t in both:
            for piece in ((1, 2) if edge else (0,)):
                for m in (1, 2, 0):
                    reply(t, m, piece).start()
            if edge:
                keep(t).start()

    for t in range(2):
        relay(t)
    group(False, [0, 1])
    for t in range(2, tracer_count):
        relay(t)

    @pl.loop(2, tracer_count)
    def _(t):
        group(False, [t])

    @pl.when(north_there)
    def _():
        for copy in rim_speeds():
            copy.wait_recv()

    @pl.loop(0, tracer_count // 2)
    def _(pair):
        group(True, [2 * pair, 2 * pair + 1])

    for m in range(3):
        speeds(m).wait_send()

    @pl.when(south_there)
    def _():
        for copy in rim_speeds():
            copy.wait_send()

    for t in range(tracer_count):
        for m in range(3):
            for piece in range(3):
                cells(t, m, piece).wait_send()
        each_rim((north_there, "wait_send"), (south_there, "wait_send"), rims(t))
        for m in range(3):
            for piece in range(3):
                back = reply(t, m, piece)
                back.wait_send()
                back.wait_recv()
        keep(t).wait()


def deliver_kernel(held, out, sem):
    copy = pltpu.make_async_copy(held, out, sem.at[0])
    copy.start()
    copy.wait()


def body(tracers, merid_courant, zonal_shift, zonal_fraction, cutoff, damping):
    tracer_count, level_count, row_count, columns = tracers.shape
    lat_count = lax.axis_size("lat")
    lon_count = lax.axis_size("lon")
    per = level_count // lon_count
    twid, kabs, scale, fwd, inv = tables(columns * lon_count)
    operands = (
        tracers, merid_courant, zonal_shift.T, zonal_fraction.T,
        cutoff.reshape(-1, LANES), damping.reshape(-1, LANES),
        jnp.asarray(twid), jnp.asarray(kabs), jnp.asarray(scale), *halves(fwd), *halves(inv),
    )
    any_space = pl.BlockSpec(memory_space=pl.ANY)
    operands = tuple(pltpu.with_memory_space_constraint(a, pltpu.HBM) for a in operands)
    tile = (per, row_count, columns)
    f32 = jnp.float32
    small = [pltpu.VMEM(a.shape, a.dtype) for a in operands[2:]]
    dma = pltpu.SemaphoreType.DMA
    result = pl.pallas_call(
        functools.partial(fused_kernel, lat_count, lon_count),
        out_shape=jax.ShapeDtypeStruct(tracers.shape, f32),
        in_specs=[any_space] * len(operands),
        out_specs=pl.BlockSpec(memory_space=pltpu.VMEM),
        scratch_shapes=[
            pltpu.VMEM((lon_count, tracer_count) + tile, f32),
            pltpu.VMEM((lon_count,) + tile, f32),
            pltpu.VMEM((lon_count, tracer_count) + tile, f32),
            pltpu.VMEM((lon_count,) + tile, f32),
            pltpu.VMEM((lon_count, tracer_count) + tile, f32),
            *small,
            pltpu.VMEM((8, columns * lon_count), f32),
            pltpu.VMEM((8, columns * lon_count), f32),
            pltpu.VMEM((HALF * 8, 2 * LANES), f32),
            pltpu.VMEM((HALF * 8, LANES), f32),
            dma((tracer_count, 9)), dma((tracer_count, 9)),
            dma((3,)), dma((3,)),
            dma((tracer_count, 6)), dma((tracer_count, 6)),
            dma((3,)), dma((3,)),
            dma((tracer_count, 9)), dma((tracer_count, 9)),
            dma((tracer_count,)),
            dma((len(operands),)),
            pltpu.SemaphoreType.REGULAR,
        ],
        compiler_params=pltpu.CompilerParams(
            collective_id=0, has_side_effects=True, vmem_limit_bytes=16 << 20
        ),
    )(*operands)
    return pl.pallas_call(
        deliver_kernel,
        out_shape=jax.ShapeDtypeStruct(tracers.shape, f32),
        in_specs=[pl.BlockSpec(memory_space=pltpu.VMEM)],
        out_specs=any_space,
        scratch_shapes=[dma((1,))],
        compiler_params=pltpu.CompilerParams(vmem_limit_bytes=4 << 20),
    )(result)


def solution(mesh):
    placed = (
        P(None, None, "lat", "lon"),
        P(None, "lat", "lon"),
        P(None, "lat"),
        P(None, "lat"),
        P(),
        P(),
    )
    return jax.shard_map(
        body, mesh=mesh, in_specs=placed, out_specs=P(None, None, "lat", "lon"), check_vma=False
    )
```

```python
import functools
import math

import jax
import jax.numpy as jnp
import numpy as np
from jax import lax
from jax.experimental import pallas as pl
from jax.experimental.pallas import tpu as pltpu
from jax.sharding import PartitionSpec as P

MODES = 1024
LANES = 128
PTS = 45
HALF = 23
SPAN = 23
MESH = pl.DeviceIdType.MESH


def residues():
    found = []
    for k5 in range(3):
        for k9 in range(5 if k5 == 0 else 9):
            kk = next(k for k in range(PTS) if k % 5 == k5 and k % 9 == k9)
            found.append(kk if kk <= PTS // 2 else kk - PTS)
    return found


def tables(lon_cells):
    res = np.array(residues(), np.int64)
    lane = np.arange(LANES, dtype=np.int64)
    ang = (res[:, None] * lane[None, :] % lon_cells) * (2 * math.pi / lon_cells)
    twid = np.stack([np.cos(ang), np.sin(ang)]).astype(np.float32)
    half = LANES // 2
    k2 = np.zeros(LANES, np.int64)
    valid = np.zeros(LANES, bool)
    for part in range(2):
        k2[part * half : part * half + 2 * SPAN + 1] = np.arange(-SPAN, SPAN + 1)
        valid[part * half : part * half + 2 * SPAN + 1] = True
    mode = res[:, None] + PTS * k2[None, :]
    kabs = np.abs(mode)
    keep = valid[None, :] & (kabs < MODES) & ~((res[:, None] == 0) & (mode < 0))
    kabs = np.where(keep, kabs, 1 << 20).astype(np.int32)
    scale = np.where(mode == 0, 1.0, 2.0) / lon_cells
    scale = np.where(keep, scale, 0.0).astype(np.float32)
    ang2 = (k2[None, :] * lane[:, None] % LANES) * (2 * math.pi / LANES)
    c2 = np.cos(ang2) * valid[None, :]
    s2 = np.sin(ang2) * valid[None, :]
    first = np.arange(LANES) < half
    fwd = np.concatenate(
        [np.where(first, c2, -s2), np.where(first, s2, c2)], axis=0
    )
    inv = np.concatenate(
        [np.where(first, c2, -s2), np.where(first, s2, c2)], axis=0
    ).T
    return twid, kabs, scale, fwd.astype(np.float32), inv.astype(np.float32)


def halves(table):
    high = jnp.asarray(table).astype(jnp.bfloat16)
    low = (jnp.asarray(table) - high.astype(jnp.float32)).astype(jnp.bfloat16)
    return high, low


def split_dot(value, high, low):
    vh = value.astype(jnp.bfloat16)
    vl = (value - vh.astype(jnp.float32)).astype(jnp.bfloat16)
    dot = functools.partial(jnp.dot, preferred_element_type=jnp.float32)
    return dot(vh, high) + (dot(vl, high) + dot(vh, low))


def cs(count, turn):
    return math.cos(2 * math.pi * turn / count), math.sin(2 * math.pi * turn / count)


def real5(x):
    e1, o1, e2, o2 = x[1] + x[4], x[1] - x[4], x[2] + x[3], x[2] - x[3]
    c1, s1 = cs(5, 1)
    c2, s2 = cs(5, 2)
    return (
        x[0] + (e1 + e2),
        (x[0] + (c1 * e1 + c2 * e2), -(s1 * o1 + s2 * o2)),
        (x[0] + (c2 * e1 + c1 * e2), s1 * o2 - s2 * o1),
    )


def total(terms):
    while len(terms) > 1:
        terms = [sum(terms[i : i + 2][1:], terms[i]) for i in range(0, len(terms), 2)]
    return terms[0]


def real9(x):
    e = [x[j] + x[9 - j] for j in range(1, 5)]
    o = [x[j] - x[9 - j] for j in range(1, 5)]
    out = [(total([x[0]] + e), None)]
    for k in range(1, 5):
        re = total([x[0]] + [cs(9, j * k)[0] * e[j - 1] for j in range(1, 5)])
        im = total([-cs(9, j * k)[1] * o[j - 1] for j in range(1, 5)])
        out.append((re, im))
    return out


def complex9(re, im, sign):
    er = [re[j] + re[9 - j] for j in range(1, 5)]
    ei = [im[j] + im[9 - j] for j in range(1, 5)]
    dr = [re[j] - re[9 - j] for j in range(1, 5)]
    di = [im[j] - im[9 - j] for j in range(1, 5)]
    out = [None] * 9
    out[0] = (total([re[0]] + er), total([im[0]] + ei))
    for k in range(1, 5):
        c = [cs(9, j * k)[0] for j in range(1, 5)]
        s = [sign * cs(9, j * k)[1] for j in range(1, 5)]
        pr = total([re[0]] + [c[j] * er[j] for j in range(4)])
        pi = total([im[0]] + [c[j] * ei[j] for j in range(4)])
        qr = total([s[j] * di[j] for j in range(4)])
        qi = total([s[j] * dr[j] for j in range(4)])
        out[k] = (pr - qr, pi + qi)
        out[9 - k] = (pr + qr, pi - qi)
    return out


def forward45(x):
    zero, one, two = [], [], []
    for p9 in range(9):
        a0, a1, a2 = real5([x[(9 * p5 + 5 * p9) % PTS] for p5 in range(5)])
        zero.append(a0)
        one.append(a1)
        two.append(a2)
    out = real9(zero)
    for part in (one, two):
        out += complex9([a[0] for a in part], [a[1] for a in part], -1.0)
    return out


def inverse45(v):
    zero, one, two = v[:5], v[5:14], v[14:]
    b0 = [None] * 9
    b0[0] = total([z[0] for z in zero])
    for p in range(1, 5):
        pr = total([zero[0][0]] + [cs(9, p * k)[0] * zero[k][0] for k in range(1, 5)])
        qr = total([cs(9, p * k)[1] * zero[k][1] for k in range(1, 5)])
        b0[p] = pr - qr
        b0[9 - p] = pr + qr
    b1 = complex9([a[0] for a in one], [a[1] for a in one], 1.0)
    b2 = complex9([a[0] for a in two], [a[1] for a in two], 1.0)
    c1, s1 = cs(5, 1)
    c2, s2 = cs(5, 2)
    out = [None] * PTS
    for p9 in range(9):
        (r1, i1), (r2, i2), base = b1[p9], b2[p9], b0[p9]
        ca = base + (c1 * r1 + c2 * r2)
        sa = s1 * i1 + s2 * i2
        cb = base + (c2 * r1 + c1 * r2)
        sb = s2 * i1 - s1 * i2
        vals = [base + (r1 + r2), ca - sa, cb - sb, cb + sb, ca + sa]
        for p5 in range(5):
            out[(9 * p5 + 5 * p9) % PTS] = vals[p5]
    return out


def fused_kernel(
    lat_count, lon_count,
    tr, cour, zs_in, zf_in, cut_in, damp_in,
    twid_in, kabs_in, scale_in, fwd_h_in, fwd_l_in, inv_h_in, inv_l_in,
    out,
    got_t, got_c, halo_t, halo_c, parts, strips, joint, got_j,
    zs, zf, cut, damp, twid, kabs, scale, fwd_h, fwd_l, inv_h, inv_l,
    line, moved, spec, wave,
    t_send, t_recv, c_send, c_recv, h_send, h_recv, hc_send, hc_recv, b_send, b_recv, b_local, local, ready,
    s_send, s_recv, s_local,
):
    tracer_count, _, row_count, columns = tr.shape
    lat = lax.axis_index("lat")
    lon = lax.axis_index("lon")
    up = lax.rem(lat + 1, lat_count)
    down = lax.rem(lat + lat_count - 1, lat_count)
    flip = 2 * lax.rem(lat, 2)
    peers = [lon + 1 - 2 * lax.rem(lon, 2), lax.rem(lon + 2, lon_count), lon_count - 1 - lon]
    levels = [pl.ds(2 * lax.rem(peer + flip, lon_count), 2) for peer in peers]
    mine = pl.ds(2 * lax.rem(lon + flip, lon_count), 2)

    staged = [
        (tr.at[:, mine], got_t.at[lon]), (cour.at[mine], got_c.at[lon]),
        (zs_in, zs), (zf_in, zf), (cut_in, cut), (damp_in, damp),
        (twid_in, twid), (kabs_in, kabs), (scale_in, scale),
        (fwd_h_in, fwd_h), (fwd_l_in, fwd_l), (inv_h_in, inv_h), (inv_l_in, inv_l),
    ]
    staged = [
        pltpu.make_async_copy(a, b, local.at[i]) for i, (a, b) in enumerate(staged)
    ]
    for copy in staged:
        copy.start()

    def remote(src, dst, send, recv, device):
        return pltpu.make_async_remote_copy(
            src_ref=src, dst_ref=dst, send_sem=send, recv_sem=recv,
            device_id=device, device_id_type=MESH,
        )

    last = pl.ds(row_count - 1, 1)
    first = pl.ds(0, 1)
    pieces = (pl.ds(1, row_count - 2), first, last)

    whole = columns // LANES * LANES
    spare = columns - whole
    body = pl.ds(0, whole)
    strip = pltpu.make_async_copy(
        tr.at[:, :, :, pl.ds(whole, spare)], strips, s_local.at[0]
    )
    strip.start()

    def ends(m):
        return remote(
            joint.at[levels[m]], got_j.at[lon], s_send.at[m], s_recv.at[m],
            {"lat": lat, "lon": peers[m]},
        )

    def cells(t, m, piece):
        return remote(
            tr.at[t, levels[m], pieces[piece], body], got_t.at[lon, t, :, pieces[piece], body],
            t_send.at[t, 3 * m + piece], t_recv.at[t, 3 * m + piece],
            {"lat": lat, "lon": peers[m]},
        )

    def speeds(m):
        return remote(
            cour.at[levels[m]], got_c.at[lon], c_send.at[m], c_recv.at[m],
            {"lat": lat, "lon": peers[m]},
        )

    far = pl.ds(2 - 2 * (lon // 2), 2)
    direct = [(mine, peers[1]), (levels[0], peers[2])]

    def rims(t):
        copies = []
        for j, (owned, owner) in enumerate(direct):
            copies.append((
                remote(tr.at[t, owned, last], halo_t.at[lon, t, :, last],
                       h_send.at[t, j], h_recv.at[t, j], {"lat": up, "lon": owner}),
                remote(tr.at[t, owned, first], halo_t.at[lon, t, :, first],
                       h_send.at[t, j + 3], h_recv.at[t, j + 3], {"lat": down, "lon": owner}),
            ))
        copies.append((
            remote(got_t.at[far, t, :, last], halo_t.at[far, t, :, last],
                   h_send.at[t, 2], h_recv.at[t, 2], {"lat": up, "lon": peers[1]}),
            remote(got_t.at[far, t, :, first], halo_t.at[far, t, :, first],
                   h_send.at[t, 5], h_recv.at[t, 5], {"lat": down, "lon": peers[1]}),
        ))
        return copies

    def rim_speeds():
        copies = [
            remote(cour.at[owned, first], halo_c.at[lon, :, first],
                   hc_send.at[j], hc_recv.at[j], {"lat": down, "lon": owner})
            for j, (owned, owner) in enumerate(direct)
        ]
        copies.append(
            remote(got_c.at[far, :, first], halo_c.at[far, :, first],
                   hc_send.at[2], hc_recv.at[2], {"lat": down, "lon": peers[1]})
        )
        return copies

    def reply(t, m, piece):
        rows = pieces[piece]
        return remote(
            parts.at[peers[m], t, :, rows], out.at[t, mine, rows],
            b_send.at[t, 3 * m + piece], b_recv.at[t, 3 * m + piece],
            {"lat": lat, "lon": peers[m]},
        )

    def keep(t):
        return pltpu.make_async_copy(parts.at[lon, t], out.at[t, mine], b_local.at[t])

    barrier = pltpu.get_barrier_semaphore()
    has_north = (2 * lat_count - 3 - lat) // (lat_count - 1)
    has_south = (lat + lat_count - 2) // (lat_count - 1)
    north_there, south_there = has_north == 1, has_south == 1

    def signal(friend):
        pl.semaphore_signal(barrier, inc=1, device_id=friend, device_id_type=MESH)

    for peer in peers:
        signal({"lat": lat, "lon": peer})
    core = lax.rem(lon, 2)
    keeper = peers[1] + 1 - core
    pl.when(north_there)(functools.partial(signal, {"lat": up, "lon": keeper}))
    pl.when(south_there)(functools.partial(signal, {"lat": down, "lon": keeper}))
    pl.semaphore_wait(barrier, len(peers) + core * (2 * has_north + 2 * has_south))
    for m in (1, 2, 0):
        speeds(m).start()
    strip.wait()
    for level in range(tr.shape[1]):
        joint[level] = jnp.concatenate([strips[t, level] for t in range(tracer_count)], axis=1)
    for m in (1, 2, 0):
        ends(m).start()
    for group_of in ((0,), (1,), (2, 3)):
        for piece in (1, 2, 0):
            for t in group_of:
                for m in (1, 2, 0):
                    cells(t, m, piece).start()

    @pl.when(core == 1)
    def _():
        pl.semaphore_signal(ready, inc=1, device_id={"lat": lat, "lon": peers[0]}, device_id_type=MESH)

    @pl.when(core == 0)
    def _():
        pl.semaphore_wait(ready, 1)

    def each_rim(north_act, south_act, copies):
        @pl.when(north_act[0])
        def _():
            for north, _ in copies:
                getattr(north, north_act[1])()

        @pl.when(south_act[0])
        def _():
            for _, south in copies:
                getattr(south, south_act[1])()

    def start_rims(copies):
        each_rim((north_there, "start"), (south_there, "start"), copies)

    @pl.when(south_there)
    def _():
        for copy in rim_speeds()[:2]:
            copy.start()

    for t in range(tracer_count):
        start_rims(rims(t)[:2])
    for copy in staged:
        copy.wait()

    def relay(t):
        for m in (1, 2):
            for piece in (1, 2):
                cells(t, m, piece).wait_recv()
        start_rims(rims(t)[2:])

    speeds(1).wait_recv()
    speeds(2).wait_recv()
    pl.when(south_there)(rim_speeds()[2].start)
    speeds(0).wait_recv()

    shape = (8, LANES)
    sub = lax.broadcasted_iota(jnp.int32, (8, columns), 0)
    sub1 = lax.broadcasted_iota(jnp.int32, shape, 0)
    lane = lax.broadcasted_iota(jnp.int32, shape, 1)

    def own_levels(ref):
        rows = ref[...].astype(jnp.float32)
        wide = jnp.concatenate([rows, rows], axis=0)
        a = lax.broadcasted_iota(jnp.int32, wide.shape, 0)
        b = lax.broadcasted_iota(jnp.int32, wide.shape, 1)
        at = 2 * lax.rem(lon + flip, lon_count) + (a // 4)
        value = jnp.sum(jnp.where(b == at, wide, 0.0), axis=1, keepdims=True)
        return jnp.broadcast_to(value, shape)

    def own_rows(ref):
        rows = ref[pl.ds(lat * row_count // LANES, 1)].astype(jnp.float32)
        wide = jnp.broadcast_to(rows, shape)
        at = lax.rem(lat * row_count, LANES) + (sub1 & 3)
        value = jnp.sum(jnp.where(lane == at, wide, 0.0), axis=1, keepdims=True)
        return jnp.broadcast_to(value, shape)

    face = lat * row_count + (sub & 3)
    open_s8 = face > 0
    open_n8 = face + 1 < lat_count * row_count
    quarter = lat_count // 4
    in_cap = (lat < quarter) | (lat >= lat_count - quarter)
    given = (own_levels(zs), own_levels(zf), own_rows(cut), own_rows(damp))

    def joined(edge, one, two):
        inner = (lax.broadcasted_iota(jnp.int32, one.shape, 0) + 1) & 2
        return jnp.where(inner == (0 if edge else 2), one, pltpu.roll(two, 2, 0))

    def stacked(ref, *at):
        return jnp.concatenate([ref[(*at, 0)], ref[(*at, 1)]], axis=0)

    def advected(seg, t, edge):
        x = stacked(got_t, seg, t)
        c = stacked(got_c, seg)
        below = pltpu.roll(x, 1, 0)
        if edge:
            rim = stacked(halo_t, seg, t)
            rim_c = stacked(halo_c, seg)
            below = jnp.where((sub & 3) == 0, pltpu.roll(rim, 5, 0), below)
        flux = jnp.maximum(c, 0.0) * below + jnp.minimum(c, 0.0) * x
        if edge:
            flux = jnp.where(open_s8, flux, 0.0)
        top = pltpu.roll(flux, 7, 0)
        if edge:
            hi, ch = pltpu.roll(rim, 3, 0), pltpu.roll(rim_c, 3, 0)
            top = jnp.where(
                (sub & 3) == 3, jnp.maximum(ch, 0.0) * x + jnp.minimum(ch, 0.0) * hi, top
            )
            top = jnp.where(open_n8, top, 0.0)
        return x + flux - top

    def group(edge, both):
        for t in both:
            if edge:
                each_rim((south_there, "wait_recv"), (north_there, "wait_recv"), rims(t))
            else:
                for m in range(3):
                    cells(t, m, 0).wait_recv()
                for piece in (1, 2):
                    cells(t, 0, piece).wait_recv()
        alone = len(both) == 1
        s0, here, cut8, damp8 = [value if alone else joined(edge, value, value) for value in given]
        s0, cut8 = s0.astype(jnp.int32), cut8.astype(jnp.int32)
        s1 = s0 + 1
        fold0, fold1 = (lane - s0) & (LANES - 1), (lane - s1) & (LANES - 1)
        own0, own1 = lane >= s0, lane >= s1
        for seg in range(lon_count):
            tiles = [advected(seg, t, edge) for t in both]
            line[:, seg * columns : (seg + 1) * columns] = tiles[0] if alone else joined(edge, *tiles)

        def gathered(p):
            tile = line[:, p * LANES : (p + 1) * LANES]
            return (
                jnp.take_along_axis(tile, fold0, axis=1),
                jnp.take_along_axis(tile, fold1, axis=1),
            )

        @pl.when(in_cap)
        def _():
            previous = gathered(PTS - 1)
            x = []
            for p in range(PTS):
                now = gathered(p)
                current = jnp.where(own0, now[0], previous[0])
                earlier = jnp.where(own1, now[1], previous[1])
                value = (1.0 - here) * current + here * earlier
                moved[:, p * LANES : (p + 1) * LANES] = value
                x.append(value)
                previous = now
            for r, (re, im) in enumerate(forward45(x)):
                tc, ts = twid[0, r : r + 1], twid[1, r : r + 1]
                if im is None:
                    spec[8 * r : 8 * r + 8, :LANES] = re * tc
                    spec[8 * r : 8 * r + 8, LANES:] = -(re * ts)
                else:
                    spec[8 * r : 8 * r + 8, :LANES] = re * tc + im * ts
                    spec[8 * r : 8 * r + 8, LANES:] = im * tc - re * ts
            wave[...] = split_dot(spec[...], fwd_h[...], fwd_l[...])
            for r in range(HALF):
                weight = jnp.where(kabs[r : r + 1] <= cut8, scale[r : r + 1], 0.0)
                wave[8 * r : 8 * r + 8, :] = wave[8 * r : 8 * r + 8, :] * weight
            spec[...] = split_dot(wave[...], inv_h[...], inv_l[...])
            v = []
            for r in range(HALF):
                tc, ts = twid[0, r : r + 1], twid[1, r : r + 1]
                re, im = spec[8 * r : 8 * r + 8, :LANES], spec[8 * r : 8 * r + 8, LANES:]
                v.append((re * tc - im * ts, re * ts + im * tc))
            for p, low in enumerate(inverse45(v)):
                cols = slice(p * LANES, (p + 1) * LANES)
                shifted = moved[:, cols]
                filtered = damp8 * shifted + (1.0 - damp8) * low
                line[:, cols] = filtered

        @pl.when(jnp.logical_not(in_cap))
        def _():
            previous = gathered(PTS - 1)
            for p in range(PTS):
                now = gathered(p)
                current = jnp.where(own0, now[0], previous[0])
                earlier = jnp.where(own1, now[1], previous[1])
                moved[:, p * LANES : (p + 1) * LANES] = (1.0 - here) * current + here * earlier
                previous = now
            line[...] = moved[...]

        for seg in range(lon_count):
            value = line[:, seg * columns : (seg + 1) * columns]
            for t, rows in zip(both, (value, None if alone else pltpu.roll(value, 6, 0))):
                for level in range(2):
                    tile = rows[4 * level : 4 * level + 4]
                    if edge:
                        parts[seg, t, level, 0:1] = tile[0:1]
                        parts[seg, t, level, 3:4] = tile[3:4]
                    else:
                        parts[seg, t, level] = tile
        for t in both:
            for piece in ((1, 2) if edge else (0,)):
                for m in (1, 2, 0):
                    reply(t, m, piece).start()
            if edge:
                keep(t).start()

    for m in (0, 1, 2):
        ends(m).wait_recv()
        for level in range(2):
            value = got_j[peers[m], level]
            for t in range(tracer_count):
                part = value if t == 0 else pltpu.roll(value, LANES - spare * t, 1)
                got_t[peers[m], t, level, :, whole:columns] = part[:, :spare]
    for t in range(2):
        relay(t)
    group(False, [0, 1])
    for t in range(2, tracer_count):
        relay(t)

    @pl.loop(2, tracer_count)
    def _(t):
        group(False, [t])

    @pl.when(north_there)
    def _():
        for copy in rim_speeds():
            copy.wait_recv()

    @pl.loop(0, tracer_count // 2)
    def _(pair):
        group(True, [2 * pair, 2 * pair + 1])

    for m in range(3):
        speeds(m).wait_send()
        ends(m).wait_send()

    @pl.when(south_there)
    def _():
        for copy in rim_speeds():
            copy.wait_send()

    for t in range(tracer_count):
        for m in range(3):
            for piece in range(3):
                cells(t, m, piece).wait_send()
        each_rim((north_there, "wait_send"), (south_there, "wait_send"), rims(t))
        for m in range(3):
            for piece in range(3):
                back = reply(t, m, piece)
                back.wait_send()
                back.wait_recv()
        keep(t).wait()


def deliver_kernel(held, out, sem):
    copy = pltpu.make_async_copy(held, out, sem.at[0])
    copy.start()
    copy.wait()


def body(tracers, merid_courant, zonal_shift, zonal_fraction, cutoff, damping):
    tracer_count, level_count, row_count, columns = tracers.shape
    lat_count = lax.axis_size("lat")
    lon_count = lax.axis_size("lon")
    per = level_count // lon_count
    twid, kabs, scale, fwd, inv = tables(columns * lon_count)
    operands = (
        tracers, merid_courant, zonal_shift.T, zonal_fraction.T,
        cutoff.reshape(-1, LANES), damping.reshape(-1, LANES),
        jnp.asarray(twid), jnp.asarray(kabs), jnp.asarray(scale), *halves(fwd), *halves(inv),
    )
    any_space = pl.BlockSpec(memory_space=pl.ANY)
    operands = tuple(pltpu.with_memory_space_constraint(a, pltpu.HBM) for a in operands)
    tile = (per, row_count, columns)
    f32 = jnp.float32
    small = [pltpu.VMEM(a.shape, a.dtype) for a in operands[2:]]
    dma = pltpu.SemaphoreType.DMA
    result = pl.pallas_call(
        functools.partial(fused_kernel, lat_count, lon_count),
        out_shape=jax.ShapeDtypeStruct(tracers.shape, f32),
        in_specs=[any_space] * len(operands),
        out_specs=pl.BlockSpec(memory_space=pltpu.VMEM),
        scratch_shapes=[
            pltpu.VMEM((lon_count, tracer_count) + tile, f32),
            pltpu.VMEM((lon_count,) + tile, f32),
            pltpu.VMEM((lon_count, tracer_count) + tile, f32),
            pltpu.VMEM((lon_count,) + tile, f32),
            pltpu.VMEM((lon_count, tracer_count) + tile, f32),
            pltpu.VMEM((tracer_count, level_count, row_count, columns % LANES), f32),
            pltpu.VMEM((level_count, row_count, LANES), f32),
            pltpu.VMEM((lon_count, per, row_count, LANES), f32),
            *small,
            pltpu.VMEM((8, columns * lon_count), f32),
            pltpu.VMEM((8, columns * lon_count), f32),
            pltpu.VMEM((HALF * 8, 2 * LANES), f32),
            pltpu.VMEM((HALF * 8, LANES), f32),
            dma((tracer_count, 9)), dma((tracer_count, 9)),
            dma((3,)), dma((3,)),
            dma((tracer_count, 6)), dma((tracer_count, 6)),
            dma((3,)), dma((3,)),
            dma((tracer_count, 9)), dma((tracer_count, 9)),
            dma((tracer_count,)),
            dma((len(operands),)),
            pltpu.SemaphoreType.REGULAR,
            dma((3,)), dma((3,)), dma((1,)),
        ],
        compiler_params=pltpu.CompilerParams(
            collective_id=0, has_side_effects=True, vmem_limit_bytes=16 << 20
        ),
    )(*operands)
    return pl.pallas_call(
        deliver_kernel,
        out_shape=jax.ShapeDtypeStruct(tracers.shape, f32),
        in_specs=[pl.BlockSpec(memory_space=pltpu.VMEM)],
        out_specs=any_space,
        scratch_shapes=[dma((1,))],
        compiler_params=pltpu.CompilerParams(vmem_limit_bytes=4 << 20),
    )(result)


def solution(mesh):
    placed = (
        P(None, None, "lat", "lon"),
        P(None, "lat", "lon"),
        P(None, "lat"),
        P(None, "lat"),
        P(),
        P(),
    )
    return jax.shard_map(
        body, mesh=mesh, in_specs=placed, out_specs=P(None, None, "lat", "lon"), check_vma=False
    )
```

```python
import functools
import math

import jax
import jax.numpy as jnp
import numpy as np
from jax import lax
from jax.experimental import pallas as pl
from jax.experimental.pallas import tpu as pltpu
from jax.sharding import PartitionSpec as P

MODES = 1024
LANES = 128
PTS = 45
HALF = 23
SPAN = 23
MESH = pl.DeviceIdType.MESH


def residues():
    found = []
    for k5 in range(3):
        for k9 in range(5 if k5 == 0 else 9):
            kk = next(k for k in range(PTS) if k % 5 == k5 and k % 9 == k9)
            found.append(kk if kk <= PTS // 2 else kk - PTS)
    return found


def tables(lon_cells):
    res = np.array(residues(), np.int64)
    lane = np.arange(LANES, dtype=np.int64)
    ang = (res[:, None] * lane[None, :] % lon_cells) * (2 * math.pi / lon_cells)
    twid = np.stack([np.cos(ang), np.sin(ang)]).astype(np.float32)
    half = LANES // 2
    k2 = np.zeros(LANES, np.int64)
    valid = np.zeros(LANES, bool)
    for part in range(2):
        k2[part * half : part * half + 2 * SPAN + 1] = np.arange(-SPAN, SPAN + 1)
        valid[part * half : part * half + 2 * SPAN + 1] = True
    mode = res[:, None] + PTS * k2[None, :]
    kabs = np.abs(mode)
    keep = valid[None, :] & (kabs < MODES) & ~((res[:, None] == 0) & (mode < 0))
    kabs = np.where(keep, kabs, 1 << 20).astype(np.int32)
    scale = np.where(mode == 0, 1.0, 2.0) / lon_cells
    scale = np.where(keep, scale, 0.0).astype(np.float32)
    ang2 = (k2[None, :] * lane[:, None] % LANES) * (2 * math.pi / LANES)
    c2 = np.cos(ang2) * valid[None, :]
    s2 = np.sin(ang2) * valid[None, :]
    first = np.arange(LANES) < half
    fwd = np.concatenate(
        [np.where(first, c2, -s2), np.where(first, s2, c2)], axis=0
    )
    inv = np.concatenate(
        [np.where(first, c2, -s2), np.where(first, s2, c2)], axis=0
    ).T
    return twid, kabs, scale, fwd.astype(np.float32), inv.astype(np.float32)


def halves(table):
    high = jnp.asarray(table).astype(jnp.bfloat16)
    low = (jnp.asarray(table) - high.astype(jnp.float32)).astype(jnp.bfloat16)
    return high, low


def split_dot(value, high, low):
    vh = value.astype(jnp.bfloat16)
    vl = (value - vh.astype(jnp.float32)).astype(jnp.bfloat16)
    dot = functools.partial(jnp.dot, preferred_element_type=jnp.float32)
    return dot(vh, high) + (dot(vl, high) + dot(vh, low))


def cs(count, turn):
    return math.cos(2 * math.pi * turn / count), math.sin(2 * math.pi * turn / count)


def real5(x):
    e1, o1, e2, o2 = x[1] + x[4], x[1] - x[4], x[2] + x[3], x[2] - x[3]
    c1, s1 = cs(5, 1)
    c2, s2 = cs(5, 2)
    return (
        x[0] + (e1 + e2),
        (x[0] + (c1 * e1 + c2 * e2), -(s1 * o1 + s2 * o2)),
        (x[0] + (c2 * e1 + c1 * e2), s1 * o2 - s2 * o1),
    )


def total(terms):
    while len(terms) > 1:
        terms = [sum(terms[i : i + 2][1:], terms[i]) for i in range(0, len(terms), 2)]
    return terms[0]


def real9(x):
    e = [x[j] + x[9 - j] for j in range(1, 5)]
    o = [x[j] - x[9 - j] for j in range(1, 5)]
    out = [(total([x[0]] + e), None)]
    for k in range(1, 5):
        re = total([x[0]] + [cs(9, j * k)[0] * e[j - 1] for j in range(1, 5)])
        im = total([-cs(9, j * k)[1] * o[j - 1] for j in range(1, 5)])
        out.append((re, im))
    return out


def complex9(re, im, sign):
    er = [re[j] + re[9 - j] for j in range(1, 5)]
    ei = [im[j] + im[9 - j] for j in range(1, 5)]
    dr = [re[j] - re[9 - j] for j in range(1, 5)]
    di = [im[j] - im[9 - j] for j in range(1, 5)]
    out = [None] * 9
    out[0] = (total([re[0]] + er), total([im[0]] + ei))
    for k in range(1, 5):
        c = [cs(9, j * k)[0] for j in range(1, 5)]
        s = [sign * cs(9, j * k)[1] for j in range(1, 5)]
        pr = total([re[0]] + [c[j] * er[j] for j in range(4)])
        pi = total([im[0]] + [c[j] * ei[j] for j in range(4)])
        qr = total([s[j] * di[j] for j in range(4)])
        qi = total([s[j] * dr[j] for j in range(4)])
        out[k] = (pr - qr, pi + qi)
        out[9 - k] = (pr + qr, pi - qi)
    return out


def forward45(x):
    zero, one, two = [], [], []
    for p9 in range(9):
        a0, a1, a2 = real5([x[(9 * p5 + 5 * p9) % PTS] for p5 in range(5)])
        zero.append(a0)
        one.append(a1)
        two.append(a2)
    out = real9(zero)
    for part in (one, two):
        out += complex9([a[0] for a in part], [a[1] for a in part], -1.0)
    return out


def inverse45(v):
    zero, one, two = v[:5], v[5:14], v[14:]
    b0 = [None] * 9
    b0[0] = total([z[0] for z in zero])
    for p in range(1, 5):
        pr = total([zero[0][0]] + [cs(9, p * k)[0] * zero[k][0] for k in range(1, 5)])
        qr = total([cs(9, p * k)[1] * zero[k][1] for k in range(1, 5)])
        b0[p] = pr - qr
        b0[9 - p] = pr + qr
    b1 = complex9([a[0] for a in one], [a[1] for a in one], 1.0)
    b2 = complex9([a[0] for a in two], [a[1] for a in two], 1.0)
    c1, s1 = cs(5, 1)
    c2, s2 = cs(5, 2)
    out = [None] * PTS
    for p9 in range(9):
        (r1, i1), (r2, i2), base = b1[p9], b2[p9], b0[p9]
        ca = base + (c1 * r1 + c2 * r2)
        sa = s1 * i1 + s2 * i2
        cb = base + (c2 * r1 + c1 * r2)
        sb = s2 * i1 - s1 * i2
        vals = [base + (r1 + r2), ca - sa, cb - sb, cb + sb, ca + sa]
        for p5 in range(5):
            out[(9 * p5 + 5 * p9) % PTS] = vals[p5]
    return out


def fused_kernel(
    lat_count, lon_count,
    tr, cour, zs_in, zf_in, cut_in, damp_in,
    twid_in, kabs_in, scale_in, fwd_h_in, fwd_l_in, inv_h_in, inv_l_in,
    out,
    got_t, got_c, halo_t, halo_c, parts, strips, joint, got_j,
    zs, zf, cut, damp, twid, kabs, scale, fwd_h, fwd_l, inv_h, inv_l,
    line, moved, spec, wave,
    t_send, t_recv, c_send, c_recv, h_send, h_recv, hc_send, hc_recv, b_send, b_recv, b_local, local, ready,
    s_send, s_recv, s_local,
):
    tracer_count, _, row_count, columns = tr.shape
    lat = lax.axis_index("lat")
    lon = lax.axis_index("lon")
    up = lax.rem(lat + 1, lat_count)
    down = lax.rem(lat + lat_count - 1, lat_count)
    flip = 2 * lax.rem(lat, 2)
    peers = [lon + 1 - 2 * lax.rem(lon, 2), lax.rem(lon + 2, lon_count), lon_count - 1 - lon]
    levels = [pl.ds(2 * lax.rem(peer + flip, lon_count), 2) for peer in peers]
    mine = pl.ds(2 * lax.rem(lon + flip, lon_count), 2)

    staged = [
        (tr.at[:, mine], got_t.at[lon]), (cour.at[mine], got_c.at[lon]),
        (zs_in, zs), (zf_in, zf), (cut_in, cut), (damp_in, damp),
        (twid_in, twid), (kabs_in, kabs), (scale_in, scale),
        (fwd_h_in, fwd_h), (fwd_l_in, fwd_l), (inv_h_in, inv_h), (inv_l_in, inv_l),
    ]
    staged = [
        pltpu.make_async_copy(a, b, local.at[i]) for i, (a, b) in enumerate(staged)
    ]
    for copy in staged:
        copy.start()

    def remote(src, dst, send, recv, device):
        return pltpu.make_async_remote_copy(
            src_ref=src, dst_ref=dst, send_sem=send, recv_sem=recv,
            device_id=device, device_id_type=MESH,
        )

    last = pl.ds(row_count - 1, 1)
    first = pl.ds(0, 1)
    pieces = (pl.ds(1, row_count - 2), first, last)

    whole = columns // LANES * LANES
    spare = columns - whole
    body = pl.ds(0, whole)
    strip = pltpu.make_async_copy(
        tr.at[:, :, :, pl.ds(whole, spare)], strips, s_local.at[0]
    )
    strip.start()

    def ends(m):
        return remote(
            joint.at[levels[m]], got_j.at[lon], s_send.at[m], s_recv.at[m],
            {"lat": lat, "lon": peers[m]},
        )

    def cells(t, m, piece):
        return remote(
            tr.at[t, levels[m], pieces[piece], body], got_t.at[lon, t, :, pieces[piece], body],
            t_send.at[t, 3 * m + piece], t_recv.at[t, 3 * m + piece],
            {"lat": lat, "lon": peers[m]},
        )

    def speeds(m):
        return remote(
            cour.at[levels[m]], got_c.at[lon], c_send.at[m], c_recv.at[m],
            {"lat": lat, "lon": peers[m]},
        )

    far = pl.ds(2 - 2 * (lon // 2), 2)
    direct = [(mine, peers[1]), (levels[0], peers[2])]

    def rims(t):
        copies = []
        for j, (owned, owner) in enumerate(direct):
            copies.append((
                remote(tr.at[t, owned, last], halo_t.at[lon, t, :, last],
                       h_send.at[t, j], h_recv.at[t, j], {"lat": up, "lon": owner}),
                remote(tr.at[t, owned, first], halo_t.at[lon, t, :, first],
                       h_send.at[t, j + 3], h_recv.at[t, j + 3], {"lat": down, "lon": owner}),
            ))
        copies.append((
            remote(got_t.at[far, t, :, last], halo_t.at[far, t, :, last],
                   h_send.at[t, 2], h_recv.at[t, 2], {"lat": up, "lon": peers[1]}),
            remote(got_t.at[far, t, :, first], halo_t.at[far, t, :, first],
                   h_send.at[t, 5], h_recv.at[t, 5], {"lat": down, "lon": peers[1]}),
        ))
        return copies

    def rim_speeds():
        copies = [
            remote(cour.at[owned, first], halo_c.at[lon, :, first],
                   hc_send.at[j], hc_recv.at[j], {"lat": down, "lon": owner})
            for j, (owned, owner) in enumerate(direct)
        ]
        copies.append(
            remote(got_c.at[far, :, first], halo_c.at[far, :, first],
                   hc_send.at[2], hc_recv.at[2], {"lat": down, "lon": peers[1]})
        )
        return copies

    def reply(t, m, piece):
        rows = pieces[piece]
        return remote(
            parts.at[peers[m], t, :, rows], out.at[t, mine, rows],
            b_send.at[t, 3 * m + piece], b_recv.at[t, 3 * m + piece],
            {"lat": lat, "lon": peers[m]},
        )

    def keep(t):
        return pltpu.make_async_copy(parts.at[lon, t], out.at[t, mine], b_local.at[t])

    barrier = pltpu.get_barrier_semaphore()
    has_north = (2 * lat_count - 3 - lat) // (lat_count - 1)
    has_south = (lat + lat_count - 2) // (lat_count - 1)
    north_there, south_there = has_north == 1, has_south == 1

    def signal(friend):
        pl.semaphore_signal(barrier, inc=1, device_id=friend, device_id_type=MESH)

    for peer in peers:
        signal({"lat": lat, "lon": peer})
    core = lax.rem(lon, 2)
    keeper = peers[1] + 1 - core
    pl.when(north_there)(functools.partial(signal, {"lat": up, "lon": keeper}))
    pl.when(south_there)(functools.partial(signal, {"lat": down, "lon": keeper}))
    pl.semaphore_wait(barrier, len(peers) + core * (2 * has_north + 2 * has_south))
    for m in (1, 2, 0):
        speeds(m).start()
    strip.wait()
    for level in range(tr.shape[1]):
        joint[level] = jnp.concatenate([strips[t, level] for t in range(tracer_count)], axis=1)
    for m in (1, 2, 0):
        ends(m).start()
    for group_of in ((0,), (1,), (2, 3)):
        for piece in (1, 2, 0):
            for t in group_of:
                for m in (1, 2, 0):
                    cells(t, m, piece).start()

    @pl.when(core == 1)
    def _():
        pl.semaphore_signal(ready, inc=1, device_id={"lat": lat, "lon": peers[0]}, device_id_type=MESH)

    @pl.when(core == 0)
    def _():
        pl.semaphore_wait(ready, 1)

    def each_rim(north_act, south_act, copies):
        @pl.when(north_act[0])
        def _():
            for north, _ in copies:
                getattr(north, north_act[1])()

        @pl.when(south_act[0])
        def _():
            for _, south in copies:
                getattr(south, south_act[1])()

    def start_rims(copies):
        each_rim((north_there, "start"), (south_there, "start"), copies)

    @pl.when(south_there)
    def _():
        for copy in rim_speeds()[:2]:
            copy.start()

    for t in range(2):
        start_rims(rims(t)[:2])
    for copy in staged:
        copy.wait()

    def relay(t):
        for m in (1, 2):
            for piece in (1, 2):
                cells(t, m, piece).wait_recv()
        start_rims(rims(t)[2:])

    speeds(1).wait_recv()
    speeds(2).wait_recv()
    pl.when(south_there)(rim_speeds()[2].start)
    speeds(0).wait_recv()

    shape = (8, LANES)
    sub = lax.broadcasted_iota(jnp.int32, (8, columns), 0)
    sub1 = lax.broadcasted_iota(jnp.int32, shape, 0)
    lane = lax.broadcasted_iota(jnp.int32, shape, 1)

    def own_levels(ref):
        rows = ref[...].astype(jnp.float32)
        wide = jnp.concatenate([rows, rows], axis=0)
        a = lax.broadcasted_iota(jnp.int32, wide.shape, 0)
        b = lax.broadcasted_iota(jnp.int32, wide.shape, 1)
        at = 2 * lax.rem(lon + flip, lon_count) + (a // 4)
        value = jnp.sum(jnp.where(b == at, wide, 0.0), axis=1, keepdims=True)
        return jnp.broadcast_to(value, shape)

    def own_rows(ref):
        rows = ref[pl.ds(lat * row_count // LANES, 1)].astype(jnp.float32)
        wide = jnp.broadcast_to(rows, shape)
        at = lax.rem(lat * row_count, LANES) + (sub1 & 3)
        value = jnp.sum(jnp.where(lane == at, wide, 0.0), axis=1, keepdims=True)
        return jnp.broadcast_to(value, shape)

    face = lat * row_count + (sub & 3)
    open_s8 = face > 0
    open_n8 = face + 1 < lat_count * row_count
    quarter = lat_count // 4
    in_cap = (lat < quarter) | (lat >= lat_count - quarter)
    given = (own_levels(zs), own_levels(zf), own_rows(cut), own_rows(damp))

    def joined(edge, one, two):
        inner = (lax.broadcasted_iota(jnp.int32, one.shape, 0) + 1) & 2
        return jnp.where(inner == (0 if edge else 2), one, pltpu.roll(two, 2, 0))

    def stacked(ref, *at):
        return jnp.concatenate([ref[(*at, 0)], ref[(*at, 1)]], axis=0)

    def advected(seg, t, edge):
        x = stacked(got_t, seg, t)
        c = stacked(got_c, seg)
        below = pltpu.roll(x, 1, 0)
        if edge:
            rim = stacked(halo_t, seg, t)
            rim_c = stacked(halo_c, seg)
            below = jnp.where((sub & 3) == 0, pltpu.roll(rim, 5, 0), below)
        flux = jnp.maximum(c, 0.0) * below + jnp.minimum(c, 0.0) * x
        if edge:
            flux = jnp.where(open_s8, flux, 0.0)
        top = pltpu.roll(flux, 7, 0)
        if edge:
            hi, ch = pltpu.roll(rim, 3, 0), pltpu.roll(rim_c, 3, 0)
            top = jnp.where(
                (sub & 3) == 3, jnp.maximum(ch, 0.0) * x + jnp.minimum(ch, 0.0) * hi, top
            )
            top = jnp.where(open_n8, top, 0.0)
        return x + flux - top

    def group(edge, both):
        for t in both:
            if edge:
                each_rim((south_there, "wait_recv"), (north_there, "wait_recv"), rims(t))
            else:
                for m in range(3):
                    cells(t, m, 0).wait_recv()
                for piece in (1, 2):
                    cells(t, 0, piece).wait_recv()
        alone = len(both) == 1
        s0, here, cut8, damp8 = [value if alone else joined(edge, value, value) for value in given]
        s0, cut8 = s0.astype(jnp.int32), cut8.astype(jnp.int32)
        s1 = s0 + 1
        fold0, fold1 = (lane - s0) & (LANES - 1), (lane - s1) & (LANES - 1)
        own0, own1 = lane >= s0, lane >= s1
        for seg in range(lon_count):
            tiles = [advected(seg, t, edge) for t in both]
            line[:, seg * columns : (seg + 1) * columns] = tiles[0] if alone else joined(edge, *tiles)

        def gathered(p):
            tile = line[:, p * LANES : (p + 1) * LANES]
            return (
                jnp.take_along_axis(tile, fold0, axis=1),
                jnp.take_along_axis(tile, fold1, axis=1),
            )

        @pl.when(in_cap)
        def _():
            previous = gathered(PTS - 1)
            x = []
            for p in range(PTS):
                now = gathered(p)
                current = jnp.where(own0, now[0], previous[0])
                earlier = jnp.where(own1, now[1], previous[1])
                value = (1.0 - here) * current + here * earlier
                moved[:, p * LANES : (p + 1) * LANES] = value
                x.append(value)
                previous = now
            for r, (re, im) in enumerate(forward45(x)):
                tc, ts = twid[0, r : r + 1], twid[1, r : r + 1]
                if im is None:
                    spec[8 * r : 8 * r + 8, :LANES] = re * tc
                    spec[8 * r : 8 * r + 8, LANES:] = -(re * ts)
                else:
                    spec[8 * r : 8 * r + 8, :LANES] = re * tc + im * ts
                    spec[8 * r : 8 * r + 8, LANES:] = im * tc - re * ts
            wave[...] = split_dot(spec[...], fwd_h[...], fwd_l[...])
            for r in range(HALF):
                weight = jnp.where(kabs[r : r + 1] <= cut8, scale[r : r + 1], 0.0)
                wave[8 * r : 8 * r + 8, :] = wave[8 * r : 8 * r + 8, :] * weight
            spec[...] = split_dot(wave[...], inv_h[...], inv_l[...])
            v = []
            for r in range(HALF):
                tc, ts = twid[0, r : r + 1], twid[1, r : r + 1]
                re, im = spec[8 * r : 8 * r + 8, :LANES], spec[8 * r : 8 * r + 8, LANES:]
                v.append((re * tc - im * ts, re * ts + im * tc))
            for p, low in enumerate(inverse45(v)):
                cols = slice(p * LANES, (p + 1) * LANES)
                shifted = moved[:, cols]
                filtered = damp8 * shifted + (1.0 - damp8) * low
                line[:, cols] = filtered

        @pl.when(jnp.logical_not(in_cap))
        def _():
            previous = gathered(PTS - 1)
            for p in range(PTS):
                now = gathered(p)
                current = jnp.where(own0, now[0], previous[0])
                earlier = jnp.where(own1, now[1], previous[1])
                moved[:, p * LANES : (p + 1) * LANES] = (1.0 - here) * current + here * earlier
                previous = now
            line[...] = moved[...]

        for seg in range(lon_count):
            value = line[:, seg * columns : (seg + 1) * columns]
            for t, rows in zip(both, (value, None if alone else pltpu.roll(value, 6, 0))):
                for level in range(2):
                    tile = rows[4 * level : 4 * level + 4]
                    if edge:
                        parts[seg, t, level, 0:1] = tile[0:1]
                        parts[seg, t, level, 3:4] = tile[3:4]
                    else:
                        parts[seg, t, level] = tile
        for t in both:
            for piece in ((1, 2) if edge else (0,)):
                for m in (1, 2, 0):
                    reply(t, m, piece).start()
            if edge:
                keep(t).start()

    for m in (0, 1, 2):
        ends(m).wait_recv()
        for level in range(2):
            value = got_j[peers[m], level]
            for t in range(tracer_count):
                part = value if t == 0 else pltpu.roll(value, LANES - spare * t, 1)
                got_t[peers[m], t, level, :, whole:columns] = part[:, :spare]
    for t in range(2):
        relay(t)
        start_rims(rims(t + 2)[:2])
    group(False, [0, 1])
    for t in range(2, tracer_count):
        relay(t)

    @pl.loop(2, tracer_count)
    def _(t):
        group(False, [t])

    @pl.when(north_there)
    def _():
        for copy in rim_speeds():
            copy.wait_recv()

    @pl.loop(0, tracer_count // 2)
    def _(pair):
        group(True, [2 * pair, 2 * pair + 1])

    for m in range(3):
        speeds(m).wait_send()
        ends(m).wait_send()

    @pl.when(south_there)
    def _():
        for copy in rim_speeds():
            copy.wait_send()

    for t in range(tracer_count):
        for m in range(3):
            for piece in range(3):
                cells(t, m, piece).wait_send()
        each_rim((north_there, "wait_send"), (south_there, "wait_send"), rims(t))
        for m in range(3):
            for piece in range(3):
                back = reply(t, m, piece)
                back.wait_send()
                back.wait_recv()
        keep(t).wait()


def deliver_kernel(held, out, sem):
    copy = pltpu.make_async_copy(held, out, sem.at[0])
    copy.start()
    copy.wait()


def body(tracers, merid_courant, zonal_shift, zonal_fraction, cutoff, damping):
    tracer_count, level_count, row_count, columns = tracers.shape
    lat_count = lax.axis_size("lat")
    lon_count = lax.axis_size("lon")
    per = level_count // lon_count
    twid, kabs, scale, fwd, inv = tables(columns * lon_count)
    operands = (
        tracers, merid_courant, zonal_shift.T, zonal_fraction.T,
        cutoff.reshape(-1, LANES), damping.reshape(-1, LANES),
        jnp.asarray(twid), jnp.asarray(kabs), jnp.asarray(scale), *halves(fwd), *halves(inv),
    )
    any_space = pl.BlockSpec(memory_space=pl.ANY)
    operands = tuple(pltpu.with_memory_space_constraint(a, pltpu.HBM) for a in operands)
    tile = (per, row_count, columns)
    f32 = jnp.float32
    small = [pltpu.VMEM(a.shape, a.dtype) for a in operands[2:]]
    dma = pltpu.SemaphoreType.DMA
    result = pl.pallas_call(
        functools.partial(fused_kernel, lat_count, lon_count),
        out_shape=jax.ShapeDtypeStruct(tracers.shape, f32),
        in_specs=[any_space] * len(operands),
        out_specs=pl.BlockSpec(memory_space=pltpu.VMEM),
        scratch_shapes=[
            pltpu.VMEM((lon_count, tracer_count) + tile, f32),
            pltpu.VMEM((lon_count,) + tile, f32),
            pltpu.VMEM((lon_count, tracer_count) + tile, f32),
            pltpu.VMEM((lon_count,) + tile, f32),
            pltpu.VMEM((lon_count, tracer_count) + tile, f32),
            pltpu.VMEM((tracer_count, level_count, row_count, columns % LANES), f32),
            pltpu.VMEM((level_count, row_count, LANES), f32),
            pltpu.VMEM((lon_count, per, row_count, LANES), f32),
            *small,
            pltpu.VMEM((8, columns * lon_count), f32),
            pltpu.VMEM((8, columns * lon_count), f32),
            pltpu.VMEM((HALF * 8, 2 * LANES), f32),
            pltpu.VMEM((HALF * 8, LANES), f32),
            dma((tracer_count, 9)), dma((tracer_count, 9)),
            dma((3,)), dma((3,)),
            dma((tracer_count, 6)), dma((tracer_count, 6)),
            dma((3,)), dma((3,)),
            dma((tracer_count, 9)), dma((tracer_count, 9)),
            dma((tracer_count,)),
            dma((len(operands),)),
            pltpu.SemaphoreType.REGULAR,
            dma((3,)), dma((3,)), dma((1,)),
        ],
        compiler_params=pltpu.CompilerParams(
            collective_id=0, has_side_effects=True, vmem_limit_bytes=16 << 20
        ),
    )(*operands)
    return pl.pallas_call(
        deliver_kernel,
        out_shape=jax.ShapeDtypeStruct(tracers.shape, f32),
        in_specs=[pl.BlockSpec(memory_space=pltpu.VMEM)],
        out_specs=any_space,
        scratch_shapes=[dma((1,))],
        compiler_params=pltpu.CompilerParams(vmem_limit_bytes=4 << 20),
    )(result)


def solution(mesh):
    placed = (
        P(None, None, "lat", "lon"),
        P(None, "lat", "lon"),
        P(None, "lat"),
        P(None, "lat"),
        P(),
        P(),
    )
    return jax.shard_map(
        body, mesh=mesh, in_specs=placed, out_specs=P(None, None, "lat", "lon"), check_vma=False
    )
```

```python
import functools
import math

import jax
import jax.numpy as jnp
import numpy as np
from jax import lax
from jax.experimental import pallas as pl
from jax.experimental.pallas import tpu as pltpu
from jax.sharding import PartitionSpec as P

MODES = 1024
LANES = 128
PTS = 45
HALF = 23
SPAN = 23
MESH = pl.DeviceIdType.MESH


def residues():
    found = []
    for k5 in range(3):
        for k9 in range(5 if k5 == 0 else 9):
            kk = next(k for k in range(PTS) if k % 5 == k5 and k % 9 == k9)
            found.append(kk if kk <= PTS // 2 else kk - PTS)
    return found


def tables(lon_cells):
    res = np.array(residues(), np.int64)
    lane = np.arange(LANES, dtype=np.int64)
    ang = (res[:, None] * lane[None, :] % lon_cells) * (2 * math.pi / lon_cells)
    twid = np.stack([np.cos(ang), np.sin(ang)]).astype(np.float32)
    half = LANES // 2
    k2 = np.zeros(LANES, np.int64)
    valid = np.zeros(LANES, bool)
    for part in range(2):
        k2[part * half : part * half + 2 * SPAN + 1] = np.arange(-SPAN, SPAN + 1)
        valid[part * half : part * half + 2 * SPAN + 1] = True
    mode = res[:, None] + PTS * k2[None, :]
    kabs = np.abs(mode)
    keep = valid[None, :] & (kabs < MODES) & ~((res[:, None] == 0) & (mode < 0))
    kabs = np.where(keep, kabs, 1 << 20).astype(np.int32)
    scale = np.where(mode == 0, 1.0, 2.0) / lon_cells
    scale = np.where(keep, scale, 0.0).astype(np.float32)
    ang2 = (k2[None, :] * lane[:, None] % LANES) * (2 * math.pi / LANES)
    c2 = np.cos(ang2) * valid[None, :]
    s2 = np.sin(ang2) * valid[None, :]
    first = np.arange(LANES) < half
    fwd = np.concatenate(
        [np.where(first, c2, -s2), np.where(first, s2, c2)], axis=0
    )
    inv = np.concatenate(
        [np.where(first, c2, -s2), np.where(first, s2, c2)], axis=0
    ).T
    return twid, kabs, scale, fwd.astype(np.float32), inv.astype(np.float32)


def halves(table):
    high = jnp.asarray(table).astype(jnp.bfloat16)
    low = (jnp.asarray(table) - high.astype(jnp.float32)).astype(jnp.bfloat16)
    return high, low


def split_dot(value, high, low):
    vh = value.astype(jnp.bfloat16)
    vl = (value - vh.astype(jnp.float32)).astype(jnp.bfloat16)
    dot = functools.partial(jnp.dot, preferred_element_type=jnp.float32)
    return dot(vh, high) + (dot(vl, high) + dot(vh, low))


def cs(count, turn):
    return math.cos(2 * math.pi * turn / count), math.sin(2 * math.pi * turn / count)


def real5(x):
    e1, o1, e2, o2 = x[1] + x[4], x[1] - x[4], x[2] + x[3], x[2] - x[3]
    c1, s1 = cs(5, 1)
    c2, s2 = cs(5, 2)
    return (
        x[0] + (e1 + e2),
        (x[0] + (c1 * e1 + c2 * e2), -(s1 * o1 + s2 * o2)),
        (x[0] + (c2 * e1 + c1 * e2), s1 * o2 - s2 * o1),
    )


def total(terms):
    while len(terms) > 1:
        terms = [sum(terms[i : i + 2][1:], terms[i]) for i in range(0, len(terms), 2)]
    return terms[0]


def real9(x):
    e = [x[j] + x[9 - j] for j in range(1, 5)]
    o = [x[j] - x[9 - j] for j in range(1, 5)]
    out = [(total([x[0]] + e), None)]
    for k in range(1, 5):
        re = total([x[0]] + [cs(9, j * k)[0] * e[j - 1] for j in range(1, 5)])
        im = total([-cs(9, j * k)[1] * o[j - 1] for j in range(1, 5)])
        out.append((re, im))
    return out


def complex9(re, im, sign):
    er = [re[j] + re[9 - j] for j in range(1, 5)]
    ei = [im[j] + im[9 - j] for j in range(1, 5)]
    dr = [re[j] - re[9 - j] for j in range(1, 5)]
    di = [im[j] - im[9 - j] for j in range(1, 5)]
    out = [None] * 9
    out[0] = (total([re[0]] + er), total([im[0]] + ei))
    for k in range(1, 5):
        c = [cs(9, j * k)[0] for j in range(1, 5)]
        s = [sign * cs(9, j * k)[1] for j in range(1, 5)]
        pr = total([re[0]] + [c[j] * er[j] for j in range(4)])
        pi = total([im[0]] + [c[j] * ei[j] for j in range(4)])
        qr = total([s[j] * di[j] for j in range(4)])
        qi = total([s[j] * dr[j] for j in range(4)])
        out[k] = (pr - qr, pi + qi)
        out[9 - k] = (pr + qr, pi - qi)
    return out


def forward45(x):
    zero, one, two = [], [], []
    for p9 in range(9):
        a0, a1, a2 = real5([x[(9 * p5 + 5 * p9) % PTS] for p5 in range(5)])
        zero.append(a0)
        one.append(a1)
        two.append(a2)
    out = real9(zero)
    for part in (one, two):
        out += complex9([a[0] for a in part], [a[1] for a in part], -1.0)
    return out


def inverse45(v):
    zero, one, two = v[:5], v[5:14], v[14:]
    b0 = [None] * 9
    b0[0] = total([z[0] for z in zero])
    for p in range(1, 5):
        pr = total([zero[0][0]] + [cs(9, p * k)[0] * zero[k][0] for k in range(1, 5)])
        qr = total([cs(9, p * k)[1] * zero[k][1] for k in range(1, 5)])
        b0[p] = pr - qr
        b0[9 - p] = pr + qr
    b1 = complex9([a[0] for a in one], [a[1] for a in one], 1.0)
    b2 = complex9([a[0] for a in two], [a[1] for a in two], 1.0)
    c1, s1 = cs(5, 1)
    c2, s2 = cs(5, 2)
    out = [None] * PTS
    for p9 in range(9):
        (r1, i1), (r2, i2), base = b1[p9], b2[p9], b0[p9]
        ca = base + (c1 * r1 + c2 * r2)
        sa = s1 * i1 + s2 * i2
        cb = base + (c2 * r1 + c1 * r2)
        sb = s2 * i1 - s1 * i2
        vals = [base + (r1 + r2), ca - sa, cb - sb, cb + sb, ca + sa]
        for p5 in range(5):
            out[(9 * p5 + 5 * p9) % PTS] = vals[p5]
    return out


def fused_kernel(
    lat_count, lon_count,
    tr, cour, zs_in, zf_in, cut_in, damp_in,
    twid_in, kabs_in, scale_in, fwd_h_in, fwd_l_in, inv_h_in, inv_l_in,
    out,
    got_t, got_c, halo_t, halo_c, parts, strips, joint, got_j,
    zs, zf, cut, damp, twid, kabs, scale, fwd_h, fwd_l, inv_h, inv_l,
    line, moved, spec, wave,
    t_send, t_recv, c_send, c_recv, h_send, h_recv, hc_send, hc_recv, b_send, b_recv, b_local, local, ready,
    s_send, s_recv, s_local,
):
    tracer_count, _, row_count, columns = tr.shape
    lat = lax.axis_index("lat")
    lon = lax.axis_index("lon")
    up = lax.rem(lat + 1, lat_count)
    down = lax.rem(lat + lat_count - 1, lat_count)
    flip = 2 * lax.rem(lat, 2)
    peers = [lon + 1 - 2 * lax.rem(lon, 2), lax.rem(lon + 2, lon_count), lon_count - 1 - lon]
    levels = [pl.ds(2 * lax.rem(peer + flip, lon_count), 2) for peer in peers]
    mine = pl.ds(2 * lax.rem(lon + flip, lon_count), 2)

    staged = [
        (tr.at[:, mine], got_t.at[lon]), (cour.at[mine], got_c.at[lon]),
        (zs_in, zs), (zf_in, zf), (cut_in, cut), (damp_in, damp),
        (twid_in, twid), (kabs_in, kabs), (scale_in, scale),
        (fwd_h_in, fwd_h), (fwd_l_in, fwd_l), (inv_h_in, inv_h), (inv_l_in, inv_l),
    ]
    staged = [
        pltpu.make_async_copy(a, b, local.at[i]) for i, (a, b) in enumerate(staged)
    ]

    def remote(src, dst, send, recv, device):
        return pltpu.make_async_remote_copy(
            src_ref=src, dst_ref=dst, send_sem=send, recv_sem=recv,
            device_id=device, device_id_type=MESH,
        )

    last = pl.ds(row_count - 1, 1)
    first = pl.ds(0, 1)
    pieces = (pl.ds(1, row_count - 2), first, last)

    whole = columns // LANES * LANES
    spare = columns - whole
    body = pl.ds(0, whole)
    strip = pltpu.make_async_copy(
        tr.at[:, :, :, pl.ds(whole, spare)], strips, s_local.at[0]
    )

    def ends(m):
        return remote(
            joint.at[levels[m]], got_j.at[lon], s_send.at[m], s_recv.at[m],
            {"lat": lat, "lon": peers[m]},
        )

    def cells(t, m, piece):
        return remote(
            tr.at[t, levels[m], pieces[piece], body], got_t.at[lon, t, :, pieces[piece], body],
            t_send.at[t, 3 * m + piece], t_recv.at[t, 3 * m + piece],
            {"lat": lat, "lon": peers[m]},
        )

    def speeds(m):
        return remote(
            cour.at[levels[m]], got_c.at[lon], c_send.at[m], c_recv.at[m],
            {"lat": lat, "lon": peers[m]},
        )

    far = pl.ds(2 - 2 * (lon // 2), 2)
    direct = [(mine, peers[1]), (levels[0], peers[2])]

    def rims(t):
        copies = []
        for j, (owned, owner) in enumerate(direct):
            copies.append((
                remote(tr.at[t, owned, last], halo_t.at[lon, t, :, last],
                       h_send.at[t, j], h_recv.at[t, j], {"lat": up, "lon": owner}),
                remote(tr.at[t, owned, first], halo_t.at[lon, t, :, first],
                       h_send.at[t, j + 3], h_recv.at[t, j + 3], {"lat": down, "lon": owner}),
            ))
        copies.append((
            remote(got_t.at[far, t, :, last], halo_t.at[far, t, :, last],
                   h_send.at[t, 2], h_recv.at[t, 2], {"lat": up, "lon": peers[1]}),
            remote(got_t.at[far, t, :, first], halo_t.at[far, t, :, first],
                   h_send.at[t, 5], h_recv.at[t, 5], {"lat": down, "lon": peers[1]}),
        ))
        return copies

    def rim_speeds():
        copies = [
            remote(cour.at[owned, first], halo_c.at[lon, :, first],
                   hc_send.at[j], hc_recv.at[j], {"lat": down, "lon": owner})
            for j, (owned, owner) in enumerate(direct)
        ]
        copies.append(
            remote(got_c.at[far, :, first], halo_c.at[far, :, first],
                   hc_send.at[2], hc_recv.at[2], {"lat": down, "lon": peers[1]})
        )
        return copies

    def reply(t, m, piece):
        rows = pieces[piece]
        return remote(
            parts.at[peers[m], t, :, rows], out.at[t, mine, rows],
            b_send.at[t, 3 * m + piece], b_recv.at[t, 3 * m + piece],
            {"lat": lat, "lon": peers[m]},
        )

    def keep(t):
        return pltpu.make_async_copy(parts.at[lon, t], out.at[t, mine], b_local.at[t])

    barrier = pltpu.get_barrier_semaphore()
    has_north = (2 * lat_count - 3 - lat) // (lat_count - 1)
    has_south = (lat + lat_count - 2) // (lat_count - 1)
    north_there, south_there = has_north == 1, has_south == 1

    def signal(friend):
        pl.semaphore_signal(barrier, inc=1, device_id=friend, device_id_type=MESH)

    for peer in peers:
        signal({"lat": lat, "lon": peer})
    core = lax.rem(lon, 2)
    keeper = peers[1] + 1 - core
    pl.when(north_there)(functools.partial(signal, {"lat": up, "lon": keeper}))
    pl.when(south_there)(functools.partial(signal, {"lat": down, "lon": keeper}))
    strip.start()
    for copy in staged:
        copy.start()
    pl.semaphore_wait(barrier, len(peers) + core * (2 * has_north + 2 * has_south))
    for m in (1, 2, 0):
        speeds(m).start()
    strip.wait()
    for level in range(tr.shape[1]):
        joint[level] = jnp.concatenate([strips[t, level] for t in range(tracer_count)], axis=1)
    for m in (1, 2, 0):
        ends(m).start()
    for group_of in ((0,), (1,), (2, 3)):
        for piece in (1, 2, 0):
            for t in group_of:
                for m in (1, 2, 0):
                    cells(t, m, piece).start()

    @pl.when(core == 1)
    def _():
        pl.semaphore_signal(ready, inc=1, device_id={"lat": lat, "lon": peers[0]}, device_id_type=MESH)

    @pl.when(core == 0)
    def _():
        pl.semaphore_wait(ready, 1)

    def each_rim(north_act, south_act, copies):
        @pl.when(north_act[0])
        def _():
            for north, _ in copies:
                getattr(north, north_act[1])()

        @pl.when(south_act[0])
        def _():
            for _, south in copies:
                getattr(south, south_act[1])()

    def start_rims(copies):
        each_rim((north_there, "start"), (south_there, "start"), copies)

    @pl.when(south_there)
    def _():
        for copy in rim_speeds()[:2]:
            copy.start()

    for t in range(2):
        start_rims(rims(t)[:2])
    for copy in staged:
        copy.wait()

    def relay(t):
        for m in (1, 2):
            for piece in (1, 2):
                cells(t, m, piece).wait_recv()
        start_rims(rims(t)[2:])

    speeds(1).wait_recv()
    speeds(2).wait_recv()
    pl.when(south_there)(rim_speeds()[2].start)
    speeds(0).wait_recv()

    shape = (8, LANES)
    sub = lax.broadcasted_iota(jnp.int32, (8, columns), 0)
    sub1 = lax.broadcasted_iota(jnp.int32, shape, 0)
    lane = lax.broadcasted_iota(jnp.int32, shape, 1)

    def own_levels(ref):
        rows = ref[...].astype(jnp.float32)
        wide = jnp.concatenate([rows, rows], axis=0)
        a = lax.broadcasted_iota(jnp.int32, wide.shape, 0)
        b = lax.broadcasted_iota(jnp.int32, wide.shape, 1)
        at = 2 * lax.rem(lon + flip, lon_count) + (a // 4)
        value = jnp.sum(jnp.where(b == at, wide, 0.0), axis=1, keepdims=True)
        return jnp.broadcast_to(value, shape)

    def own_rows(ref):
        rows = ref[pl.ds(lat * row_count // LANES, 1)].astype(jnp.float32)
        wide = jnp.broadcast_to(rows, shape)
        at = lax.rem(lat * row_count, LANES) + (sub1 & 3)
        value = jnp.sum(jnp.where(lane == at, wide, 0.0), axis=1, keepdims=True)
        return jnp.broadcast_to(value, shape)

    face = lat * row_count + (sub & 3)
    open_s8 = face > 0
    open_n8 = face + 1 < lat_count * row_count
    quarter = lat_count // 4
    in_cap = (lat < quarter) | (lat >= lat_count - quarter)
    given = (own_levels(zs), own_levels(zf), own_rows(cut), own_rows(damp))

    def joined(edge, one, two):
        inner = (lax.broadcasted_iota(jnp.int32, one.shape, 0) + 1) & 2
        return jnp.where(inner == (0 if edge else 2), one, pltpu.roll(two, 2, 0))

    def stacked(ref, *at):
        return jnp.concatenate([ref[(*at, 0)], ref[(*at, 1)]], axis=0)

    def advected(seg, t, edge):
        x = stacked(got_t, seg, t)
        c = stacked(got_c, seg)
        below = pltpu.roll(x, 1, 0)
        if edge:
            rim = stacked(halo_t, seg, t)
            rim_c = stacked(halo_c, seg)
            below = jnp.where((sub & 3) == 0, pltpu.roll(rim, 5, 0), below)
        flux = jnp.maximum(c, 0.0) * below + jnp.minimum(c, 0.0) * x
        if edge:
            flux = jnp.where(open_s8, flux, 0.0)
        top = pltpu.roll(flux, 7, 0)
        if edge:
            hi, ch = pltpu.roll(rim, 3, 0), pltpu.roll(rim_c, 3, 0)
            top = jnp.where(
                (sub & 3) == 3, jnp.maximum(ch, 0.0) * x + jnp.minimum(ch, 0.0) * hi, top
            )
            top = jnp.where(open_n8, top, 0.0)
        return x + flux - top

    def group(edge, both):
        for t in both:
            if edge:
                each_rim((south_there, "wait_recv"), (north_there, "wait_recv"), rims(t))
            else:
                for m in range(3):
                    cells(t, m, 0).wait_recv()
                for piece in (1, 2):
                    cells(t, 0, piece).wait_recv()
        alone = len(both) == 1
        s0, here, cut8, damp8 = [value if alone else joined(edge, value, value) for value in given]
        s0, cut8 = s0.astype(jnp.int32), cut8.astype(jnp.int32)
        s1 = s0 + 1
        fold0, fold1 = (lane - s0) & (LANES - 1), (lane - s1) & (LANES - 1)
        own0, own1 = lane >= s0, lane >= s1
        for seg in range(lon_count):
            tiles = [advected(seg, t, edge) for t in both]
            line[:, seg * columns : (seg + 1) * columns] = tiles[0] if alone else joined(edge, *tiles)

        def gathered(p):
            tile = line[:, p * LANES : (p + 1) * LANES]
            return (
                jnp.take_along_axis(tile, fold0, axis=1),
                jnp.take_along_axis(tile, fold1, axis=1),
            )

        @pl.when(in_cap)
        def _():
            previous = gathered(PTS - 1)
            x = []
            for p in range(PTS):
                now = gathered(p)
                current = jnp.where(own0, now[0], previous[0])
                earlier = jnp.where(own1, now[1], previous[1])
                value = (1.0 - here) * current + here * earlier
                moved[:, p * LANES : (p + 1) * LANES] = value
                x.append(value)
                previous = now
            for r, (re, im) in enumerate(forward45(x)):
                tc, ts = twid[0, r : r + 1], twid[1, r : r + 1]
                if im is None:
                    spec[8 * r : 8 * r + 8, :LANES] = re * tc
                    spec[8 * r : 8 * r + 8, LANES:] = -(re * ts)
                else:
                    spec[8 * r : 8 * r + 8, :LANES] = re * tc + im * ts
                    spec[8 * r : 8 * r + 8, LANES:] = im * tc - re * ts
            wave[...] = split_dot(spec[...], fwd_h[...], fwd_l[...])
            for r in range(HALF):
                weight = jnp.where(kabs[r : r + 1] <= cut8, scale[r : r + 1], 0.0)
                wave[8 * r : 8 * r + 8, :] = wave[8 * r : 8 * r + 8, :] * weight
            spec[...] = split_dot(wave[...], inv_h[...], inv_l[...])
            v = []
            for r in range(HALF):
                tc, ts = twid[0, r : r + 1], twid[1, r : r + 1]
                re, im = spec[8 * r : 8 * r + 8, :LANES], spec[8 * r : 8 * r + 8, LANES:]
                v.append((re * tc - im * ts, re * ts + im * tc))
            for p, low in enumerate(inverse45(v)):
                cols = slice(p * LANES, (p + 1) * LANES)
                shifted = moved[:, cols]
                filtered = damp8 * shifted + (1.0 - damp8) * low
                line[:, cols] = filtered

        @pl.when(jnp.logical_not(in_cap))
        def _():
            previous = gathered(PTS - 1)
            for p in range(PTS):
                now = gathered(p)
                current = jnp.where(own0, now[0], previous[0])
                earlier = jnp.where(own1, now[1], previous[1])
                moved[:, p * LANES : (p + 1) * LANES] = (1.0 - here) * current + here * earlier
                previous = now
            line[...] = moved[...]

        for seg in range(lon_count):
            value = line[:, seg * columns : (seg + 1) * columns]
            for t, rows in zip(both, (value, None if alone else pltpu.roll(value, 6, 0))):
                for level in range(2):
                    tile = rows[4 * level : 4 * level + 4]
                    if edge:
                        parts[seg, t, level, 0:1] = tile[0:1]
                        parts[seg, t, level, 3:4] = tile[3:4]
                    else:
                        parts[seg, t, level] = tile
        for t in both:
            for piece in ((1, 2) if edge else (0,)):
                for m in (1, 2, 0):
                    reply(t, m, piece).start()
            if edge:
                keep(t).start()

    for m in (0, 1, 2):
        ends(m).wait_recv()
        for level in range(2):
            value = got_j[peers[m], level]
            for t in range(tracer_count):
                part = value if t == 0 else pltpu.roll(value, LANES - spare * t, 1)
                got_t[peers[m], t, level, :, whole:columns] = part[:, :spare]
    for t in range(2):
        relay(t)
        start_rims(rims(t + 2)[:2])
    group(False, [0, 1])
    for t in range(2, tracer_count):
        relay(t)

    @pl.loop(2, tracer_count)
    def _(t):
        group(False, [t])

    @pl.when(north_there)
    def _():
        for copy in rim_speeds():
            copy.wait_recv()

    @pl.loop(0, tracer_count // 2)
    def _(pair):
        group(True, [2 * pair, 2 * pair + 1])

    for m in range(3):
        speeds(m).wait_send()
        ends(m).wait_send()

    @pl.when(south_there)
    def _():
        for copy in rim_speeds():
            copy.wait_send()

    for t in range(tracer_count):
        for m in range(3):
            for piece in range(3):
                cells(t, m, piece).wait_send()
        each_rim((north_there, "wait_send"), (south_there, "wait_send"), rims(t))
        for m in range(3):
            for piece in range(3):
                back = reply(t, m, piece)
                back.wait_send()
                back.wait_recv()
        keep(t).wait()


def deliver_kernel(held, out, sem):
    copy = pltpu.make_async_copy(held, out, sem.at[0])
    copy.start()
    copy.wait()


def body(tracers, merid_courant, zonal_shift, zonal_fraction, cutoff, damping):
    tracer_count, level_count, row_count, columns = tracers.shape
    lat_count = lax.axis_size("lat")
    lon_count = lax.axis_size("lon")
    per = level_count // lon_count
    twid, kabs, scale, fwd, inv = tables(columns * lon_count)
    operands = (
        tracers, merid_courant, zonal_shift.T, zonal_fraction.T,
        cutoff.reshape(-1, LANES), damping.reshape(-1, LANES),
        jnp.asarray(twid), jnp.asarray(kabs), jnp.asarray(scale), *halves(fwd), *halves(inv),
    )
    any_space = pl.BlockSpec(memory_space=pl.ANY)
    operands = tuple(pltpu.with_memory_space_constraint(a, pltpu.HBM) for a in operands)
    tile = (per, row_count, columns)
    f32 = jnp.float32
    small = [pltpu.VMEM(a.shape, a.dtype) for a in operands[2:]]
    dma = pltpu.SemaphoreType.DMA
    result = pl.pallas_call(
        functools.partial(fused_kernel, lat_count, lon_count),
        out_shape=jax.ShapeDtypeStruct(tracers.shape, f32),
        in_specs=[any_space] * len(operands),
        out_specs=pl.BlockSpec(memory_space=pltpu.VMEM),
        scratch_shapes=[
            pltpu.VMEM((lon_count, tracer_count) + tile, f32),
            pltpu.VMEM((lon_count,) + tile, f32),
            pltpu.VMEM((lon_count, tracer_count) + tile, f32),
            pltpu.VMEM((lon_count,) + tile, f32),
            pltpu.VMEM((lon_count, tracer_count) + tile, f32),
            pltpu.VMEM((tracer_count, level_count, row_count, columns % LANES), f32),
            pltpu.VMEM((level_count, row_count, LANES), f32),
            pltpu.VMEM((lon_count, per, row_count, LANES), f32),
            *small,
            pltpu.VMEM((8, columns * lon_count), f32),
            pltpu.VMEM((8, columns * lon_count), f32),
            pltpu.VMEM((HALF * 8, 2 * LANES), f32),
            pltpu.VMEM((HALF * 8, LANES), f32),
            dma((tracer_count, 9)), dma((tracer_count, 9)),
            dma((3,)), dma((3,)),
            dma((tracer_count, 6)), dma((tracer_count, 6)),
            dma((3,)), dma((3,)),
            dma((tracer_count, 9)), dma((tracer_count, 9)),
            dma((tracer_count,)),
            dma((len(operands),)),
            pltpu.SemaphoreType.REGULAR,
            dma((3,)), dma((3,)), dma((1,)),
        ],
        compiler_params=pltpu.CompilerParams(
            collective_id=0, has_side_effects=True, vmem_limit_bytes=16 << 20
        ),
    )(*operands)
    return pl.pallas_call(
        deliver_kernel,
        out_shape=jax.ShapeDtypeStruct(tracers.shape, f32),
        in_specs=[pl.BlockSpec(memory_space=pltpu.VMEM)],
        out_specs=any_space,
        scratch_shapes=[dma((1,))],
        compiler_params=pltpu.CompilerParams(vmem_limit_bytes=4 << 20),
    )(result)


def solution(mesh):
    placed = (
        P(None, None, "lat", "lon"),
        P(None, "lat", "lon"),
        P(None, "lat"),
        P(None, "lat"),
        P(),
        P(),
    )
    return jax.shard_map(
        body, mesh=mesh, in_specs=placed, out_specs=P(None, None, "lat", "lon"), check_vma=False
    )
```

```python
import functools
import math

import jax
import jax.numpy as jnp
import numpy as np
from jax import lax
from jax.experimental import pallas as pl
from jax.experimental.pallas import tpu as pltpu
from jax.sharding import PartitionSpec as P

MODES = 1024
LANES = 128
PTS = 45
HALF = 23
SPAN = 23
MESH = pl.DeviceIdType.MESH


def residues():
    found = []
    for k5 in range(3):
        for k9 in range(5 if k5 == 0 else 9):
            kk = next(k for k in range(PTS) if k % 5 == k5 and k % 9 == k9)
            found.append(kk if kk <= PTS // 2 else kk - PTS)
    return found


def tables(lon_cells):
    res = np.array(residues(), np.int64)
    lane = np.arange(LANES, dtype=np.int64)
    ang = (res[:, None] * lane[None, :] % lon_cells) * (2 * math.pi / lon_cells)
    twid = np.stack([np.cos(ang), np.sin(ang)]).astype(np.float32)
    half = LANES // 2
    k2 = np.zeros(LANES, np.int64)
    valid = np.zeros(LANES, bool)
    for part in range(2):
        k2[part * half : part * half + 2 * SPAN + 1] = np.arange(-SPAN, SPAN + 1)
        valid[part * half : part * half + 2 * SPAN + 1] = True
    mode = res[:, None] + PTS * k2[None, :]
    kabs = np.abs(mode)
    keep = valid[None, :] & (kabs < MODES) & ~((res[:, None] == 0) & (mode < 0))
    kabs = np.where(keep, kabs, 1 << 20).astype(np.int32)
    scale = np.where(mode == 0, 1.0, 2.0) / lon_cells
    scale = np.where(keep, scale, 0.0).astype(np.float32)
    ang2 = (k2[None, :] * lane[:, None] % LANES) * (2 * math.pi / LANES)
    c2 = np.cos(ang2) * valid[None, :]
    s2 = np.sin(ang2) * valid[None, :]
    first = np.arange(LANES) < half
    fwd = np.concatenate(
        [np.where(first, c2, -s2), np.where(first, s2, c2)], axis=0
    )
    inv = np.concatenate(
        [np.where(first, c2, -s2), np.where(first, s2, c2)], axis=0
    ).T
    return twid, kabs, scale, fwd.astype(np.float32), inv.astype(np.float32)


def halves(table):
    high = jnp.asarray(table).astype(jnp.bfloat16)
    low = (jnp.asarray(table) - high.astype(jnp.float32)).astype(jnp.bfloat16)
    return high, low


def split_dot(value, high, low):
    vh = value.astype(jnp.bfloat16)
    vl = (value - vh.astype(jnp.float32)).astype(jnp.bfloat16)
    dot = functools.partial(jnp.dot, preferred_element_type=jnp.float32)
    return dot(vh, high) + (dot(vl, high) + dot(vh, low))


def cs(count, turn):
    return math.cos(2 * math.pi * turn / count), math.sin(2 * math.pi * turn / count)


def real5(x):
    e1, o1, e2, o2 = x[1] + x[4], x[1] - x[4], x[2] + x[3], x[2] - x[3]
    c1, s1 = cs(5, 1)
    c2, s2 = cs(5, 2)
    return (
        x[0] + (e1 + e2),
        (x[0] + (c1 * e1 + c2 * e2), -(s1 * o1 + s2 * o2)),
        (x[0] + (c2 * e1 + c1 * e2), s1 * o2 - s2 * o1),
    )


def total(terms):
    while len(terms) > 1:
        terms = [sum(terms[i : i + 2][1:], terms[i]) for i in range(0, len(terms), 2)]
    return terms[0]


def real9(x):
    e = [x[j] + x[9 - j] for j in range(1, 5)]
    o = [x[j] - x[9 - j] for j in range(1, 5)]
    out = [(total([x[0]] + e), None)]
    for k in range(1, 5):
        re = total([x[0]] + [cs(9, j * k)[0] * e[j - 1] for j in range(1, 5)])
        im = total([-cs(9, j * k)[1] * o[j - 1] for j in range(1, 5)])
        out.append((re, im))
    return out


def complex9(re, im, sign):
    er = [re[j] + re[9 - j] for j in range(1, 5)]
    ei = [im[j] + im[9 - j] for j in range(1, 5)]
    dr = [re[j] - re[9 - j] for j in range(1, 5)]
    di = [im[j] - im[9 - j] for j in range(1, 5)]
    out = [None] * 9
    out[0] = (total([re[0]] + er), total([im[0]] + ei))
    for k in range(1, 5):
        c = [cs(9, j * k)[0] for j in range(1, 5)]
        s = [sign * cs(9, j * k)[1] for j in range(1, 5)]
        pr = total([re[0]] + [c[j] * er[j] for j in range(4)])
        pi = total([im[0]] + [c[j] * ei[j] for j in range(4)])
        qr = total([s[j] * di[j] for j in range(4)])
        qi = total([s[j] * dr[j] for j in range(4)])
        out[k] = (pr - qr, pi + qi)
        out[9 - k] = (pr + qr, pi - qi)
    return out


def forward45(x):
    zero, one, two = [], [], []
    for p9 in range(9):
        a0, a1, a2 = real5([x[(9 * p5 + 5 * p9) % PTS] for p5 in range(5)])
        zero.append(a0)
        one.append(a1)
        two.append(a2)
    out = real9(zero)
    for part in (one, two):
        out += complex9([a[0] for a in part], [a[1] for a in part], -1.0)
    return out


def inverse45(v):
    zero, one, two = v[:5], v[5:14], v[14:]
    b0 = [None] * 9
    b0[0] = total([z[0] for z in zero])
    for p in range(1, 5):
        pr = total([zero[0][0]] + [cs(9, p * k)[0] * zero[k][0] for k in range(1, 5)])
        qr = total([cs(9, p * k)[1] * zero[k][1] for k in range(1, 5)])
        b0[p] = pr - qr
        b0[9 - p] = pr + qr
    b1 = complex9([a[0] for a in one], [a[1] for a in one], 1.0)
    b2 = complex9([a[0] for a in two], [a[1] for a in two], 1.0)
    c1, s1 = cs(5, 1)
    c2, s2 = cs(5, 2)
    out = [None] * PTS
    for p9 in range(9):
        (r1, i1), (r2, i2), base = b1[p9], b2[p9], b0[p9]
        ca = base + (c1 * r1 + c2 * r2)
        sa = s1 * i1 + s2 * i2
        cb = base + (c2 * r1 + c1 * r2)
        sb = s2 * i1 - s1 * i2
        vals = [base + (r1 + r2), ca - sa, cb - sb, cb + sb, ca + sa]
        for p5 in range(5):
            out[(9 * p5 + 5 * p9) % PTS] = vals[p5]
    return out


def fused_kernel(
    lat_count, lon_count,
    tr, cour, zs_in, zf_in, cut_in, damp_in,
    twid_in, kabs_in, scale_in, fwd_h_in, fwd_l_in, inv_h_in, inv_l_in,
    out,
    got_t, got_c, halo_t, halo_c, parts, strips, joint, got_j,
    zs, zf, cut, damp, twid, kabs, scale, fwd_h, fwd_l, inv_h, inv_l,
    line, moved, spec, wave,
    t_send, t_recv, c_send, c_recv, h_send, h_recv, hc_send, hc_recv, b_send, b_recv, b_local, local, ready,
    s_send, s_recv, s_local,
):
    tracer_count, _, row_count, columns = tr.shape
    lat = lax.axis_index("lat")
    lon = lax.axis_index("lon")
    up = lax.rem(lat + 1, lat_count)
    down = lax.rem(lat + lat_count - 1, lat_count)
    flip = 2 * lax.rem(lat, 2)
    peers = [lon + 1 - 2 * lax.rem(lon, 2), lax.rem(lon + 2, lon_count), lon_count - 1 - lon]
    levels = [pl.ds(2 * lax.rem(peer + flip, lon_count), 2) for peer in peers]
    mine = pl.ds(2 * lax.rem(lon + flip, lon_count), 2)

    staged = [
        (tr.at[:, mine], got_t.at[lon]), (cour.at[mine], got_c.at[lon]),
        (zs_in, zs), (zf_in, zf), (cut_in, cut), (damp_in, damp),
        (twid_in, twid), (kabs_in, kabs), (scale_in, scale),
        (fwd_h_in, fwd_h), (fwd_l_in, fwd_l), (inv_h_in, inv_h), (inv_l_in, inv_l),
    ]
    staged = [
        pltpu.make_async_copy(a, b, local.at[i]) for i, (a, b) in enumerate(staged)
    ]

    def remote(src, dst, send, recv, device):
        return pltpu.make_async_remote_copy(
            src_ref=src, dst_ref=dst, send_sem=send, recv_sem=recv,
            device_id=device, device_id_type=MESH,
        )

    last = pl.ds(row_count - 1, 1)
    first = pl.ds(0, 1)
    pieces = (pl.ds(1, row_count - 2), first, last)

    whole = columns // LANES * LANES
    spare = columns - whole
    body = pl.ds(0, whole)
    strip = pltpu.make_async_copy(
        tr.at[:, :, :, pl.ds(whole, spare)], strips, s_local.at[0]
    )

    def ends(m):
        return remote(
            joint.at[levels[m]], got_j.at[lon], s_send.at[m], s_recv.at[m],
            {"lat": lat, "lon": peers[m]},
        )

    def cells(t, m, piece):
        return remote(
            tr.at[t, levels[m], pieces[piece], body], got_t.at[lon, t, :, pieces[piece], body],
            t_send.at[t, 3 * m + piece], t_recv.at[t, 3 * m + piece],
            {"lat": lat, "lon": peers[m]},
        )

    def speeds(m):
        return remote(
            cour.at[levels[m]], got_c.at[lon], c_send.at[m], c_recv.at[m],
            {"lat": lat, "lon": peers[m]},
        )

    far = pl.ds(2 - 2 * (lon // 2), 2)
    direct = [(mine, peers[1]), (levels[0], peers[2])]

    def rims(t):
        copies = []
        for j, (owned, owner) in enumerate(direct):
            copies.append((
                remote(tr.at[t, owned, last], halo_t.at[lon, t, :, last],
                       h_send.at[t, j], h_recv.at[t, j], {"lat": up, "lon": owner}),
                remote(tr.at[t, owned, first], halo_t.at[lon, t, :, first],
                       h_send.at[t, j + 3], h_recv.at[t, j + 3], {"lat": down, "lon": owner}),
            ))
        copies.append((
            remote(got_t.at[far, t, :, last], halo_t.at[far, t, :, last],
                   h_send.at[t, 2], h_recv.at[t, 2], {"lat": up, "lon": peers[1]}),
            remote(got_t.at[far, t, :, first], halo_t.at[far, t, :, first],
                   h_send.at[t, 5], h_recv.at[t, 5], {"lat": down, "lon": peers[1]}),
        ))
        return copies

    def rim_speeds():
        copies = [
            remote(cour.at[owned, first], halo_c.at[lon, :, first],
                   hc_send.at[j], hc_recv.at[j], {"lat": down, "lon": owner})
            for j, (owned, owner) in enumerate(direct)
        ]
        copies.append(
            remote(got_c.at[far, :, first], halo_c.at[far, :, first],
                   hc_send.at[2], hc_recv.at[2], {"lat": down, "lon": peers[1]})
        )
        return copies

    def reply(t, m, piece):
        rows = pieces[piece]
        return remote(
            parts.at[peers[m], t, :, rows], out.at[t, mine, rows],
            b_send.at[t, 3 * m + piece], b_recv.at[t, 3 * m + piece],
            {"lat": lat, "lon": peers[m]},
        )

    def keep(t):
        return pltpu.make_async_copy(parts.at[lon, t], out.at[t, mine], b_local.at[t])

    barrier = pltpu.get_barrier_semaphore()
    has_north = (2 * lat_count - 3 - lat) // (lat_count - 1)
    has_south = (lat + lat_count - 2) // (lat_count - 1)
    north_there, south_there = has_north == 1, has_south == 1

    def signal(friend):
        pl.semaphore_signal(barrier, inc=1, device_id=friend, device_id_type=MESH)

    core = lax.rem(lon, 2)
    keeper = peers[1] + 1 - core
    pl.when(north_there)(functools.partial(signal, {"lat": up, "lon": keeper}))
    pl.when(south_there)(functools.partial(signal, {"lat": down, "lon": keeper}))
    for peer in peers:
        signal({"lat": lat, "lon": peer})
    strip.start()
    for copy in staged:
        copy.start()
    pl.semaphore_wait(barrier, len(peers) + core * (2 * has_north + 2 * has_south))
    for m in (1, 2, 0):
        speeds(m).start()
    strip.wait()
    for level in range(tr.shape[1]):
        joint[level] = jnp.concatenate([strips[t, level] for t in range(tracer_count)], axis=1)
    for m in (1, 2, 0):
        ends(m).start()
    for group_of in ((0,), (1,), (2, 3)):
        for piece in (1, 2, 0):
            for t in group_of:
                for m in (1, 2, 0):
                    cells(t, m, piece).start()

    @pl.when(core == 1)
    def _():
        pl.semaphore_signal(ready, inc=1, device_id={"lat": lat, "lon": peers[0]}, device_id_type=MESH)

    @pl.when(core == 0)
    def _():
        pl.semaphore_wait(ready, 1)

    def each_rim(north_act, south_act, copies):
        @pl.when(north_act[0])
        def _():
            for north, _ in copies:
                getattr(north, north_act[1])()

        @pl.when(south_act[0])
        def _():
            for _, south in copies:
                getattr(south, south_act[1])()

    def start_rims(copies):
        each_rim((north_there, "start"), (south_there, "start"), copies)

    @pl.when(south_there)
    def _():
        for copy in rim_speeds()[:2]:
            copy.start()

    for t in range(2):
        start_rims(rims(t)[:2])
    for copy in staged:
        copy.wait()

    def relay(t):
        for m in (1, 2):
            for piece in (1, 2):
                cells(t, m, piece).wait_recv()
        start_rims(rims(t)[2:])

    speeds(1).wait_recv()
    speeds(2).wait_recv()
    pl.when(south_there)(rim_speeds()[2].start)
    speeds(0).wait_recv()

    shape = (8, LANES)
    sub = lax.broadcasted_iota(jnp.int32, (8, columns), 0)
    sub1 = lax.broadcasted_iota(jnp.int32, shape, 0)
    lane = lax.broadcasted_iota(jnp.int32, shape, 1)

    def own_levels(ref):
        rows = ref[...].astype(jnp.float32)
        wide = jnp.concatenate([rows, rows], axis=0)
        a = lax.broadcasted_iota(jnp.int32, wide.shape, 0)
        b = lax.broadcasted_iota(jnp.int32, wide.shape, 1)
        at = 2 * lax.rem(lon + flip, lon_count) + (a // 4)
        value = jnp.sum(jnp.where(b == at, wide, 0.0), axis=1, keepdims=True)
        return jnp.broadcast_to(value, shape)

    def own_rows(ref):
        rows = ref[pl.ds(lat * row_count // LANES, 1)].astype(jnp.float32)
        wide = jnp.broadcast_to(rows, shape)
        at = lax.rem(lat * row_count, LANES) + (sub1 & 3)
        value = jnp.sum(jnp.where(lane == at, wide, 0.0), axis=1, keepdims=True)
        return jnp.broadcast_to(value, shape)

    face = lat * row_count + (sub & 3)
    open_s8 = face > 0
    open_n8 = face + 1 < lat_count * row_count
    quarter = lat_count // 4
    in_cap = (lat < quarter) | (lat >= lat_count - quarter)
    given = (own_levels(zs), own_levels(zf), own_rows(cut), own_rows(damp))

    def joined(edge, one, two):
        inner = (lax.broadcasted_iota(jnp.int32, one.shape, 0) + 1) & 2
        return jnp.where(inner == (0 if edge else 2), one, pltpu.roll(two, 2, 0))

    def stacked(ref, *at):
        return jnp.concatenate([ref[(*at, 0)], ref[(*at, 1)]], axis=0)

    def advected(seg, t, edge):
        x = stacked(got_t, seg, t)
        c = stacked(got_c, seg)
        below = pltpu.roll(x, 1, 0)
        if edge:
            rim = stacked(halo_t, seg, t)
            rim_c = stacked(halo_c, seg)
            below = jnp.where((sub & 3) == 0, pltpu.roll(rim, 5, 0), below)
        flux = jnp.maximum(c, 0.0) * below + jnp.minimum(c, 0.0) * x
        if edge:
            flux = jnp.where(open_s8, flux, 0.0)
        top = pltpu.roll(flux, 7, 0)
        if edge:
            hi, ch = pltpu.roll(rim, 3, 0), pltpu.roll(rim_c, 3, 0)
            top = jnp.where(
                (sub & 3) == 3, jnp.maximum(ch, 0.0) * x + jnp.minimum(ch, 0.0) * hi, top
            )
            top = jnp.where(open_n8, top, 0.0)
        return x + flux - top

    def group(edge, both):
        for t in both:
            if edge:
                each_rim((south_there, "wait_recv"), (north_there, "wait_recv"), rims(t))
            else:
                for m in range(3):
                    cells(t, m, 0).wait_recv()
                for piece in (1, 2):
                    cells(t, 0, piece).wait_recv()
        alone = len(both) == 1
        s0, here, cut8, damp8 = [value if alone else joined(edge, value, value) for value in given]
        s0, cut8 = s0.astype(jnp.int32), cut8.astype(jnp.int32)
        s1 = s0 + 1
        fold0, fold1 = (lane - s0) & (LANES - 1), (lane - s1) & (LANES - 1)
        own0, own1 = lane >= s0, lane >= s1
        for seg in range(lon_count):
            tiles = [advected(seg, t, edge) for t in both]
            line[:, seg * columns : (seg + 1) * columns] = tiles[0] if alone else joined(edge, *tiles)

        def gathered(p):
            tile = line[:, p * LANES : (p + 1) * LANES]
            return (
                jnp.take_along_axis(tile, fold0, axis=1),
                jnp.take_along_axis(tile, fold1, axis=1),
            )

        @pl.when(in_cap)
        def _():
            previous = gathered(PTS - 1)
            x = []
            for p in range(PTS):
                now = gathered(p)
                current = jnp.where(own0, now[0], previous[0])
                earlier = jnp.where(own1, now[1], previous[1])
                value = (1.0 - here) * current + here * earlier
                moved[:, p * LANES : (p + 1) * LANES] = value
                x.append(value)
                previous = now
            for r, (re, im) in enumerate(forward45(x)):
                tc, ts = twid[0, r : r + 1], twid[1, r : r + 1]
                if im is None:
                    spec[8 * r : 8 * r + 8, :LANES] = re * tc
                    spec[8 * r : 8 * r + 8, LANES:] = -(re * ts)
                else:
                    spec[8 * r : 8 * r + 8, :LANES] = re * tc + im * ts
                    spec[8 * r : 8 * r + 8, LANES:] = im * tc - re * ts
            wave[...] = split_dot(spec[...], fwd_h[...], fwd_l[...])
            for r in range(HALF):
                weight = jnp.where(kabs[r : r + 1] <= cut8, scale[r : r + 1], 0.0)
                wave[8 * r : 8 * r + 8, :] = wave[8 * r : 8 * r + 8, :] * weight
            spec[...] = split_dot(wave[...], inv_h[...], inv_l[...])
            v = []
            for r in range(HALF):
                tc, ts = twid[0, r : r + 1], twid[1, r : r + 1]
                re, im = spec[8 * r : 8 * r + 8, :LANES], spec[8 * r : 8 * r + 8, LANES:]
                v.append((re * tc - im * ts, re * ts + im * tc))
            for p, low in enumerate(inverse45(v)):
                cols = slice(p * LANES, (p + 1) * LANES)
                shifted = moved[:, cols]
                filtered = damp8 * shifted + (1.0 - damp8) * low
                line[:, cols] = filtered

        @pl.when(jnp.logical_not(in_cap))
        def _():
            previous = gathered(PTS - 1)
            for p in range(PTS):
                now = gathered(p)
                current = jnp.where(own0, now[0], previous[0])
                earlier = jnp.where(own1, now[1], previous[1])
                moved[:, p * LANES : (p + 1) * LANES] = (1.0 - here) * current + here * earlier
                previous = now
            line[...] = moved[...]

        for seg in range(lon_count):
            value = line[:, seg * columns : (seg + 1) * columns]
            for t, rows in zip(both, (value, None if alone else pltpu.roll(value, 6, 0))):
                for level in range(2):
                    tile = rows[4 * level : 4 * level + 4]
                    if edge:
                        parts[seg, t, level, 0:1] = tile[0:1]
                        parts[seg, t, level, 3:4] = tile[3:4]
                    else:
                        parts[seg, t, level] = tile
        for t in both:
            for piece in ((1, 2) if edge else (0,)):
                for m in (1, 2, 0):
                    reply(t, m, piece).start()
            if edge:
                keep(t).start()

    for m in (0, 1, 2):
        ends(m).wait_recv()
        for level in range(2):
            value = got_j[peers[m], level]
            for t in range(tracer_count):
                part = value if t == 0 else pltpu.roll(value, LANES - spare * t, 1)
                got_t[peers[m], t, level, :, whole:columns] = part[:, :spare]
    for t in range(2):
        relay(t)
        start_rims(rims(t + 2)[:2])
    group(False, [0, 1])
    for t in range(2, tracer_count):
        relay(t)

    @pl.loop(2, tracer_count)
    def _(t):
        group(False, [t])

    @pl.when(north_there)
    def _():
        for copy in rim_speeds():
            copy.wait_recv()

    @pl.loop(0, tracer_count // 2)
    def _(pair):
        group(True, [2 * pair, 2 * pair + 1])

    for m in range(3):
        speeds(m).wait_send()
        ends(m).wait_send()

    @pl.when(south_there)
    def _():
        for copy in rim_speeds():
            copy.wait_send()

    for t in range(tracer_count):
        for m in range(3):
            for piece in range(3):
                cells(t, m, piece).wait_send()
        each_rim((north_there, "wait_send"), (south_there, "wait_send"), rims(t))
        for m in range(3):
            for piece in range(3):
                back = reply(t, m, piece)
                back.wait_send()
                back.wait_recv()
        keep(t).wait()


def deliver_kernel(held, out, sem):
    copy = pltpu.make_async_copy(held, out, sem.at[0])
    copy.start()
    copy.wait()


def body(tracers, merid_courant, zonal_shift, zonal_fraction, cutoff, damping):
    tracer_count, level_count, row_count, columns = tracers.shape
    lat_count = lax.axis_size("lat")
    lon_count = lax.axis_size("lon")
    per = level_count // lon_count
    twid, kabs, scale, fwd, inv = tables(columns * lon_count)
    operands = (
        tracers, merid_courant, zonal_shift.T, zonal_fraction.T,
        cutoff.reshape(-1, LANES), damping.reshape(-1, LANES),
        jnp.asarray(twid), jnp.asarray(kabs), jnp.asarray(scale), *halves(fwd), *halves(inv),
    )
    any_space = pl.BlockSpec(memory_space=pl.ANY)
    operands = tuple(pltpu.with_memory_space_constraint(a, pltpu.HBM) for a in operands)
    tile = (per, row_count, columns)
    f32 = jnp.float32
    small = [pltpu.VMEM(a.shape, a.dtype) for a in operands[2:]]
    dma = pltpu.SemaphoreType.DMA
    result = pl.pallas_call(
        functools.partial(fused_kernel, lat_count, lon_count),
        out_shape=jax.ShapeDtypeStruct(tracers.shape, f32),
        in_specs=[any_space] * len(operands),
        out_specs=pl.BlockSpec(memory_space=pltpu.VMEM),
        scratch_shapes=[
            pltpu.VMEM((lon_count, tracer_count) + tile, f32),
            pltpu.VMEM((lon_count,) + tile, f32),
            pltpu.VMEM((lon_count, tracer_count) + tile, f32),
            pltpu.VMEM((lon_count,) + tile, f32),
            pltpu.VMEM((lon_count, tracer_count) + tile, f32),
            pltpu.VMEM((tracer_count, level_count, row_count, columns % LANES), f32),
            pltpu.VMEM((level_count, row_count, LANES), f32),
            pltpu.VMEM((lon_count, per, row_count, LANES), f32),
            *small,
            pltpu.VMEM((8, columns * lon_count), f32),
            pltpu.VMEM((8, columns * lon_count), f32),
            pltpu.VMEM((HALF * 8, 2 * LANES), f32),
            pltpu.VMEM((HALF * 8, LANES), f32),
            dma((tracer_count, 9)), dma((tracer_count, 9)),
            dma((3,)), dma((3,)),
            dma((tracer_count, 6)), dma((tracer_count, 6)),
            dma((3,)), dma((3,)),
            dma((tracer_count, 9)), dma((tracer_count, 9)),
            dma((tracer_count,)),
            dma((len(operands),)),
            pltpu.SemaphoreType.REGULAR,
            dma((3,)), dma((3,)), dma((1,)),
        ],
        compiler_params=pltpu.CompilerParams(
            collective_id=0, has_side_effects=True, vmem_limit_bytes=16 << 20
        ),
    )(*operands)
    return pl.pallas_call(
        deliver_kernel,
        out_shape=jax.ShapeDtypeStruct(tracers.shape, f32),
        in_specs=[pl.BlockSpec(memory_space=pltpu.VMEM)],
        out_specs=any_space,
        scratch_shapes=[dma((1,))],
        compiler_params=pltpu.CompilerParams(vmem_limit_bytes=4 << 20),
    )(result)


def solution(mesh):
    placed = (
        P(None, None, "lat", "lon"),
        P(None, "lat", "lon"),
        P(None, "lat"),
        P(None, "lat"),
        P(),
        P(),
    )
    return jax.shard_map(
        body, mesh=mesh, in_specs=placed, out_specs=P(None, None, "lat", "lon"), check_vma=False
    )
```
